32 devices in a mesh: replica: 8 (over z, y), group: 4 (over x, core).
Axes of the slice: x: 2, y: 2, z: 4, core: 2. Of those that a mesh axis runs over, the one named last changes fastest.
Arguments:
- target: bfloat16 [16, 1024, 512], P('replica', 'group'), may hold values from -6 to 6
- encoder: bfloat16 [16, 1024, 512], P('replica', 'group'), may hold values from -6 to 6
- target_len: int32 [16], P('replica'), may hold values from 256 to 1024, as said below
- encoder_len: int32 [16], P('replica'), may hold values from 256 to 1024, as said below
- self_wq: bfloat16 [512, 512], P('group'), may hold values from -0.25 to 0.25
- self_wk: bfloat16 [512, 512], P('group'), may hold values from -0.25 to 0.25
- self_wv: bfloat16 [512, 512], P('group'), may hold values from -0.25 to 0.25
- self_wo: bfloat16 [512, 512], P('group'), may hold values from -4 to 4
- self_bq: bfloat16 [512], P('group'), may hold values from -3 to 3
- self_bv: bfloat16 [512], P('group'), may hold values from -3 to 3
- self_bo: bfloat16 [512], P('group'), may hold values from -3 to 3
- norm1_gain: bfloat16 [512], P('group'), may hold values from 0.5 to 1.5
- norm1_bias: bfloat16 [512], P('group'), may hold values from -1.25 to 1.25
- cross_wq: bfloat16 [512, 512], P('group'), may hold values from -0.25 to 0.25
- cross_wk: bfloat16 [512, 512], P('group'), may hold values from -0.25 to 0.25
- cross_wv: bfloat16 [512, 512], P('group'), may hold values from -0.25 to 0.25
- cross_wo: bfloat16 [512, 512], P('group'), may hold values from -4 to 4
- cross_bq: bfloat16 [512], P('group'), may hold values from -3 to 3
- cross_bv: bfloat16 [512], P('group'), may hold values from -3 to 3
- cross_bo: bfloat16 [512], P('group'), may hold values from -3 to 3
- norm2_gain: bfloat16 [512], P('group'), may hold values from 0.5 to 1.5
- norm2_bias: bfloat16 [512], P('group'), may hold values from -1.25 to 1.25
- ffn_in: bfloat16 [512, 2048], P('group'), may hold values from -0.25 to 0.25
- ffn_in_bias: bfloat16 [2048], P('group'), may hold values from -3 to 3
- ffn_out: bfloat16 [2048, 512], P('group'), may hold values from -0.125 to 0.125
- ffn_out_bias: bfloat16 [512], P('group'), may hold values from -3 to 3
- norm3_gain: bfloat16 [512], P('group'), may hold values from 0.5 to 1.5
- norm3_bias: bfloat16 [512], P('group'), may hold values from -1.25 to 1.25
- out_grad: bfloat16 [16, 1024, 512], P('replica', 'group'), may hold values from -6 to 6
Outputs:
- output: bfloat16 [16, 1024, 512], P('replica', 'group')
- grad_target: bfloat16 [16, 1024, 512], P('replica', 'group')
- grad_encoder: bfloat16 [16, 1024, 512], P('replica', 'group')
- grad_self_wq: float32 [512, 512], P('group')
- grad_self_wk: float32 [512, 512], P('group')
- grad_self_wv: float32 [512, 512], P('group')
- grad_self_wo: float32 [512, 512], P('group')
- grad_self_bq: float32 [512], P('group')
- grad_self_bv: float32 [512], P('group')
- grad_self_bo: float32 [512], P('group')
- grad_norm1_gain: float32 [512], P('group')
- grad_norm1_bias: float32 [512], P('group')
- grad_cross_wq: float32 [512, 512], P('group')
- grad_cross_wk: float32 [512, 512], P('group')
- grad_cross_wv: float32 [512, 512], P('group')
- grad_cross_wo: float32 [512, 512], P('group')
- grad_cross_bq: float32 [512], P('group')
- grad_cross_bv: float32 [512], P('group')
- grad_cross_bo: float32 [512], P('group')
- grad_norm2_gain: float32 [512], P('group')
- grad_norm2_bias: float32 [512], P('group')
- grad_ffn_in: float32 [512, 2048], P('group')
- grad_ffn_in_bias: float32 [2048], P('group')
- grad_ffn_out: float32 [2048, 512], P('group')
- grad_ffn_out_bias: float32 [512], P('group')
- grad_norm3_gain: float32 [512], P('group')
- grad_norm3_bias: float32 [512], P('group')
The draws below stay inside these ranges and needn't reach their ends.
Inputs may be any that keep to these rules, and one draw needn't show every extreme that they name: `target_len`: some slot of every draw has all 1024 positions live. `encoder_len`: some slot of every draw has all 1024 positions live.
All inputs are finite; a program needn't handle non-finite values.
Results may differ from the reference program's by a relative error of at most 0.025.
Values may be sent and summed in bfloat16 or wider, within the bound.
No kernel may reach another device: no remote copies, remote signals or barrier semaphores. Data moves between devices by JAX's collectives and lax.ppermute only.
A program may use at most 384 MiB of HBM per device.

```python
import jax
import jax.numpy as jnp
from jax import lax

D = 512
HEADS = 8
FF = 2048
SLOT = 1024
NSEQ = 16


def draw_lengths(key):
    least = SLOT // 4
    values = jax.random.randint(key, (NSEQ,), least, SLOT + 1)
    spot = jax.random.randint(jax.random.fold_in(key, 7), (), 0, NSEQ)
    return jnp.where(jnp.arange(NSEQ) == spot, SLOT, values).astype(jnp.int32)


def draw_target_len(key, part):
    return draw_lengths(jax.random.fold_in(key, 1))


def draw_encoder_len(key, part):
    return draw_lengths(jax.random.fold_in(key, 2))


def steps_of(own_key, dims, cuts, smallest, high):
    factor_of = 1.0
    for dim, parts in cuts:
        heights = jax.random.uniform(jax.random.fold_in(jax.random.fold_in(own_key, 6), dim), (parts,), jnp.float32, smallest / len(cuts), high / len(cuts))
        factor_of = factor_of * jnp.repeat(jnp.exp(heights), dims[dim] // parts).reshape((-1,) + (1,) * (len(dims) - 1 - dim))
    return factor_of


def scatter_about(key, extent, width, most, split=(), held_as=jnp.bfloat16):
    level = steps_of(key, extent, split, -0.22, 0.18) if split else 1.0
    entries = jax.random.normal(key, extent, jnp.float32) * width * level
    return jnp.minimum(jnp.maximum(entries, -most), most).astype(held_as)


def setup_inputs(seed: int = 0) -> dict:
    arg_keys = jax.random.split(jax.random.key(seed), 30)
    return {
        "target": scatter_about(arg_keys[0], (NSEQ, SLOT, D), 1.0, 6.0, ((0, 8), (1, 4))),
        "encoder": scatter_about(arg_keys[1], (NSEQ, SLOT, D), 1.0, 6.0, ((0, 8), (1, 4))),
        "target_len": draw_target_len(jax.random.fold_in(arg_keys[29], 71), 0),
        "encoder_len": draw_encoder_len(jax.random.fold_in(arg_keys[29], 71), 0),
        "self_wq": scatter_about(arg_keys[4], (D, D), D ** -0.5, 0.25, ((0, 4),)),
        "self_wk": scatter_about(arg_keys[5], (D, D), D ** -0.5, 0.25, ((0, 4),)),
        "self_wv": scatter_about(arg_keys[6], (D, D), D ** -0.5, 0.25, ((0, 4),)),
        "self_wo": scatter_about(arg_keys[7], (D, D), (max(1, D // 256)) ** -0.5, 4.0, ((0, 4),)),
        "self_bq": scatter_about(arg_keys[8], (D,), 0.5, 3.0, ((0, 4),)),
        "self_bv": scatter_about(arg_keys[9], (D,), 0.5, 3.0, ((0, 4),)),
        "self_bo": scatter_about(arg_keys[10], (D,), 0.5, 3.0, ((0, 4),)),
        "norm1_gain": jnp.clip(1.0 + 0.1 * jax.random.normal(arg_keys[11], (D,), jnp.float32), 0.5, 1.5).astype(jnp.bfloat16),
        "norm1_bias": scatter_about(arg_keys[12], (D,), 0.2, 1.25, ((0, 4),)),
        "cross_wq": scatter_about(arg_keys[13], (D, D), D ** -0.5, 0.25, ((0, 4),)),
        "cross_wk": scatter_about(arg_keys[14], (D, D), D ** -0.5, 0.25, ((0, 4),)),
        "cross_wv": scatter_about(arg_keys[15], (D, D), D ** -0.5, 0.25, ((0, 4),)),
        "cross_wo": scatter_about(arg_keys[16], (D, D), (max(1, D // 256)) ** -0.5, 4.0, ((0, 4),)),
        "cross_bq": scatter_about(arg_keys[17], (D,), 0.5, 3.0, ((0, 4),)),
        "cross_bv": scatter_about(arg_keys[18], (D,), 0.5, 3.0, ((0, 4),)),
        "cross_bo": scatter_about(arg_keys[19], (D,), 0.5, 3.0, ((0, 4),)),
        "norm2_gain": jnp.clip(1.0 + 0.1 * jax.random.normal(arg_keys[20], (D,), jnp.float32), 0.5, 1.5).astype(jnp.bfloat16),
        "norm2_bias": scatter_about(arg_keys[21], (D,), 0.2, 1.25, ((0, 4),)),
        "ffn_in": scatter_about(arg_keys[22], (D, FF), D ** -0.5, 0.25, ((0, 4),)),
        "ffn_in_bias": scatter_about(arg_keys[23], (FF,), 0.5, 3.0, ((0, 4),)),
        "ffn_out": scatter_about(arg_keys[24], (FF, D), FF ** -0.5, 0.125, ((0, 4),)),
        "ffn_out_bias": scatter_about(arg_keys[25], (D,), 0.5, 3.0, ((0, 4),)),
        "norm3_gain": jnp.clip(1.0 + 0.1 * jax.random.normal(arg_keys[26], (D,), jnp.float32), 0.5, 1.5).astype(jnp.bfloat16),
        "norm3_bias": scatter_about(arg_keys[27], (D,), 0.2, 1.25, ((0, 4),)),
        "out_grad": scatter_about(arg_keys[28], (NSEQ, SLOT, D), 1.0, 6.0, ((0, 8), (1, 4))),
    }


NEGATIVE = -1e+30
EPSILON = 1e-05

@jax.custom_vjp
def low(v):
    return lax.optimization_barrier(v.astype(jnp.bfloat16)).astype(jnp.float32)

@jax.custom_vjp
def low_back(v):
    return v

def low_keep(v):
    return (low(v), None)

def low_pass(kept, grad):
    return (grad,)

def back_keep(v):
    return (v, None)

def back_low(kept, grad):
    return (low(grad),)
low.defvjp(low_keep, low_pass)
low_back.defvjp(back_keep, back_low)

def rounded(value):
    return low(low_back(value))

def matmul(left, right):
    return jnp.dot(left, right, precision=lax.Precision.HIGHEST, preferred_element_type=jnp.float32)

def layer_norm(resid, gain, shift):
    centred = resid - lax.optimization_barrier(jnp.mean(resid, axis=-1, keepdims=True))
    variance = lax.optimization_barrier(jnp.mean(centred * centred, axis=-1, keepdims=True))
    return centred * lax.rsqrt(variance + EPSILON) * gain + shift

def attention(queries, keys, values, limit, causal):
    length = queries.shape[0]
    block = min(512, length)
    count = length // block
    key_pos = jnp.arange(keys.shape[0], dtype=jnp.int32)
    heads_k = keys.reshape(keys.shape[0], HEADS, -1)
    heads_v = values.reshape(values.shape[0], HEADS, -1)

    def one_block(item):
        query_block, start = item
        heads_q = query_block.reshape(block, HEADS, -1)
        logits = low_back(jnp.einsum('qhd,khd->hqk', heads_q, heads_k, precision=lax.Precision.HIGHEST))
        query_pos = start + jnp.arange(block, dtype=jnp.int32)
        allowed = key_pos[None, :] < limit
        if causal:
            allowed = allowed & (key_pos[None, :] <= query_pos[:, None])
        masked = jnp.where(allowed[None], logits, NEGATIVE)
        probs = low(jnp.exp(masked - jax.nn.logsumexp(masked, axis=-1, keepdims=True)))
        return jnp.einsum('hqk,khd->qhd', probs, heads_v, precision=lax.Precision.HIGHEST).reshape(block, -1)
    starts = (jnp.arange(count) * block).astype(jnp.int32)
    result = lax.map(jax.checkpoint(one_block), (queries.reshape(count, block, -1), starts))
    return result.reshape(length, -1)

def layer(weights, target_seq, encoder_seq, target_limit, encoder_limit):
    self_wq, self_wk, self_wv, self_wo, self_bq, self_bv, self_bo, norm1_gain, norm1_bias, cross_wq, cross_wk, cross_wv, cross_wo, cross_bq, cross_bv, cross_bo, norm2_gain, norm2_bias, ffn_in, ffn_in_bias, ffn_out, ffn_out_bias, norm3_gain, norm3_bias = weights
    self_queries = rounded((matmul(target_seq, self_wq) + self_bq) * 0.125)
    self_keys = rounded(matmul(target_seq, self_wk))
    self_values = rounded(matmul(target_seq, self_wv) + self_bv)
    self_context = rounded(attention(self_queries, self_keys, self_values, target_limit, True))
    self_branch = low_back(matmul(self_context, self_wo) + self_bo)
    first = low(layer_norm(target_seq + self_branch, norm1_gain, norm1_bias))
    cross_queries = rounded((matmul(first, cross_wq) + cross_bq) * 0.125)
    cross_keys = rounded(matmul(encoder_seq, cross_wk))
    cross_values = rounded(matmul(encoder_seq, cross_wv) + cross_bv)
    cross_context = rounded(attention(cross_queries, cross_keys, cross_values, encoder_limit, False))
    cross_branch = low_back(matmul(cross_context, cross_wo) + cross_bo)
    second = low(layer_norm(first + cross_branch, norm2_gain, norm2_bias))
    pre_act = low_back(matmul(second, ffn_in) + ffn_in_bias)
    hidden = low(jax.nn.silu(pre_act))
    ffn_branch = low_back(matmul(hidden, ffn_out) + ffn_out_bias)
    return layer_norm(second + ffn_branch, norm3_gain, norm3_bias)

def reference(target, encoder, target_len, encoder_len, self_wq, self_wk, self_wv, self_wo, self_bq, self_bv, self_bo, norm1_gain, norm1_bias, cross_wq, cross_wk, cross_wv, cross_wo, cross_bq, cross_bv, cross_bo, norm2_gain, norm2_bias, ffn_in, ffn_in_bias, ffn_out, ffn_out_bias, norm3_gain, norm3_bias, out_grad):
    weights = tuple((item.astype(jnp.float32) for item in (self_wq, self_wk, self_wv, self_wo, self_bq, self_bv, self_bo, norm1_gain, norm1_bias, cross_wq, cross_wk, cross_wv, cross_wo, cross_bq, cross_bv, cross_bo, norm2_gain, norm2_bias, ffn_in, ffn_in_bias, ffn_out, ffn_out_bias, norm3_gain, norm3_bias)))

    def forward(weight_set, target_all, encoder_all):

        def one_sequence(item):
            target_seq, encoder_seq, target_limit, encoder_limit = item
            return layer(weight_set, target_seq, encoder_seq, target_limit, encoder_limit)
        return lax.map(one_sequence, (target_all, encoder_all, target_len, encoder_len))
    result, pullback = jax.vjp(forward, weights, target.astype(jnp.float32), encoder.astype(jnp.float32))
    positions = jnp.arange(SLOT, dtype=jnp.int32)
    live = (positions[None, :] < target_len[:, None]).astype(jnp.float32)
    grad_weights, grad_target, grad_encoder = pullback(out_grad.astype(jnp.float32) * live[:, :, None])
    g_sq, g_sk, g_sv, g_so, g_sbq, g_sbv, g_sbo, g_n1g, g_n1b, g_cq, g_ck, g_cv, g_co, g_cbq, g_cbv, g_cbo, g_n2g, g_n2b, g_fi, g_fib, g_fo, g_fob, g_n3g, g_n3b = grad_weights
    return (result.astype(jnp.bfloat16), grad_target.astype(jnp.bfloat16), grad_encoder.astype(jnp.bfloat16), g_sq, g_sk, g_sv, g_so, g_sbq, g_sbv, g_sbo, g_n1g, g_n1b, g_cq, g_ck, g_cv, g_co, g_cbq, g_cbv, g_cbo, g_n2g, g_n2b, g_fi, g_fib, g_fo, g_fob, g_n3g, g_n3b)
```

```python
import functools

import jax
import jax.numpy as jnp
import numpy as np
from jax import lax
from jax.experimental import pallas as pl
from jax.experimental.pallas import tpu as pltpu
from jax.sharding import PartitionSpec as P

F32 = jnp.float32
BF16 = jnp.bfloat16
HEADS = 8
PAIR = 128
HALF = 64
SCALE = 0.125
NEGATIVE = -1e30
EPSILON = 1e-5
LOG2E = 1.4426950408889634
VMEM_LIMIT = 56 << 20

(SBQ, SBV, SBO, N1G, N1B, CBQ, CBV, CBO, N2G, N2B, FOB, N3G, N3B, FIB) = range(14)
VEC_ROWS = 32
INFO_HEAD = 6

VMEM_SPEC = pl.BlockSpec(memory_space=pltpu.VMEM)
SMEM_SPEC = pl.BlockSpec(memory_space=pltpu.SMEM)


def nn(left, right):
    return lax.dot_general(left, right, (((1,), (0,)), ((), ())), preferred_element_type=F32)


def nt(left, right):
    return lax.dot_general(left, right, (((1,), (1,)), ((), ())), preferred_element_type=F32)


def tn(left, right):
    return lax.dot_general(left, right, (((0,), (0,)), ((), ())), preferred_element_type=F32)


def as_struct(shape, dtype):
    return jax.ShapeDtypeStruct(shape, dtype)


def cost(flops, nbytes, special=0):
    return pl.CostEstimate(flops=int(flops), bytes_accessed=int(nbytes), transcendentals=int(special))


def send_xor(value, axis, mask):
    size = lax.axis_size(axis)
    return lax.ppermute(value, axis, [(i, i ^ mask) for i in range(size)])


def gather_xor(value, axis, size):
    found = {0: value}
    bit = size // 2
    while bit:
        found.update({k | bit: send_xor(v, axis, bit) for k, v in list(found.items())})
        bit //= 2
    return [found[k] for k in range(size)]


def chain(value, *after):
    return lax.optimization_barrier((value, *after))[0]


def group_table(size, rows):
    half = size // 2
    table = []
    for g in range(size):
        upper = g >= half
        row = [g, int(upper), g * rows, (size - 1 - g) * rows, 0, 0]
        for k in range(half):
            d = g ^ k
            row += [d * rows, (size - 1 - d) * rows]

        def place(b):
            d, slot = (b, 0) if (b >= half) == upper else (size - 1 - b, 1)
            return ((g ^ d) * 2 + slot) * rows

        slots = {g: 0, size - 1 - g: 1}
        full = [(slots[b] * rows, place(k)) for b in sorted(slots) for k in range(b)]
        row += [q for q, _ in full] + [k for _, k in full]
        table.append(row)
    return np.asarray(table, np.int32)


def assemble(dest, refs, place, rows, source, index=None):
    for k, ref in enumerate(refs):
        start = pl.multiple_of((place ^ k) * rows, rows)
        block = ref[source : source + rows, :]
        if index is None:
            dest[pl.ds(start, rows), :] = block
        else:
            dest[index, pl.ds(start, rows), :] = block


def scatter_rows(keep, send, grad, place, rows, offset, size):
    for k in range(size):
        start = pl.multiple_of((place ^ k) * rows, rows)
        target = send if k & 1 else keep
        target[k >> 1, offset : offset + rows, :] = grad[pl.ds(start, rows), :].astype(BF16)


def norm(resid):
    centred = resid - jnp.mean(resid, axis=-1, keepdims=True)
    inverse = lax.rsqrt(jnp.mean(centred * centred, axis=-1, keepdims=True) + EPSILON)
    return centred * inverse, inverse


def norm_back(grad, normed, inverse, gain):
    scaled = grad * gain
    return inverse * (
        scaled
        - jnp.mean(scaled, axis=-1, keepdims=True)
        - normed * jnp.mean(scaled * normed, axis=-1, keepdims=True)
    )


def row_sum(value):
    return jnp.sum(value, axis=0, keepdims=True)


def qkv_kernel(size, info, own, other, *rest):
    ws, (vec, x_out, q_out, kv_out, weight) = rest[:size], rest[size:]
    place, half = info[0], info[1]
    rows, width = other.shape
    part = width // size
    for i in range(3):
        assemble(weight, ws, place, part, i * part, i)
    x_out[:rows] = own[half]
    x_out[rows:] = other[...]
    x = x_out[...]
    q_out[...] = ((nn(x, weight[0]) + vec[SBQ : SBQ + 1, :]) * SCALE).astype(BF16)
    kv_out[0] = nn(x, weight[1]).astype(BF16)
    kv_out[1] = (nn(x, weight[2]) + vec[SBV : SBV + 1, :]).astype(BF16)


def run_qkv(info, own, other, ws, vec):
    rows, width = other.shape
    tokens = 2 * rows
    return pl.pallas_call(
        functools.partial(qkv_kernel, len(ws)),
        out_shape=(
            as_struct((tokens, width), BF16),
            as_struct((tokens, width), BF16),
            as_struct((2, tokens, width), BF16),
        ),
        in_specs=[SMEM_SPEC] + [VMEM_SPEC] * (3 + len(ws)),
        out_specs=(VMEM_SPEC,) * 3,
        scratch_shapes=[pltpu.VMEM((3, width, width), BF16)],
        compiler_params=pltpu.CompilerParams(vmem_limit_bytes=VMEM_LIMIT),
        cost_estimate=cost(6 * tokens * width * width, 4e6),
        name="qkv",
    )(info, own, other, *ws, vec)


def cross_kv_kernel(size, info, own, other, *rest):
    ws, (vec, x_out, kv_out, weight) = rest[:size], rest[size:]
    place, half = info[0], info[1]
    rows, width = other.shape
    part = width // size
    for i in range(2):
        assemble(weight, ws, place, part, (2 + i) * part, i)
    x_out[:rows] = own[half]
    x_out[rows:] = other[...]
    x = x_out[...]
    kv_out[0] = nn(x, weight[0]).astype(BF16)
    kv_out[1] = (nn(x, weight[1]) + vec[CBV : CBV + 1, :]).astype(BF16)


def run_cross_kv(info, own, other, ws, vec):
    rows, width = other.shape
    tokens = 2 * rows
    return pl.pallas_call(
        functools.partial(cross_kv_kernel, len(ws)),
        out_shape=(as_struct((tokens, width), BF16), as_struct((2, tokens, width), BF16)),
        in_specs=[SMEM_SPEC] + [VMEM_SPEC] * (3 + len(ws)),
        out_specs=(VMEM_SPEC,) * 2,
        scratch_shapes=[pltpu.VMEM((2, width, width), BF16)],
        compiler_params=pltpu.CompilerParams(vmem_limit_bytes=VMEM_LIMIT),
        cost_estimate=cost(4 * tokens * width * width, 4e6),
        name="cross_kv",
    )(info, own, other, *ws, vec)


def after_self_kernel(size, info, x_ref, ctx, *rest):
    ws, (vec, first_out, q_out, weight) = rest[:size], rest[size:]
    place = info[0]
    width = x_ref.shape[1]
    part = width // size
    for i in range(2):
        assemble(weight, ws, place, part, i * part, i)
    resid = x_ref[...].astype(F32) + nn(ctx[...], weight[0]) + vec[SBO : SBO + 1, :]
    normed, _ = norm(resid)
    first = (normed * vec[N1G : N1G + 1, :] + vec[N1B : N1B + 1, :]).astype(BF16)
    first_out[...] = first
    q_out[...] = ((nn(first, weight[1]) + vec[CBQ : CBQ + 1, :]) * SCALE).astype(BF16)


def run_after_self(info, x, ctx, ws, vec):
    tokens, width = x.shape
    return pl.pallas_call(
        functools.partial(after_self_kernel, len(ws)),
        out_shape=(as_struct((tokens, width), BF16),) * 2,
        in_specs=[SMEM_SPEC] + [VMEM_SPEC] * (3 + len(ws)),
        out_specs=(VMEM_SPEC,) * 2,
        scratch_shapes=[pltpu.VMEM((2, width, width), BF16)],
        compiler_params=pltpu.CompilerParams(vmem_limit_bytes=VMEM_LIMIT),
        cost_estimate=cost(4 * tokens * width * width, 4e6),
        name="after_self",
    )(info, x, ctx, *ws, vec)


def lanes_of(rows):
    return lax.broadcasted_iota(jnp.int32, (rows, PAIR), 1)


def put_queries(dest, q, head, aux=None):
    lane = lanes_of(q.shape[0])
    mine = (lane // HALF) == head
    spare = HALF * (1 - head)
    scaled = q.astype(F32) * LOG2E
    high = scaled.astype(BF16)
    low = (scaled - high.astype(F32)).astype(BF16)
    extra = jnp.where(lane == spare, jnp.asarray(1, BF16), jnp.asarray(0, BF16))
    if aux is not None:
        extra = extra + aux
    dest[:, :PAIR] = jnp.where(mine, high, extra)
    dest[:, PAIR:] = jnp.where(mine, low, jnp.asarray(0, BF16))


def put_keys(dest, keys, at, head, start, limit, ones):
    rows = keys.shape[0]
    lane = lanes_of(rows)
    mine = (lane // HALF) == head
    spare = HALF * (1 - head)
    pos = start + lax.broadcasted_iota(jnp.int32, (rows, PAIR), 0)
    mask = jnp.where((lane == spare) & (pos >= limit), NEGATIVE, 0.0)
    if ones:
        mask = jnp.where((lane > spare) & (lane < spare + 4), 1.0, mask)
    dest[pl.ds(at, rows), :PAIR] = jnp.where(mine, keys, mask.astype(BF16))
    dest[pl.ds(at, rows), PAIR:] = keys


def put_values(dest, values, at, head, count):
    rows = values.shape[0]
    lane = lanes_of(rows)
    mine = (lane // HALF) == head
    spare = HALF * (1 - head)
    ones = jnp.where((lane >= spare) & (lane < spare + count), 1.0, 0.0).astype(BF16)
    dest[pl.ds(at, rows), :] = jnp.where(mine, values, ones)


def split3(value):
    a = value.astype(BF16)
    rest = value - a.astype(F32)
    b = rest.astype(BF16)
    c = (rest - b.astype(F32)).astype(BF16)
    return a, b, c


def lane_pieces(value, base, rows):
    lane = lanes_of(rows)
    a, b, c = (p.astype(F32) for p in split3(value))
    out = jnp.where(lane == base, a, jnp.where(lane == base + 1, b, jnp.where(lane == base + 2, c, 0.0)))
    return out.astype(BF16)


def finish_rows(acc, top, head):
    rows = acc.shape[0]
    spare = HALF * (1 - head)
    total = acc[:, spare : spare + 1]
    context = acc / total
    pieces = lane_pieces(-(top + jnp.log2(total)), spare + 1, rows)
    return context, pieces


def cross_forward_kernel(count, info, q_ref, *rest):
    kvs, (ctx_out, lse_out, qa, ka, va) = rest[:count], rest[count:]
    limit = info[5]
    tokens = q_ref.shape[0]
    rows = tokens // 2
    contexts, pieces = [], []
    for head in range(2):
        put_queries(qa, q_ref[...], head)
        for p in range(count):
            for slot in range(2):
                cut = slice(slot * rows, (slot + 1) * rows)
                at = (2 * p + slot) * rows
                put_keys(ka, kvs[p][0, cut], at, head, info[INFO_HEAD + 2 * p + slot], limit, False)
                put_values(va, kvs[p][1, cut], at, head, 1)
        parts = []
        for c in range(2):
            logits = nt(qa[c * rows : (c + 1) * rows], ka[...])
            top = jnp.max(logits, axis=-1, keepdims=True)
            weights = jnp.exp2(logits - top).astype(BF16)
            parts.append(finish_rows(nn(weights, va[...]), top, head))
        contexts.append([p[0] for p in parts])
        pieces.append([p[1] for p in parts])
    lane = lanes_of(rows)
    for c in range(2):
        cut = slice(c * rows, (c + 1) * rows)
        ctx_out[cut] = jnp.where(lane < HALF, contexts[0][c], contexts[1][c]).astype(BF16)
        lse_out[cut] = pieces[0][c] + pieces[1][c]


def self_forward_kernel(count, n_full, info, q_ref, *rest):
    kvs, (ctx_out, lse_out, qa, ka, va, store, tops, acc, keep, keep_lse) = rest[:count], rest[count:]
    limit = info[4]
    tokens = q_ref.shape[0]
    rows = tokens // 2
    base = INFO_HEAD + 2 * count
    lane = lanes_of(rows)
    causal = lax.broadcasted_iota(jnp.int32, (rows, rows), 1) <= lax.broadcasted_iota(jnp.int32, (rows, rows), 0)

    def widest(logits):
        parts = [logits[:, i : i + PAIR] for i in range(0, rows, PAIR)]
        return functools.reduce(jnp.maximum, parts)

    for head in range(2):
        put_queries(qa, q_ref[...], head)
        for p in range(count):
            for slot in range(2):
                cut = slice(slot * rows, (slot + 1) * rows)
                at = (2 * p + slot) * rows
                put_keys(ka, kvs[p][0, cut], at, head, info[INFO_HEAD + 2 * p + slot], limit, False)
                put_values(va, kvs[p][1, cut], at, head, 1)
        for slot in range(2):
            cut = slice(slot * rows, (slot + 1) * rows)
            logits = jnp.where(causal, nt(qa[cut], ka[cut]), NEGATIVE)
            store[n_full + slot] = logits
            tops[cut] = widest(logits)
        @pl.loop(0, n_full)
        def _(i):
            q_at = pl.multiple_of(info[base + i], rows)
            k_at = pl.multiple_of(info[base + n_full + i], rows)
            logits = nt(qa[pl.ds(q_at, rows)], ka[pl.ds(k_at, rows)])
            store[i] = logits
            tops[pl.ds(q_at, rows)] = jnp.maximum(tops[pl.ds(q_at, rows)], widest(logits))
        for slot in range(2):
            cut = slice(slot * rows, (slot + 1) * rows)
            top = jnp.broadcast_to(jnp.max(tops[cut], axis=-1, keepdims=True), (rows, PAIR))
            tops[cut] = top
            weights = jnp.exp2(store[n_full + slot] - top[:, :1]).astype(BF16)
            acc[cut] = nn(weights, va[cut])
        @pl.loop(0, n_full)
        def _(i):
            q_at = pl.multiple_of(info[base + i], rows)
            k_at = pl.multiple_of(info[base + n_full + i], rows)
            weights = jnp.exp2(store[i] - tops[pl.ds(q_at, rows)][:, :1]).astype(BF16)
            acc[pl.ds(q_at, rows)] += nn(weights, va[pl.ds(k_at, rows)])
        for slot in range(2):
            cut = slice(slot * rows, (slot + 1) * rows)
            context, pieces = finish_rows(acc[cut], tops[cut][:, :1], head)
            if head == 0:
                keep[cut] = context
                keep_lse[cut] = pieces
            else:
                ctx_out[cut] = jnp.where(lane < HALF, keep[cut], context).astype(BF16)
                lse_out[cut] = keep_lse[cut] + pieces


def attention_specs(count, tokens):
    wide = pl.BlockSpec((tokens, PAIR), lambda i: (0, i))
    kv = pl.BlockSpec((2, tokens, PAIR), lambda i: (0, 0, i))
    lse = pl.BlockSpec((None, tokens, PAIR), lambda i: (i, 0, 0))
    return wide, kv, lse


def run_forward(info, q, kvs, causal):
    tokens, width = q.shape
    rows = tokens // 2
    count = len(kvs)
    keys = count * tokens
    pairs = width // PAIR
    n_full = 2 * count - 1
    wide, kv, lse = attention_specs(count, tokens)
    scratch = [
        pltpu.VMEM((tokens, 2 * PAIR), BF16),
        pltpu.VMEM((keys, 2 * PAIR), BF16),
        pltpu.VMEM((keys, PAIR), BF16),
    ]
    if causal:
        kernel = functools.partial(self_forward_kernel, count, n_full)
        scratch += [
            pltpu.VMEM((n_full + 2, rows, rows), F32),
            pltpu.VMEM((tokens, PAIR), F32),
            pltpu.VMEM((tokens, PAIR), F32),
            pltpu.VMEM((tokens, PAIR), F32),
            pltpu.VMEM((tokens, PAIR), BF16),
        ]
    else:
        kernel = functools.partial(cross_forward_kernel, count)
    work = tokens * keys * width * (0.625 if causal else 1)
    return pl.pallas_call(
        kernel,
        grid=(pairs,),
        out_shape=(as_struct((tokens, width), BF16), as_struct((pairs, tokens, PAIR), BF16)),
        in_specs=[SMEM_SPEC, wide] + [kv] * count,
        out_specs=(wide, lse),
        scratch_shapes=scratch,
        compiler_params=pltpu.CompilerParams(vmem_limit_bytes=VMEM_LIMIT),
        cost_estimate=cost(16 * work, 4e6),
        name="self_forward" if causal else "cross_forward",
    )(info, q, *kvs)


def back_operands(q_ref, ctx, lse, grad, head, qa, ga):
    tokens = q_ref.shape[0]
    lane = lanes_of(tokens)
    mine = (lane // HALF) == head
    spare = HALF * (1 - head)
    far = (lane > spare) & (lane < spare + 4)
    put_queries(qa, q_ref[...], head, jnp.where(far, lse[...], jnp.asarray(0, BF16)))
    both = grad[...].astype(F32) * ctx[...].astype(F32)
    delta = jnp.sum(jnp.where(mine, both, 0.0), axis=-1, keepdims=True)
    ga[...] = jnp.where(mine, grad[...], lane_pieces(-delta, spare, tokens))
    zero = jnp.asarray(0, BF16)
    return jnp.where(mine, q_ref[...], zero), jnp.where(mine, grad[...], zero)


def backward_kernel(count, n_full, causal, info, q_ref, ctx, lse, grad, *rest):
    kvs, rest = rest[:count], rest[count:]
    dq_out, dkvs, rest = rest[0], rest[1 : 1 + count], rest[1 + count :]
    qa, ga, ka, va, km, qm, gm, dq, dk, dv = rest
    limit = info[4 if causal else 5]
    tokens = q_ref.shape[0]
    rows = tokens // 2
    base = INFO_HEAD + 2 * count
    zero = jnp.asarray(0, BF16)
    dq[...] = jnp.zeros_like(dq)
    dk[...] = jnp.zeros_like(dk)
    dv[...] = jnp.zeros_like(dv)
    for head in range(2):
        qm[...], gm[...] = back_operands(q_ref, ctx, lse, grad, head, qa, ga)
        mine = (lanes_of(rows) // HALF) == head
        for p in range(count):
            for slot in range(2):
                cut = slice(slot * rows, (slot + 1) * rows)
                at = (2 * p + slot) * rows
                keys = kvs[p][0, cut]
                put_keys(ka, keys, at, head, info[INFO_HEAD + 2 * p + slot], limit, True)
                put_values(va, kvs[p][1, cut], at, head, 3)
                km[at : at + rows] = jnp.where(mine, keys, zero)

        def tile(q_cut, k_cut, masked):
            logits = nt(ka[k_cut], qa[q_cut])
            if masked:
                shape = logits.shape
                logits = jnp.where(
                    lax.broadcasted_iota(jnp.int32, shape, 0) <= lax.broadcasted_iota(jnp.int32, shape, 1),
                    logits,
                    NEGATIVE,
                )
            probs = jnp.exp2(logits)
            scores = (probs * nt(va[k_cut], ga[q_cut])).astype(BF16)
            dv[k_cut] += nn(probs.astype(BF16), gm[q_cut])
            dk[k_cut] += nn(scores, qm[q_cut])
            dq[q_cut] += tn(scores, km[k_cut])

        if causal:
            for slot in range(2):
                cut = slice(slot * rows, (slot + 1) * rows)
                tile(cut, cut, True)
            @pl.loop(0, n_full)
            def _(i):
                q_at = pl.multiple_of(info[base + i], rows)
                k_at = pl.multiple_of(info[base + n_full + i], rows)
                tile(pl.ds(q_at, rows), pl.ds(k_at, rows), False)
        else:
            for i in range(2 * count):
                tile(slice(None), slice(i * rows, (i + 1) * rows), False)
    dq_out[...] = dq[...].astype(BF16)
    for p in range(count):
        cut = slice(p * tokens, (p + 1) * tokens)
        dkvs[p][0] = dk[cut].astype(BF16)
        dkvs[p][1] = dv[cut].astype(BF16)


def run_backward(info, q, ctx, lse, grad, kvs, causal):
    tokens, width = q.shape
    count = len(kvs)
    keys = count * tokens
    pairs = width // PAIR
    n_full = 2 * count - 1
    wide, kv, lse_spec = attention_specs(count, tokens)
    work = tokens * keys * width * (0.625 if causal else 1)
    return pl.pallas_call(
        functools.partial(backward_kernel, count, n_full, causal),
        grid=(pairs,),
        out_shape=(as_struct((tokens, width), BF16),) + (as_struct((2, tokens, width), BF16),) * count,
        in_specs=[SMEM_SPEC, wide, wide, lse_spec, wide] + [kv] * count,
        out_specs=(wide,) + (kv,) * count,
        scratch_shapes=[
            pltpu.VMEM((tokens, 2 * PAIR), BF16),
            pltpu.VMEM((tokens, PAIR), BF16),
            pltpu.VMEM((keys, 2 * PAIR), BF16),
            pltpu.VMEM((keys, PAIR), BF16),
            pltpu.VMEM((keys, PAIR), BF16),
            pltpu.VMEM((tokens, PAIR), BF16),
            pltpu.VMEM((tokens, PAIR), BF16),
            pltpu.VMEM((tokens, PAIR), F32),
            pltpu.VMEM((keys, PAIR), F32),
            pltpu.VMEM((keys, PAIR), F32),
        ],
        compiler_params=pltpu.CompilerParams(vmem_limit_bytes=VMEM_LIMIT),
        cost_estimate=cost(40 * work, 6e6),
        name="self_backward" if causal else "cross_backward",
    )(info, q, ctx, lse, grad, *kvs)


def middle_kernel(size, info, first_ref, ctx, og_own, og_other, *rest):
    w2, w_in, w_out, rest = rest[:size], rest[size : 2 * size], rest[2 * size : 3 * size], rest[3 * size :]
    vec, fib, keep_out, pass_out, dz2_out, dcross_out, keep, send, vecs, co, fi, fo, pre, scr, wide = rest
    place, half = info[0], info[1]
    tokens, width = first_ref.shape
    rows = tokens // 2
    part = width // size
    hidden_part = w_out[0].shape[0]
    chunks = fi.shape[1] // width
    assemble(co, w2, place, part, 4 * part)
    assemble(fi, w_in, place, part, 0)
    assemble(fo, w_out, place, hidden_part, 0)

    def vector(i):
        return vec[i : i + 1, :]

    resid2 = first_ref[...].astype(F32) + nn(ctx[...], co[...]) + vector(CBO)
    normed2, inverse2 = norm(resid2)
    second = (normed2 * vector(N2G) + vector(N2B)).astype(BF16)
    branch = jnp.zeros((tokens, width), F32)
    for c in range(chunks):
        cut = slice(c * width, (c + 1) * width)
        value = nn(second, fi[:, cut]) + fib[:, cut]
        pre[:, cut] = value
        hidden = (value * (0.5 * jnp.tanh(0.5 * value) + 0.5)).astype(BF16)
        scr[:, cut] = hidden
        branch = branch + nn(hidden, fo[cut])
    resid3 = second.astype(F32) + branch + vector(FOB)
    normed3, inverse3 = norm(resid3)
    out = (normed3 * vector(N3G) + vector(N3B)).astype(BF16)
    keep_out[...] = out[:rows]
    pass_out[...] = out[rows:]

    live = info[4]
    iota = lax.broadcasted_iota(jnp.int32, (rows, 1), 0)
    grad3 = jnp.concatenate(
        [
            jnp.where(iota + info[2] < live, og_own[half].astype(F32), 0.0),
            jnp.where(iota + info[3] < live, og_other[...].astype(F32), 0.0),
        ],
        axis=0,
    )
    dz3 = norm_back(grad3, normed3, inverse3, vector(N3G))
    vecs[...] = jnp.zeros_like(vecs)
    vecs[N3G : N3G + 1] = row_sum(grad3 * normed3)
    vecs[N3B : N3B + 1] = row_sum(grad3)
    dy = dz3.astype(BF16)
    vecs[FOB : FOB + 1] = row_sum(dy.astype(F32))
    dsecond = dz3
    for c in range(chunks):
        cut = slice(c * width, (c + 1) * width)
        wide[...] = tn(scr[:, cut], dy)
        for b in range(width // min(hidden_part, width)):
            row = c * width + b * hidden_part
            owner = row // hidden_part
            block = wide[b * hidden_part : (b + 1) * hidden_part].astype(BF16)
            slot = place ^ owner

            @pl.when((slot & 1) == 0)
            def _():
                keep[slot >> 1, chunks * part : chunks * part + hidden_part, :] = block

            @pl.when((slot & 1) == 1)
            def _():
                send[slot >> 1, chunks * part : chunks * part + hidden_part, :] = block

        value = pre[:, cut]
        sig = 0.5 * jnp.tanh(0.5 * value) + 0.5
        dpre = (nt(dy, fo[cut]) * (sig * (1.0 + value * (1.0 - sig)))).astype(BF16)
        vecs[FIB + c : FIB + c + 1] = row_sum(dpre.astype(F32))
        dsecond = dsecond + nt(dpre, fi[:, cut])
        wide[...] = tn(second, dpre)
        scatter_rows(keep, send, wide, place, part, c * part, size)
    dz2 = norm_back(dsecond, normed2, inverse2, vector(N2G))
    vecs[N2G : N2G + 1] = row_sum(dsecond * normed2)
    vecs[N2B : N2B + 1] = row_sum(dsecond)
    dz2_out[...] = dz2
    da2 = dz2.astype(BF16)
    vecs[CBO : CBO + 1] = row_sum(da2.astype(F32))
    dcross_out[...] = nt(da2, co[...]).astype(BF16)
    wide[...] = tn(ctx[...], da2)
    scatter_rows(keep, send, wide, place, part, chunks * part + hidden_part, size)


def run_middle(info, first, ctx, og_own, og_other, w2, w_in, w_out, vec, fib):
    tokens, width = first.shape
    size = len(w2)
    part = width // size
    ff = w_in[0].shape[1]
    grad_rows = (ff // width) * part + w_out[0].shape[0] + part
    pack = as_struct((size // 2, grad_rows, width), BF16)
    return pl.pallas_call(
        functools.partial(middle_kernel, size),
        out_shape=(
            as_struct((tokens // 2, width), BF16),
            as_struct((tokens // 2, width), BF16),
            as_struct((tokens, width), F32),
            as_struct((tokens, width), BF16),
            pack,
            pack,
            as_struct((VEC_ROWS, width), F32),
        ),
        in_specs=[SMEM_SPEC] + [VMEM_SPEC] * (4 + 3 * size + 2),
        out_specs=(VMEM_SPEC,) * 7,
        scratch_shapes=[
            pltpu.VMEM((width, width), BF16),
            pltpu.VMEM((width, ff), BF16),
            pltpu.VMEM((ff, width), BF16),
            pltpu.VMEM((tokens, ff), F32),
            pltpu.VMEM((tokens, ff), BF16),
            pltpu.VMEM((width, width), F32),
        ],
        compiler_params=pltpu.CompilerParams(vmem_limit_bytes=VMEM_LIMIT),
        cost_estimate=cost(12 * tokens * width * ff, 2e7),
        name="middle",
    )(info, first, ctx, og_own, og_other, *w2, *w_in, *w_out, vec, fib)


def after_cross_kernel(size, info, dz2, dq, first_ref, x_ref, ctx, *rest):
    w2, rest = rest[:size], rest[size:]
    vec, dz1_out, dself_out, keep, send, vecs, weight, wide = rest
    place = info[0]
    width = x_ref.shape[1]
    part = width // size
    for i in range(2):
        assemble(weight, w2, place, part, i * part, i)

    def vector(i):
        return vec[i : i + 1, :]

    vecs[...] = jnp.zeros_like(vecs)
    dfirst = dz2[...] + SCALE * nt(dq[...], weight[1])
    resid = x_ref[...].astype(F32) + nn(ctx[...], weight[0]) + vector(SBO)
    normed, inverse = norm(resid)
    dz1 = norm_back(dfirst, normed, inverse, vector(N1G))
    vecs[N1G : N1G + 1] = row_sum(dfirst * normed)
    vecs[N1B : N1B + 1] = row_sum(dfirst)
    vecs[CBQ : CBQ + 1] = row_sum(dq[...].astype(F32)) * SCALE
    dz1_out[...] = dz1
    da1 = dz1.astype(BF16)
    vecs[SBO : SBO + 1] = row_sum(da1.astype(F32))
    dself_out[...] = nt(da1, weight[0]).astype(BF16)
    wide[...] = tn(ctx[...], da1)
    scatter_rows(keep, send, wide, place, part, 0, size)
    wide[...] = tn(first_ref[...], dq[...]) * SCALE
    scatter_rows(keep, send, wide, place, part, part, size)


def run_after_cross(info, dz2, dq, first, x, ctx, w2, vec):
    tokens, width = x.shape
    size = len(w2)
    pack = as_struct((size // 2, 2 * (width // size), width), BF16)
    return pl.pallas_call(
        functools.partial(after_cross_kernel, size),
        out_shape=(
            as_struct((tokens, width), F32),
            as_struct((tokens, width), BF16),
            pack,
            pack,
            as_struct((VEC_ROWS, width), F32),
        ),
        in_specs=[SMEM_SPEC] + [VMEM_SPEC] * (6 + size),
        out_specs=(VMEM_SPEC,) * 5,
        scratch_shapes=[pltpu.VMEM((2, width, width), BF16), pltpu.VMEM((width, width), F32)],
        compiler_params=pltpu.CompilerParams(vmem_limit_bytes=VMEM_LIMIT),
        cost_estimate=cost(10 * tokens * width * width, 8e6),
        name="after_cross",
    )(info, dz2, dq, first, x, ctx, *w2, vec)


def encoder_back_kernel(size, info, own, got, x_ref, *rest):
    w2, rest = rest[:size], rest[size:]
    keep_out, pass_out, keep, send, vecs, weight, wide = rest
    place = info[0]
    width = x_ref.shape[1]
    rows = x_ref.shape[0] // 2
    part = width // size
    for i in range(2):
        assemble(weight, w2, place, part, (2 + i) * part, i)
    vecs[...] = jnp.zeros_like(vecs)
    total = None
    for i in range(2):
        grad = (own[i].astype(F32) + got[i].astype(F32)).astype(BF16)
        if i == 1:
            vecs[CBV : CBV + 1] = row_sum(grad.astype(F32))
        wide[...] = tn(x_ref[...], grad)
        scatter_rows(keep, send, wide, place, part, i * part, size)
        term = nt(grad, weight[i])
        total = term if total is None else total + term
    total = total.astype(BF16)
    keep_out[...] = total[:rows]
    pass_out[...] = total[rows:]


def run_encoder_back(info, own, got, x, w2):
    tokens, width = x.shape
    size = len(w2)
    pack = as_struct((size // 2, 2 * (width // size), width), BF16)
    return pl.pallas_call(
        functools.partial(encoder_back_kernel, size),
        out_shape=(
            as_struct((tokens // 2, width), BF16),
            as_struct((tokens // 2, width), BF16),
            pack,
            pack,
            as_struct((VEC_ROWS, width), F32),
        ),
        in_specs=[SMEM_SPEC] + [VMEM_SPEC] * (3 + size),
        out_specs=(VMEM_SPEC,) * 5,
        scratch_shapes=[pltpu.VMEM((2, width, width), BF16), pltpu.VMEM((width, width), F32)],
        compiler_params=pltpu.CompilerParams(vmem_limit_bytes=VMEM_LIMIT),
        cost_estimate=cost(8 * tokens * width * width, 8e6),
        name="encoder_back",
    )(info, own, got, x, *w2)


def target_back_kernel(size, info, dz1, dq, own, got, x_ref, *rest):
    w1, rest = rest[:size], rest[size:]
    keep_out, pass_out, keep, send, vecs, weight, wide = rest
    place = info[0]
    width = x_ref.shape[1]
    rows = x_ref.shape[0] // 2
    part = width // size
    for i in range(3):
        assemble(weight, w1, place, part, i * part, i)
    vecs[...] = jnp.zeros_like(vecs)
    vecs[SBQ : SBQ + 1] = row_sum(dq[...].astype(F32)) * SCALE
    total = dz1[...] + SCALE * nt(dq[...], weight[0])
    wide[...] = tn(x_ref[...], dq[...]) * SCALE
    scatter_rows(keep, send, wide, place, part, 0, size)
    for i in range(2):
        grad = (own[i].astype(F32) + got[i].astype(F32)).astype(BF16)
        if i == 1:
            vecs[SBV : SBV + 1] = row_sum(grad.astype(F32))
        wide[...] = tn(x_ref[...], grad)
        scatter_rows(keep, send, wide, place, part, (1 + i) * part, size)
        total = total + nt(grad, weight[1 + i])
    total = total.astype(BF16)
    keep_out[...] = total[:rows]
    pass_out[...] = total[rows:]


def run_target_back(info, dz1, dq, own, got, x, w1):
    tokens, width = x.shape
    size = len(w1)
    pack = as_struct((size // 2, 3 * (width // size), width), BF16)
    return pl.pallas_call(
        functools.partial(target_back_kernel, size),
        out_shape=(
            as_struct((tokens // 2, width), BF16),
            as_struct((tokens // 2, width), BF16),
            pack,
            pack,
            as_struct((VEC_ROWS, width), F32),
        ),
        in_specs=[SMEM_SPEC] + [VMEM_SPEC] * (5 + size),
        out_specs=(VMEM_SPEC,) * 5,
        scratch_shapes=[pltpu.VMEM((3, width, width), BF16), pltpu.VMEM((width, width), F32)],
        compiler_params=pltpu.CompilerParams(vmem_limit_bytes=VMEM_LIMIT),
        cost_estimate=cost(12 * tokens * width * width, 8e6),
        name="target_back",
    )(info, dz1, dq, own, got, x, *w1)


def add(left, right):
    return (left.astype(F32) + right.astype(F32)).astype(BF16)


def sum_over_group(keep, send):
    got = send_xor(send, "group", 1)
    mask = 2
    parts = [add(keep[i], got[i]) for i in range(keep.shape[0])]
    while len(parts) > 1:
        arrived = [send_xor(p, "group", mask) for p in parts[1::2]]
        parts = [add(a, b) for a, b in zip(parts[0::2], arrived)]
        mask *= 2
    return parts[0]


def halves(value, dim):
    cut = value.shape[dim] // 2
    return lax.slice_in_dim(value, 0, cut, axis=dim), lax.slice_in_dim(value, cut, 2 * cut, axis=dim)


def sum_over_replicas(value):
    size = lax.axis_size("replica")
    place = lax.axis_index("replica")
    mask, dims = 1, []
    while mask < size:
        dim = 0 if mask == 1 else 1
        if value.shape[dim] % 2:
            dim = 1 - dim
        low, high = halves(value, dim)
        up = (place & mask) != 0
        arrived = send_xor(jnp.where(up, low, high), "replica", mask)
        value = add(jnp.where(up, high, low), arrived)
        dims.append((mask, dim))
        mask *= 2
    for mask, dim in reversed(dims):
        arrived = send_xor(value, "replica", mask)
        up = (place & mask) != 0
        value = jnp.where(
            up,
            jnp.concatenate([arrived, value], axis=dim),
            jnp.concatenate([value, arrived], axis=dim),
        )
    return value


def butterfly(stacked, place, size):
    bit = 1
    while bit < size:
        order = np.arange(size) ^ bit
        flipped = jnp.stack([stacked[int(i)] for i in order])
        stacked = jnp.where((place & bit) != 0, flipped, stacked)
        bit *= 2
    return stacked


def body(
    target, encoder, target_len, encoder_len,
    self_wq, self_wk, self_wv, self_wo, self_bq, self_bv, self_bo, norm1_gain, norm1_bias,
    cross_wq, cross_wk, cross_wv, cross_wo, cross_bq, cross_bv, cross_bo, norm2_gain, norm2_bias,
    ffn_in, ffn_in_bias, ffn_out, ffn_out_bias, norm3_gain, norm3_bias, out_grad,
):
    size = lax.axis_size("group")
    place = lax.axis_index("group")
    _, rows, width = target.shape
    part = width // size
    ff = ffn_in.shape[1]
    chunks = ff // width
    half = (place >= size // 2).astype(jnp.int32)
    table = jnp.asarray(group_table(size, rows))
    lengths = jnp.stack([target_len, encoder_len])[:, half]
    info = lax.dynamic_update_slice(table[place], lengths, (4,))
    mirror = [(i, size - 1 - i) for i in range(size)]

    def swap(value):
        return lax.ppermute(value, "group", mirror)

    def other_half(value):
        return lax.dynamic_index_in_dim(value, 1 - half, 0, keepdims=False)

    vec_own = jnp.concatenate(
        [
            v.reshape(-1, part)
            for v in (
                self_bq, self_bv, self_bo, norm1_gain, norm1_bias, cross_bq, cross_bv, cross_bo,
                norm2_gain, norm2_bias, ffn_out_bias, norm3_gain, norm3_bias, ffn_in_bias,
            )
        ]
    )
    used = vec_own.shape[0]
    vec_own = jnp.pad(vec_own, ((0, VEC_ROWS - used), (0, 0)))
    w1 = gather_xor(jnp.concatenate([self_wq, self_wk, self_wv]), "group", size)
    target_got = swap(other_half(target))
    vec_all = jnp.stack(gather_xor(vec_own, "group", size))
    vec_all = butterfly(vec_all, place, size)
    vec = jnp.transpose(vec_all, (1, 0, 2)).reshape(VEC_ROWS, width).astype(F32)
    fib = vec_all[:, FIB : FIB + ff // width].reshape(1, ff).astype(F32)
    encoder_got = swap(chain(other_half(encoder), target_got, w1[-1]))
    w2 = gather_xor(chain(jnp.concatenate([self_wo, cross_wq, cross_wk, cross_wv, cross_wo]), w1[size // 2], target_got), "group", size)
    w_in = gather_xor(chain(ffn_in, w2[size // 2]), "group", size)
    w_out = gather_xor(chain(ffn_out, w_in[size // 2]), "group", size)
    og_got = swap(chain(other_half(out_grad), w_in[size // 2]))

    x, q1, kv1 = run_qkv(info, target, target_got, w1, vec)
    kvs1 = gather_xor(kv1, "group", size // 2) if size > 2 else [kv1]
    xe, kv2 = run_cross_kv(info, encoder, encoder_got, w2, vec)
    kvs2 = gather_xor(kv2, "group", size // 2) if size > 2 else [kv2]
    ctx1, lse1 = run_forward(info, q1, kvs1, True)
    first, q2 = run_after_self(info, x, ctx1, w2, vec)
    ctx2, lse2 = run_forward(info, q2, kvs2, False)
    out_keep, out_pass, dz2, dcross, keep_a, send_a, vecs_a = run_middle(
        info, first, ctx2, out_grad, og_got, w2, w_in, w_out, vec, fib
    )

    def key_value_sums(parts):
        bit = len(parts) // 2
        while bit > 1:
            arrived = [send_xor(parts[k | bit], "group", bit) for k in range(bit)]
            parts = [add(parts[k], arrived[k]) for k in range(bit)]
            bit //= 2
        return parts[0], send_xor(parts[1], "group", 1)

    sum_a = sum_over_replicas(sum_over_group(keep_a, send_a))
    out_got = swap(out_pass)
    dq2, *dkvs2 = run_backward(info, q2, ctx2, lse2, dcross, kvs2, False)
    own2, got2 = key_value_sums(dkvs2)
    dz1, dself, keep_b, send_b, vecs_b = run_after_cross(info, dz2, dq2, first, x, ctx1, w2, vec)
    enc_keep, enc_pass, keep_e, send_e, vecs_e = run_encoder_back(info, own2, got2, xe, w2)
    enc_got = swap(enc_pass)
    sum_b = sum_over_replicas(
        sum_over_group(jnp.concatenate([keep_b, keep_e], axis=1), jnp.concatenate([send_b, send_e], axis=1))
    )
    dq1, *dkvs1 = run_backward(info, q1, ctx1, lse1, dself, kvs1, True)
    own1, got1 = key_value_sums(dkvs1)
    tgt_keep, tgt_pass, keep_c, send_c, vecs_c = run_target_back(info, dz1, dq1, own1, got1, x, w1)
    tgt_got = swap(tgt_pass)

    vecs = (vecs_a + vecs_b + vecs_e + vecs_c).astype(BF16)
    by_owner = jnp.transpose(vecs.reshape(VEC_ROWS, size, part), (1, 0, 2))
    hidden_bias = vecs[FIB : FIB + chunks].reshape(size, chunks, part)
    by_owner = jnp.concatenate([by_owner[:, :FIB], hidden_bias, by_owner[:, FIB + chunks :]], axis=1)
    by_slot = butterfly(by_owner, place, size).reshape(size // 2, 2, VEC_ROWS * part // width, width)
    spare = -(3 * part + by_slot.shape[2]) % 32
    by_slot = jnp.pad(by_slot, ((0, 0), (0, 0), (0, spare), (0, 0)))
    sum_c = sum_over_replicas(
        sum_over_group(
            jnp.concatenate([keep_c, by_slot[:, 0]], axis=1), jnp.concatenate([send_c, by_slot[:, 1]], axis=1)
        )
    )

    def unswap(kept, arrived):
        return jnp.where(half == 0, jnp.stack([kept, arrived]), jnp.stack([arrived, kept]))

    a = sum_a.astype(F32)
    b = sum_b.astype(F32)
    c = sum_c.astype(F32)
    g_fi = jnp.transpose(a[: chunks * part].reshape(chunks, part, width), (1, 0, 2)).reshape(part, ff)
    g_fo = a[chunks * part : chunks * part + ffn_out.shape[0]]
    g_co = a[chunks * part + ffn_out.shape[0] :]
    g_so, g_cq, g_ck, g_cv = (b[i * part : (i + 1) * part] for i in range(4))
    g_sq, g_sk, g_sv = (c[i * part : (i + 1) * part] for i in range(3))
    g_vec = c[3 * part : 3 * part + VEC_ROWS * part // width].reshape(VEC_ROWS, part)
    return (
        unswap(out_keep, out_got),
        unswap(tgt_keep, tgt_got),
        unswap(enc_keep, enc_got),
        g_sq, g_sk, g_sv, g_so, g_vec[SBQ], g_vec[SBV], g_vec[SBO], g_vec[N1G], g_vec[N1B],
        g_cq, g_ck, g_cv, g_co, g_vec[CBQ], g_vec[CBV], g_vec[CBO], g_vec[N2G], g_vec[N2B],
        g_fi, g_vec[FIB : FIB + chunks].reshape(-1), g_fo, g_vec[FOB], g_vec[N3G], g_vec[N3B],
    )


def solution(mesh):
    seq, lens, mat, vec = P("replica", "group", None), P("replica"), P("group", None), P("group")
    layer = (mat,) * 4 + (vec,) * 5 + (mat,) * 4 + (vec,) * 5 + (mat, vec, mat, vec, vec, vec)
    in_specs = (seq, seq, lens, lens) + layer + (seq,)
    out_specs = (seq,) * 3 + layer
    return jax.shard_map(body, mesh=mesh, in_specs=in_specs, out_specs=out_specs, check_vma=False)
```

```python
import functools

import jax
import jax.numpy as jnp
import numpy as np
from jax import lax
from jax.experimental import pallas as pl
from jax.experimental.pallas import tpu as pltpu
from jax.sharding import PartitionSpec as P

F32 = jnp.float32
BF16 = jnp.bfloat16
HEADS = 8
PAIR = 128
HALF = 64
SCALE = 0.125
NEGATIVE = -1e30
EPSILON = 1e-5
LOG2E = 1.4426950408889634
VMEM_LIMIT = 56 << 20

(SBQ, SBV, SBO, N1G, N1B, CBQ, CBV, CBO, N2G, N2B, FOB, N3G, N3B, FIB) = range(14)
VEC_ROWS = 32
INFO_HEAD = 7

VMEM_SPEC = pl.BlockSpec(memory_space=pltpu.VMEM)
LOHI = True
SMEM_SPEC = pl.BlockSpec(memory_space=pltpu.SMEM)


def nn(left, right):
    return lax.dot_general(left, right, (((1,), (0,)), ((), ())), preferred_element_type=F32)


def nt(left, right):
    return lax.dot_general(left, right, (((1,), (1,)), ((), ())), preferred_element_type=F32)


def tn(left, right):
    return lax.dot_general(left, right, (((0,), (0,)), ((), ())), preferred_element_type=F32)


def as_struct(shape, dtype):
    return jax.ShapeDtypeStruct(shape, dtype)


def cost(flops, nbytes):
    return pl.CostEstimate(flops=int(flops), bytes_accessed=int(nbytes), transcendentals=0)


def send_xor(value, axis, mask):
    size = lax.axis_size(axis)
    return lax.ppermute(value, axis, [(i, i ^ mask) for i in range(size)])


def gather_xor(value, axis, size):
    found = {0: value}
    bit = size // 2
    while bit:
        found.update({k | bit: send_xor(v, axis, bit) for k, v in list(found.items())})
        bit //= 2
    return [found[k] for k in range(size)]


def gather_even(value, axis, size):
    found = {0: value}
    bit = size // 2
    while bit > 1:
        found.update({k | bit: send_xor(v, axis, bit) for k, v in list(found.items())})
        bit //= 2
    return [found[k] for k in range(0, size, 2)]


def with_odd(evens, axis):
    odds = [send_xor(e, axis, 1) for e in evens]
    return [v for pair in zip(evens, odds) for v in pair]


def point(*values):
    return lax.optimization_barrier(values)


def group_table(size, rows):
    half = size // 2
    table = []
    for g in range(size):
        upper = g >= half
        low = min(g, size - 1 - g)
        row = [g, int(upper), low * rows, (size - 1 - low) * rows, 0, 0, 0]
        for k in range(half):
            d = min(g ^ k, size - 1 - (g ^ k))
            row += [d * rows, (size - 1 - d) * rows]

        def place(b):
            d = b if (b >= half) == upper else size - 1 - b
            return ((g ^ d) * 2 + int(b >= half)) * rows

        free = [(1, b) for b in range(half, size - 1 - low)] + [(0, b) for b in range(low)]
        row += [place(b) for b in range(half)]
        row += [s * rows for s, _ in free] + [place(b) for _, b in free]
        table.append(row)
    return np.asarray(table, np.int32)


def assemble(dest, refs, place, rows, source, index=None):
    for k, ref in enumerate(refs):
        start = pl.multiple_of((place ^ k) * rows, rows)
        block = ref[source : source + rows, :]
        if index is None:
            dest[pl.ds(start, rows), :] = block
        else:
            dest[index, pl.ds(start, rows), :] = block


def scatter_rows(keep, send, grad, place, rows, offset, size):
    for k in range(size):
        start = pl.multiple_of((place ^ k) * rows, rows)
        target = send if k & 1 else keep
        target[k >> 1, offset : offset + rows, :] = grad[pl.ds(start, rows), :].astype(BF16)


def norm(resid):
    centred = resid - jnp.mean(resid, axis=-1, keepdims=True)
    inverse = lax.rsqrt(jnp.mean(centred * centred, axis=-1, keepdims=True) + EPSILON)
    return centred * inverse, inverse


def norm_back(grad, normed, inverse, gain):
    scaled = grad * gain
    return inverse * (
        scaled
        - jnp.mean(scaled, axis=-1, keepdims=True)
        - normed * jnp.mean(scaled * normed, axis=-1, keepdims=True)
    )


def ordered(info, own, other):
    upper = info[1] == 1
    return jnp.where(upper, other, own), jnp.where(upper, own, other)


def row_sum(value):
    return jnp.sum(value, axis=0, keepdims=True)


def qkv_kernel(size, info, own, other, *rest):
    ws, (vec, x_out, q_out, kv_out, weight) = rest[: 3 * size], rest[3 * size :]
    place, half = info[0], info[1]
    rows, width = other.shape
    part = width // size
    for i in range(3):
        assemble(weight, ws[i * size : (i + 1) * size], place, part, 0, i)
    x = jnp.concatenate(ordered(info, own[half], other[...]), axis=0)
    x_out[...] = x
    q_out[...] = ((nn(x, weight[0]) + vec[SBQ : SBQ + 1, :]) * SCALE).astype(BF16)
    kv_out[0] = nn(x, weight[1]).astype(BF16)
    kv_out[1] = (nn(x, weight[2]) + vec[SBV : SBV + 1, :]).astype(BF16)


def run_qkv(info, own, other, ws, vec):
    rows, width = other.shape
    tokens = 2 * rows
    return pl.pallas_call(
        functools.partial(qkv_kernel, len(ws) // 3),
        out_shape=(
            as_struct((tokens, width), BF16),
            as_struct((tokens, width), BF16),
            as_struct((2, tokens, width), BF16),
        ),
        in_specs=[SMEM_SPEC] + [VMEM_SPEC] * (3 + len(ws)),
        out_specs=(VMEM_SPEC,) * 3,
        scratch_shapes=[pltpu.VMEM((3, width, width), BF16)],
        compiler_params=pltpu.CompilerParams(vmem_limit_bytes=VMEM_LIMIT),
        cost_estimate=cost(6 * tokens * width * width, 4e6),
        name="qkv",
    )(info, own, other, *ws, vec)


def cross_kv_kernel(size, info, own, other, *rest):
    ws, (vec, x_out, kv_out, weight) = rest[:size], rest[size:]
    place, half = info[0], info[1]
    rows, width = other.shape
    part = width // size
    for i in range(2):
        assemble(weight, ws, place, part, (2 + i) * part, i)
    x = jnp.concatenate(ordered(info, own[half], other[...]), axis=0)
    x_out[...] = x
    kv_out[0] = nn(x, weight[0]).astype(BF16)
    kv_out[1] = (nn(x, weight[1]) + vec[CBV : CBV + 1, :]).astype(BF16)


def run_cross_kv(info, own, other, ws, vec):
    rows, width = other.shape
    tokens = 2 * rows
    return pl.pallas_call(
        functools.partial(cross_kv_kernel, len(ws)),
        out_shape=(as_struct((tokens, width), BF16), as_struct((2, tokens, width), BF16)),
        in_specs=[SMEM_SPEC] + [VMEM_SPEC] * (3 + len(ws)),
        out_specs=(VMEM_SPEC,) * 2,
        scratch_shapes=[pltpu.VMEM((2, width, width), BF16)],
        compiler_params=pltpu.CompilerParams(vmem_limit_bytes=VMEM_LIMIT),
        cost_estimate=cost(4 * tokens * width * width, 4e6),
        name="cross_kv",
    )(info, own, other, *ws, vec)


def after_self_kernel(size, info, x_ref, ctx, *rest):
    ws, (vec, first_out, q_out, weight) = rest[:size], rest[size:]
    place = info[0]
    width = x_ref.shape[1]
    part = width // size
    for i in range(2):
        assemble(weight, ws, place, part, i * part, i)
    resid = x_ref[...].astype(F32) + nn(ctx[...], weight[0]) + vec[SBO : SBO + 1, :]
    normed, _ = norm(resid)
    first = (normed * vec[N1G : N1G + 1, :] + vec[N1B : N1B + 1, :]).astype(BF16)
    first_out[...] = first
    q_out[...] = ((nn(first, weight[1]) + vec[CBQ : CBQ + 1, :]) * SCALE).astype(BF16)


def run_after_self(info, x, ctx, ws, vec):
    tokens, width = x.shape
    return pl.pallas_call(
        functools.partial(after_self_kernel, len(ws)),
        out_shape=(as_struct((tokens, width), BF16),) * 2,
        in_specs=[SMEM_SPEC] + [VMEM_SPEC] * (3 + len(ws)),
        out_specs=(VMEM_SPEC,) * 2,
        scratch_shapes=[pltpu.VMEM((2, width, width), BF16)],
        compiler_params=pltpu.CompilerParams(vmem_limit_bytes=VMEM_LIMIT),
        cost_estimate=cost(4 * tokens * width * width, 4e6),
        name="after_self",
    )(info, x, ctx, *ws, vec)


def lanes_of(rows):
    return lax.broadcasted_iota(jnp.int32, (rows, PAIR), 1)


def lane_row(head):
    return ((lax.broadcasted_iota(jnp.int32, (1, PAIR), 1) // HALF) == head).astype(F32).astype(BF16)


def split3(value):
    a = value.astype(BF16)
    rest = value - a.astype(F32)
    b = rest.astype(BF16)
    c = (rest - b.astype(F32)).astype(BF16)
    return a, b, c


def lane_pieces(value, base, rows):
    lane = lanes_of(rows)
    a, b, c = (p.astype(F32) for p in split3(value))
    return jnp.where(lane == base, a, jnp.where(lane == base + 1, b, jnp.where(lane == base + 2, c, 0.0)))


def put_key_extras(kx, info, count, rows, limit, ones):
    for p in range(count):
        for slot in range(2):
            at = (2 * p + slot) * rows
            pos = info[INFO_HEAD + 2 * p + slot] + lax.broadcasted_iota(jnp.int32, (rows, PAIR), 0)
            lane = lanes_of(rows)
            for head in range(2):
                spare = HALF * (1 - head)
                extra = jnp.where((lane == spare) & (pos >= limit), NEGATIVE, 0.0)
                if ones:
                    extra = jnp.where((lane > spare) & (lane < spare + 4), 1.0, extra)
                kx[head, at : at + rows] = extra.astype(BF16)


def put_operands(dest, parts, head, extra):
    mine = lane_row(head)
    at = 0
    for part in parts:
        rows = part.shape[0]
        add_on = extra[at : at + rows] if extra.shape[0] > 1 else extra
        dest[head, at : at + rows] = part * mine + add_on
        at += rows


def one_lanes(head, first, last):
    lane = lax.broadcasted_iota(jnp.int32, (1, PAIR), 1) - HALF * (1 - head)
    return jnp.where((lane >= first) & (lane < last), 1.0, 0.0).astype(BF16)


def finish_rows(acc, top, head):
    rows = acc.shape[0]
    spare = HALF * (1 - head)
    total = acc[:, spare : spare + 1]
    return acc / total, lane_pieces(-(top + jnp.log(total)), spare + 1, rows)


def forward_operands(count, info, limit, q_ref, kvs, qa, ka, va, kx):
    rows = q_ref.shape[0] // 2

    @pl.when(pl.program_id(0) == 0)
    def _():
        put_key_extras(kx, info, count, rows, limit, False)

    for head in range(2):
        put_operands(qa, [q_ref[...]], head, one_lanes(head, 0, 1))
        put_operands(ka, [kv[0] for kv in kvs], head, kx.at[head])
        put_operands(va, [kv[1] for kv in kvs], head, one_lanes(head, 0, 1))


def weights_of(logits, top):
    return jnp.exp2((logits - top) * LOG2E).astype(BF16)


def store_heads(ctx_out, lse_out, cut, done):
    (context_a, pieces_a), (context_b, pieces_b) = done
    lane = lanes_of(context_a.shape[0])
    ctx_out[cut] = jnp.where(lane < HALF, context_a, context_b).astype(BF16)
    lse_out[cut] = (pieces_a + pieces_b).astype(BF16)


def cross_forward_kernel(count, info, q_ref, *rest):
    kvs, (ctx_out, lse_out, qa, ka, va, kx) = rest[:count], rest[count:]
    rows = q_ref.shape[0] // 2
    forward_operands(count, info, info[5], q_ref, kvs, qa, ka, va, kx)
    for c in range(2):
        cut = slice(c * rows, (c + 1) * rows)
        done = []
        for head in range(2):
            logits = nt(qa[head, cut], ka[head])
            top = jnp.max(logits, axis=-1, keepdims=True)
            done.append(finish_rows(nn(weights_of(logits, top), va[head]), top, head))
        store_heads(ctx_out, lse_out, cut, done)


def causal_mask(rows, transposed):
    a = lax.broadcasted_iota(jnp.int32, (rows, rows), 0)
    b = lax.broadcasted_iota(jnp.int32, (rows, rows), 1)
    return a <= b if transposed else b <= a


def tile_rows(info, count, rows):
    base = INFO_HEAD + 2 * count

    def at(i):
        return pl.multiple_of(info[base + i], rows)

    fixed = [at(i) for i in range(count)]
    free = [(at(count + i), at(2 * count - 1 + i)) for i in range(count - 1)]
    return fixed, free


def self_forward_kernel(count, info, q_ref, *rest):
    kvs, (ctx_out, lse_out, qa, ka, va, kx) = rest[:count], rest[count:]
    rows = q_ref.shape[0] // 2
    low, high = slice(0, rows), slice(rows, 2 * rows)
    forward_operands(count, info, info[4], q_ref, kvs, qa, ka, va, kx)
    causal = causal_mask(rows, False)
    fixed, free = tile_rows(info, count, rows)
    done = []
    for head in range(2):

        def logits_of(q_cut, k_cut):
            return nt(qa[head, q_cut], ka[head, k_cut])

        key_cuts = [pl.ds(k, rows) for k in fixed] + [high]
        tiles = [logits_of(high, k) for k in key_cuts]
        tiles[-1] = jnp.where(causal, tiles[-1], NEGATIVE)
        tile_low = jnp.where(causal, logits_of(low, low), NEGATIVE)
        extra = [logits_of(pl.ds(q, rows), pl.ds(k, rows)) for q, k in free]
        to_high = [q > 0 for q, _ in free]

        def widest(tile):
            return jnp.max(tile, axis=-1, keepdims=True)

        top_high = widest(functools.reduce(jnp.maximum, tiles))
        top_low = widest(tile_low)
        for tile, is_high in zip(extra, to_high):
            top = widest(tile)
            top_high = jnp.where(is_high, jnp.maximum(top_high, top), top_high)
            top_low = jnp.where(is_high, top_low, jnp.maximum(top_low, top))
        acc_high = sum(nn(weights_of(t, top_high), va[head, k]) for t, k in zip(tiles, key_cuts))
        acc_low = nn(weights_of(tile_low, top_low), va[head, low])
        for tile, is_high, (_, k) in zip(extra, to_high, free):
            part = nn(weights_of(tile, jnp.where(is_high, top_high, top_low)), va[head, pl.ds(k, rows)])
            acc_high = acc_high + jnp.where(is_high, part, 0.0)
            acc_low = acc_low + jnp.where(is_high, 0.0, part)
        done.append((finish_rows(acc_low, top_low, head), finish_rows(acc_high, top_high, head)))
    store_heads(ctx_out, lse_out, low, [d[0] for d in done])
    store_heads(ctx_out, lse_out, high, [d[1] for d in done])


def attention_specs(count, tokens, first=0):
    wide = pl.BlockSpec((tokens, PAIR), lambda i: (0, i + first))
    kv = pl.BlockSpec((2, tokens, PAIR), lambda i: (0, 0, i + first))
    lse = pl.BlockSpec((None, tokens, PAIR), lambda i: (i + first, 0, 0))
    return wide, kv, lse


def run_forward(info, q, kvs, causal):
    tokens, width = q.shape
    count = len(kvs)
    keys = count * tokens
    pairs = width // PAIR
    wide, kv, lse = attention_specs(count, tokens)
    kernel = functools.partial(self_forward_kernel if causal else cross_forward_kernel, count)
    return pl.pallas_call(
        kernel,
        grid=(pairs,),
        out_shape=(as_struct((tokens, width), BF16), as_struct((pairs, tokens, PAIR), BF16)),
        in_specs=[SMEM_SPEC, wide] + [kv] * count,
        out_specs=(wide, lse),
        scratch_shapes=[
            pltpu.VMEM((2, tokens, PAIR), BF16),
            pltpu.VMEM((2, keys, PAIR), BF16),
            pltpu.VMEM((2, keys, PAIR), BF16),
            pltpu.VMEM((2, keys, PAIR), BF16),
        ],
        compiler_params=pltpu.CompilerParams(vmem_limit_bytes=VMEM_LIMIT),
        cost_estimate=cost(8e9, 4e6),
        name="self_forward" if causal else "cross_forward",
    )(info, q, *kvs)


def backward_operands(count, info, limit, q_ref, ctx, lse, grad, kvs, qa, ga, ka, va, kx):
    tokens = q_ref.shape[0]
    rows = tokens // 2

    @pl.when(pl.program_id(0) == 0)
    def _():
        put_key_extras(kx, info, count, rows, limit, True)

    lane = lanes_of(tokens)
    both = grad[...].astype(F32) * ctx[...].astype(F32)
    for head in range(2):
        mine = (lane // HALF) == head
        spare = HALF * (1 - head)
        far = lane_row(1 - head)
        delta = jnp.sum(jnp.where(mine, both, 0.0), axis=-1, keepdims=True)
        put_operands(qa, [q_ref[...]], head, lse[...] * far + one_lanes(head, 0, 1))
        put_operands(ga, [grad[...]], head, lane_pieces(-delta, spare, tokens).astype(BF16))
        put_operands(ka, [kv[0] for kv in kvs], head, kx.at[head])
        put_operands(va, [kv[1] for kv in kvs], head, one_lanes(head, 0, 3))


def both_heads(a, b):
    return jnp.where(lanes_of(a.shape[0]) < HALF, a, b)


def cross_backward_kernel(count, info, q_ref, ctx, lse, grad, *rest):
    kvs, rest = rest[:count], rest[count:]
    dq_out, dkvs, (qa, ga, ka, va, kx) = rest[0], rest[1 : 1 + count], rest[1 + count :]
    tokens = q_ref.shape[0]
    rows = tokens // 2
    backward_operands(count, info, info[5], q_ref, ctx, lse, grad, kvs, qa, ga, ka, va, kx)
    dq = [jnp.zeros((PAIR, tokens), F32)] * 2
    for p in range(count):
        for slot in range(2):
            at = (2 * p + slot) * rows
            cut = slice(slot * rows, (slot + 1) * rows)
            keys = kvs[p][0, cut]
            dk, dv = [], []
            for head in range(2):
                probs = jnp.exp2(nt(ka[head, at : at + rows], qa[head]) * LOG2E)
                scores = (probs * nt(va[head, at : at + rows], ga[head])).astype(BF16)
                dv.append(nn(probs.astype(BF16), grad[...]))
                dk.append(nn(scores, q_ref[...]))
                dq[head] = dq[head] + tn(keys, scores)
            dkvs[p][0, cut] = both_heads(*dk).astype(BF16)
            dkvs[p][1, cut] = both_heads(*dv).astype(BF16)
    top = lax.broadcasted_iota(jnp.int32, (PAIR, tokens), 0) < HALF
    dq_out[...] = jnp.where(top, dq[0], dq[1]).T.astype(BF16)


def self_backward_kernel(count, info, q_ref, ctx, lse, grad, *rest):
    kvs, rest = rest[:count], rest[count:]
    dq_out, dkvs, (qa, ga, ka, va, kx, k_all, parts, total) = rest[0], rest[1 : 1 + count], rest[1 + count :]
    tokens = q_ref.shape[0]
    rows = tokens // 2
    low, high = slice(0, rows), slice(rows, 2 * rows)
    backward_operands(count, info, info[4], q_ref, ctx, lse, grad, kvs, qa, ga, ka, va, kx)
    for p in range(count):
        k_all[p * tokens : (p + 1) * tokens] = kvs[p][0]
    causal = causal_mask(rows, True)
    fixed, free = tile_rows(info, count, rows)
    tiles = [(high, pl.ds(k, rows), False, None) for k in fixed]
    tiles += [(high, high, True, None), (low, low, True, None)]
    tiles += [(pl.ds(q, rows), pl.ds(k, rows), False, q > 0) for q, k in free]
    dq_low, dq_high = [0.0, 0.0], [0.0, 0.0]
    for t, (q_cut, k_cut, masked, is_high) in enumerate(tiles):
        dk, dv = [], []
        for head in range(2):
            logits = nt(ka[head, k_cut], qa[head, q_cut])
            if masked:
                logits = jnp.where(causal, logits, NEGATIVE)
            probs = jnp.exp2(logits * LOG2E)
            scores = (probs * nt(va[head, k_cut], ga[head, q_cut])).astype(BF16)
            dv.append(nn(probs.astype(BF16), grad[q_cut]))
            dk.append(nn(scores, q_ref[q_cut]))
            part = tn(k_all[k_cut], scores)
            if q_cut is high:
                dq_high[head] = dq_high[head] + part
            elif q_cut is low:
                dq_low[head] = dq_low[head] + part
            else:
                dq_high[head] = dq_high[head] + jnp.where(is_high, part, 0.0)
                dq_low[head] = dq_low[head] + jnp.where(is_high, 0.0, part)
        parts[0, t] = both_heads(*dk)
        parts[1, t] = both_heads(*dv)
    top = lax.broadcasted_iota(jnp.int32, (PAIR, rows), 0) < HALF
    dq_out[low] = jnp.where(top, *dq_low).T.astype(BF16)
    dq_out[high] = jnp.where(top, *dq_high).T.astype(BF16)
    total[...] = jnp.zeros_like(total)
    for i in range(2):
        total[i, high] = parts[i, count]
        total[i, low] = parts[i, count + 1]
    base = INFO_HEAD + 2 * count

    @pl.loop(0, 2 * count - 1)
    def _(t):
        is_free = (t >= count).astype(jnp.int32)
        at = pl.multiple_of(info[base + t + is_free * (count - 1)], rows)
        for i in range(2):
            total[i, pl.ds(at, rows)] += parts[i, t + 2 * is_free]

    for p in range(count):
        cut = slice(p * tokens, (p + 1) * tokens)
        for i in range(2):
            dkvs[p][i] = total[i, cut].astype(BF16)


def run_backward(info, q, ctx, lse, grad, kvs, causal, first=0, pairs=None):
    tokens, width = q.shape
    pairs = pairs or width // PAIR
    width = pairs * PAIR
    rows = tokens // 2
    count = len(kvs)
    keys = count * tokens
    wide, kv, lse_spec = attention_specs(count, tokens, first)
    wide_out, kv_out, _ = attention_specs(count, tokens)
    scratch = [pltpu.VMEM((2, tokens, PAIR), BF16)] * 2 + [pltpu.VMEM((2, keys, PAIR), BF16)] * 3
    if causal:
        scratch += [
            pltpu.VMEM((keys, PAIR), BF16),
            pltpu.VMEM((2, 2 * count + 1, rows, PAIR), F32),
            pltpu.VMEM((2, keys, PAIR), F32),
        ]
    return pl.pallas_call(
        functools.partial(self_backward_kernel if causal else cross_backward_kernel, count),
        grid=(pairs,),
        out_shape=(as_struct((tokens, width), BF16),) + (as_struct((2, tokens, width), BF16),) * count,
        in_specs=[SMEM_SPEC, wide, wide, lse_spec, wide] + [kv] * count,
        out_specs=(wide_out,) + (kv_out,) * count,
        scratch_shapes=scratch,
        compiler_params=pltpu.CompilerParams(vmem_limit_bytes=VMEM_LIMIT),
        cost_estimate=cost(2.5e9 * pairs, 6e6),
        name="self_backward" if causal else "cross_backward",
    )(info, q, ctx, lse, grad, *kvs)


def middle_kernel(size, info, first_ref, ctx, og_own, og_other, *rest):
    w2, w3, rest = rest[:size], rest[size : 3 * size], rest[3 * size :]
    vec, fib, keep_out, pass_out, dz2_out, dcross_out, keep, send, vecs, co, fi, fo, pre, scr, wide = rest
    place, half = info[0], info[1]
    tokens, width = first_ref.shape
    rows = tokens // 2
    part = width // size
    hidden_part = fo.shape[0] // size
    chunks = fi.shape[1] // width
    assemble(co, w2, place, part, 4 * part)
    for i, ref in enumerate(w3):
        owner, which = place ^ (i // 2), info[6] ^ (i % 2)
        small, large = part // 2, hidden_part // 2
        start = pl.multiple_of(owner * part + which * small, small)
        for c in range(chunks):
            fi[pl.ds(start, small), c * width : (c + 1) * width] = ref[c * small : (c + 1) * small, :]
        start = pl.multiple_of(owner * hidden_part + which * large, large)
        fo[pl.ds(start, large), :] = ref[chunks * small :, :]

    def vector(i):
        return vec[i : i + 1, :]

    resid2 = first_ref[...].astype(F32) + nn(ctx[...], co[...]) + vector(CBO)
    normed2, inverse2 = norm(resid2)
    second = (normed2 * vector(N2G) + vector(N2B)).astype(BF16)
    branch = jnp.zeros((tokens, width), F32)
    for c in range(chunks):
        cut = slice(c * width, (c + 1) * width)
        value = nn(second, fi[:, cut]) + fib[:, cut]
        pre[:, cut] = value
        hidden = (value * (0.5 * jnp.tanh(0.5 * value) + 0.5)).astype(BF16)
        scr[:, cut] = hidden
        branch = branch + nn(hidden, fo[cut])
    resid3 = second.astype(F32) + branch + vector(FOB)
    normed3, inverse3 = norm(resid3)
    out = (normed3 * vector(N3G) + vector(N3B)).astype(BF16)
    keep_out[...], pass_out[...] = ordered(info, out[:rows], out[rows:])

    live = info[4]
    iota = lax.broadcasted_iota(jnp.int32, (rows, 1), 0)
    low, high = ordered(info, og_own[half], og_other[...])
    grad3 = jnp.concatenate(
        [
            jnp.where(iota + info[2] < live, low.astype(F32), 0.0),
            jnp.where(iota + info[3] < live, high.astype(F32), 0.0),
        ],
        axis=0,
    )
    dz3 = norm_back(grad3, normed3, inverse3, vector(N3G))
    vecs[...] = jnp.zeros_like(vecs)
    vecs[N3G : N3G + 1] = row_sum(grad3 * normed3)
    vecs[N3B : N3B + 1] = row_sum(grad3)
    dy = dz3.astype(BF16)
    vecs[FOB : FOB + 1] = row_sum(dy.astype(F32))
    dsecond = dz3
    for c in range(chunks):
        cut = slice(c * width, (c + 1) * width)
        wide[...] = tn(scr[:, cut], dy)
        for b in range(width // min(hidden_part, width)):
            row = c * width + b * hidden_part
            owner = row // hidden_part
            block = wide[b * hidden_part : (b + 1) * hidden_part].astype(BF16)
            slot = place ^ owner

            @pl.when((slot & 1) == 0)
            def _():
                keep[slot >> 1, chunks * part : chunks * part + hidden_part, :] = block

            @pl.when((slot & 1) == 1)
            def _():
                send[slot >> 1, chunks * part : chunks * part + hidden_part, :] = block

        value = pre[:, cut]
        sig = 0.5 * jnp.tanh(0.5 * value) + 0.5
        dpre = (nt(dy, fo[cut]) * (sig * (1.0 + value * (1.0 - sig)))).astype(BF16)
        vecs[FIB + c : FIB + c + 1] = row_sum(dpre.astype(F32))
        dsecond = dsecond + nt(dpre, fi[:, cut])
        wide[...] = tn(second, dpre)
        scatter_rows(keep, send, wide, place, part, c * part, size)
    dz2 = norm_back(dsecond, normed2, inverse2, vector(N2G))
    vecs[N2G : N2G + 1] = row_sum(dsecond * normed2)
    vecs[N2B : N2B + 1] = row_sum(dsecond)
    dz2_out[...] = dz2
    da2 = dz2.astype(BF16)
    vecs[CBO : CBO + 1] = row_sum(da2.astype(F32))
    dcross_out[...] = nt(da2, co[...]).astype(BF16)
    wide[...] = tn(ctx[...], da2)
    scatter_rows(keep, send, wide, place, part, chunks * part + hidden_part, size)


def run_middle(info, first, ctx, og_own, og_other, w2, w3, vec, fib):
    tokens, width = first.shape
    size = len(w2)
    part = width // size
    ff = fib.shape[1]
    grad_rows = (ff // width) * part + ff // size + part
    pack = as_struct((size // 2, grad_rows, width), BF16)
    return pl.pallas_call(
        functools.partial(middle_kernel, size),
        out_shape=(
            as_struct((tokens // 2, width), BF16),
            as_struct((tokens // 2, width), BF16),
            as_struct((tokens, width), F32),
            as_struct((tokens, width), BF16),
            pack,
            pack,
            as_struct((VEC_ROWS, width), F32),
        ),
        in_specs=[SMEM_SPEC] + [VMEM_SPEC] * (4 + 3 * size + 2),
        out_specs=(VMEM_SPEC,) * 7,
        scratch_shapes=[
            pltpu.VMEM((width, width), BF16),
            pltpu.VMEM((width, ff), BF16),
            pltpu.VMEM((ff, width), BF16),
            pltpu.VMEM((tokens, ff), F32),
            pltpu.VMEM((tokens, ff), BF16),
            pltpu.VMEM((width, width), F32),
        ],
        compiler_params=pltpu.CompilerParams(vmem_limit_bytes=VMEM_LIMIT),
        cost_estimate=cost(12 * tokens * width * ff, 2e7),
        name="middle",
    )(info, first, ctx, og_own, og_other, *w2, *w3, vec, fib)


def after_cross_kernel(size, info, dz2, dq, first_ref, x_ref, ctx, *rest):
    w2, rest = rest[:size], rest[size:]
    vec, dz1_out, dself_out, keep, send, vecs, weight, wide = rest
    place = info[0]
    width = x_ref.shape[1]
    part = width // size
    for i in range(2):
        assemble(weight, w2, place, part, i * part, i)

    def vector(i):
        return vec[i : i + 1, :]

    vecs[...] = jnp.zeros_like(vecs)
    dfirst = dz2[...] + SCALE * nt(dq[...], weight[1])
    resid = x_ref[...].astype(F32) + nn(ctx[...], weight[0]) + vector(SBO)
    normed, inverse = norm(resid)
    dz1 = norm_back(dfirst, normed, inverse, vector(N1G))
    vecs[N1G : N1G + 1] = row_sum(dfirst * normed)
    vecs[N1B : N1B + 1] = row_sum(dfirst)
    vecs[CBQ : CBQ + 1] = row_sum(dq[...].astype(F32)) * SCALE
    dz1_out[...] = dz1
    da1 = dz1.astype(BF16)
    vecs[SBO : SBO + 1] = row_sum(da1.astype(F32))
    dself_out[...] = nt(da1, weight[0]).astype(BF16)
    wide[...] = tn(ctx[...], da1)
    scatter_rows(keep, send, wide, place, part, 0, size)
    wide[...] = tn(first_ref[...], dq[...]) * SCALE
    scatter_rows(keep, send, wide, place, part, part, size)


def run_after_cross(info, dz2, dq, first, x, ctx, w2, vec):
    tokens, width = x.shape
    size = len(w2)
    pack = as_struct((size // 2, 2 * (width // size), width), BF16)
    return pl.pallas_call(
        functools.partial(after_cross_kernel, size),
        out_shape=(
            as_struct((tokens, width), F32),
            as_struct((tokens, width), BF16),
            pack,
            pack,
            as_struct((VEC_ROWS, width), F32),
        ),
        in_specs=[SMEM_SPEC] + [VMEM_SPEC] * (6 + size),
        out_specs=(VMEM_SPEC,) * 5,
        scratch_shapes=[pltpu.VMEM((2, width, width), BF16), pltpu.VMEM((width, width), F32)],
        compiler_params=pltpu.CompilerParams(vmem_limit_bytes=VMEM_LIMIT),
        cost_estimate=cost(10 * tokens * width * width, 8e6),
        name="after_cross",
    )(info, dz2, dq, first, x, ctx, *w2, vec)


def encoder_back_kernel(size, info, own, got, x_ref, *rest):
    w2, rest = rest[:size], rest[size:]
    keep_out, pass_out, keep, send, vecs, weight, wide = rest
    place = info[0]
    width = x_ref.shape[1]
    rows = x_ref.shape[0] // 2
    part = width // size
    for i in range(2):
        assemble(weight, w2, place, part, (2 + i) * part, i)
    vecs[...] = jnp.zeros_like(vecs)
    total = None
    for i in range(2):
        grad = (own[i].astype(F32) + got[i].astype(F32)).astype(BF16)
        if i == 1:
            vecs[CBV : CBV + 1] = row_sum(grad.astype(F32))
        wide[...] = tn(x_ref[...], grad)
        scatter_rows(keep, send, wide, place, part, i * part, size)
        term = nt(grad, weight[i])
        total = term if total is None else total + term
    total = total.astype(BF16)
    keep_out[...], pass_out[...] = ordered(info, total[:rows], total[rows:])


def run_encoder_back(info, own, got, x, w2):
    tokens, width = x.shape
    size = len(w2)
    pack = as_struct((size // 2, 2 * (width // size), width), BF16)
    return pl.pallas_call(
        functools.partial(encoder_back_kernel, size),
        out_shape=(
            as_struct((tokens // 2, width), BF16),
            as_struct((tokens // 2, width), BF16),
            pack,
            pack,
            as_struct((VEC_ROWS, width), F32),
        ),
        in_specs=[SMEM_SPEC] + [VMEM_SPEC] * (3 + size),
        out_specs=(VMEM_SPEC,) * 5,
        scratch_shapes=[pltpu.VMEM((2, width, width), BF16), pltpu.VMEM((width, width), F32)],
        compiler_params=pltpu.CompilerParams(vmem_limit_bytes=VMEM_LIMIT),
        cost_estimate=cost(8 * tokens * width * width, 8e6),
        name="encoder_back",
    )(info, own, got, x, *w2)


def side_by_side(refs):
    return jnp.concatenate([ref[...] for ref in refs], axis=-1)


def target_back_kernel(size, info, dz1, dq_a, dq_b, own_a, own_b, got_a, got_b, x_ref, *rest):
    w1, rest = rest[: 3 * size], rest[3 * size :]
    keep_out, pass_out, keep, send, vecs, weight, wide = rest
    place = info[0]
    width = x_ref.shape[1]
    rows = x_ref.shape[0] // 2
    part = width // size
    for i in range(3):
        assemble(weight, w1[i * size : (i + 1) * size], place, part, 0, i)
    vecs[...] = jnp.zeros_like(vecs)
    dq = side_by_side((dq_a, dq_b))
    vecs[SBQ : SBQ + 1] = row_sum(dq.astype(F32)) * SCALE
    total = dz1[...] + SCALE * nt(dq, weight[0])
    wide[...] = tn(x_ref[...], dq) * SCALE
    scatter_rows(keep, send, wide, place, part, 0, size)
    for i in range(2):
        own = side_by_side((own_a.at[i], own_b.at[i])).astype(F32)
        grad = (own + side_by_side((got_a.at[i], got_b.at[i])).astype(F32)).astype(BF16)
        if i == 1:
            vecs[SBV : SBV + 1] = row_sum(grad.astype(F32))
        wide[...] = tn(x_ref[...], grad)
        scatter_rows(keep, send, wide, place, part, (1 + i) * part, size)
        total = total + nt(grad, weight[1 + i])
    total = total.astype(BF16)
    keep_out[...], pass_out[...] = ordered(info, total[:rows], total[rows:])


def run_target_back(info, dz1, dqs, owns, gots, x, w1):
    tokens, width = x.shape
    size = len(w1) // 3
    pack = as_struct((size // 2, 3 * (width // size), width), BF16)
    return pl.pallas_call(
        functools.partial(target_back_kernel, size),
        out_shape=(
            as_struct((tokens // 2, width), BF16),
            as_struct((tokens // 2, width), BF16),
            pack,
            pack,
            as_struct((VEC_ROWS, width), F32),
        ),
        in_specs=[SMEM_SPEC] + [VMEM_SPEC] * (8 + 3 * size),
        out_specs=(VMEM_SPEC,) * 5,
        scratch_shapes=[pltpu.VMEM((3, width, width), BF16), pltpu.VMEM((width, width), F32)],
        compiler_params=pltpu.CompilerParams(vmem_limit_bytes=VMEM_LIMIT),
        cost_estimate=cost(12 * tokens * width * width, 8e6),
        name="target_back",
    )(info, dz1, *dqs, *owns, *gots, x, *w1)


def add(left, right):
    return (left.astype(F32) + right.astype(F32)).astype(BF16)


def sum_over_cores(keep, send):
    got = send_xor(send, "group", 1)
    return [add(keep[i], got[i]) for i in range(keep.shape[0])]


def sum_over_chips(parts):
    mask = 2
    while len(parts) > 1:
        arrived = [send_xor(p, "group", mask) for p in parts[1::2]]
        parts = [add(a, b) for a, b in zip(parts[0::2], arrived)]
        mask *= 2
    return parts[0]


def halves(value, dim):
    cut = value.shape[dim] // 2
    return lax.slice_in_dim(value, 0, cut, axis=dim), lax.slice_in_dim(value, cut, 2 * cut, axis=dim)


class ReplicaSum:
    def __init__(self, value):
        self.value = value
        self.size = lax.axis_size("replica")
        self.place = lax.axis_index("replica")
        masks = [1 << i for i in range(self.size.bit_length() - 1)]
        self.steps = [(m, True) for m in masks] + [(m, False) for m in reversed(masks)]
        self.dims = {}

    def start(self):
        mask, down = self.steps[0]
        up = (self.place & mask) != 0
        if down:
            dim = 0 if mask == 1 else 1
            if self.value.shape[dim] % 2:
                dim = 1 - dim
            self.dims[mask] = dim
            low, high = halves(self.value, dim)
            self.value = jnp.where(up, high, low)
            self.arrived = send_xor(jnp.where(up, low, high), "replica", mask)
        else:
            self.arrived = send_xor(self.value, "replica", mask)

    def finish(self):
        mask, down = self.steps.pop(0)
        if down:
            self.value = add(self.value, self.arrived)
        else:
            up = (self.place & mask) != 0
            dim = self.dims[mask]
            self.value = jnp.where(
                up,
                jnp.concatenate([self.arrived, self.value], axis=dim),
                jnp.concatenate([self.value, self.arrived], axis=dim),
            )


def butterfly(stacked, place, size):
    bit = 1
    while bit < size:
        order = np.arange(size) ^ bit
        flipped = jnp.stack([stacked[int(i)] for i in order])
        stacked = jnp.where((place & bit) != 0, flipped, stacked)
        bit *= 2
    return stacked


def body(
    target, encoder, target_len, encoder_len,
    self_wq, self_wk, self_wv, self_wo, self_bq, self_bv, self_bo, norm1_gain, norm1_bias,
    cross_wq, cross_wk, cross_wv, cross_wo, cross_bq, cross_bv, cross_bo, norm2_gain, norm2_bias,
    ffn_in, ffn_in_bias, ffn_out, ffn_out_bias, norm3_gain, norm3_bias, out_grad,
):
    size = lax.axis_size("group")
    place = lax.axis_index("group")
    _, rows, width = target.shape
    part = width // size
    ff = ffn_in.shape[1]
    chunks = ff // width
    half = (place >= size // 2).astype(jnp.int32)
    table = jnp.asarray(group_table(size, rows))
    side = lax.axis_index("replica") & 1
    lengths = jnp.append(jnp.stack([target_len, encoder_len])[:, half], side)
    info = lax.dynamic_update_slice(table[place], lengths, (4,))
    mirror = [(i, size - 1 - i) for i in range(size)]

    def swap(value):
        return lax.ppermute(value, "group", mirror)

    def other_half(value):
        return lax.dynamic_index_in_dim(value, 1 - half, 0, keepdims=False)

    vec_own = jnp.concatenate(
        [
            v.reshape(-1, part)
            for v in (
                self_bq, self_bv, self_bo, norm1_gain, norm1_bias, cross_bq, cross_bv, cross_bo,
                norm2_gain, norm2_bias, ffn_out_bias, norm3_gain, norm3_bias, ffn_in_bias,
            )
        ]
    )
    used = vec_own.shape[0]
    vec_own = jnp.pad(vec_own, ((0, VEC_ROWS - used), (0, 0)))
    w1 = [v for w in (self_wq, self_wk, self_wv) for v in gather_even(w, "group", size)]
    w1_odd = [send_xor(w, "group", 1) for w in (self_wq, self_wk, self_wv)]
    target_got = swap(other_half(target))
    ffn_in, ffn_out, self_wo, cross_wq, cross_wk, cross_wv, cross_wo, *w1_odd = point(
        ffn_in, ffn_out, self_wo, cross_wq, cross_wk, cross_wv, cross_wo, *w1_odd
    )
    w2_own = jnp.concatenate([self_wo, cross_wq, cross_wk, cross_wv, cross_wo])
    ffn = [
        jnp.concatenate(
            [ffn_in[cut, c * width : (c + 1) * width] for c in range(chunks)] + [ffn_out[large]]
        )
        for cut, large in (
            (slice(i * part // 2, (i + 1) * part // 2), slice(i * ff // size // 2, (i + 1) * ff // size // 2))
            for i in range(2)
        )
    ]
    w3_own = [jnp.where(side == 0, ffn[0], ffn[1]), jnp.where(side == 0, ffn[1], ffn[0])]
    vec_all = jnp.stack(gather_xor(vec_own, "group", size))
    vec_all = butterfly(vec_all, place, size)
    vec = jnp.transpose(vec_all, (1, 0, 2)).reshape(VEC_ROWS, width).astype(F32)
    fib = vec_all[:, FIB : FIB + chunks].reshape(1, ff).astype(F32)
    w2_own, encoder_half, target_got, *w1 = point(w2_own, other_half(encoder), target_got, *w1)
    each = size // 2
    w1 = [
        v
        for i in range(3)
        for j in range(each)
        for v in (w1[i * each + j], w1_odd[i] if j == 0 else send_xor(w1[i * each + j], "group", 1))
    ]
    w2 = gather_even(w2_own, "group", size)
    encoder_got = swap(encoder_half)

    x, q1, kv1 = run_qkv(info, target, target_got, w1, vec)
    kvs1 = gather_xor(kv1, "group", size // 2)
    ctx1, lse1 = run_forward(info, q1, kvs1, True)
    w3_odd = [send_xor(w, "group", 1) for w in w3_own]
    w3_first, ctx1, encoder_got, *w2 = point(w3_own[0], ctx1, encoder_got, *w2)
    w2 = with_odd(w2, "group")
    w3_even = gather_even(w3_first, "group", size)[1:]
    xe, kv2 = run_cross_kv(info, encoder, encoder_got, w2, vec)
    kv2, ctx1 = point(kv2, ctx1)
    kvs2 = gather_xor(kv2, "group", size // 2)
    first, q2 = run_after_self(info, x, ctx1, w2, vec)
    first, q2, og_half, *w3_even = point(first, q2, other_half(out_grad), *w3_even)
    w3_even = [(w, send_xor(w, "replica", 1)) for w in w3_even]
    w3_pass = [send_xor(w, "group", 1) for w, _ in w3_even]
    og_got = swap(og_half)
    ctx2, lse2 = run_forward(info, q2, kvs2, False)
    ctx2, *w3_even = point(ctx2, *[v for pair in w3_even for v in pair])
    w3_even = list(zip(w3_even[::2], w3_even[1::2]))
    w3 = [*w3_own, *w3_odd]
    for (near, far), passed in zip(w3_even, w3_pass):
        w3 += [near, far, passed, send_xor(far, "group", 1)]
    out_keep, out_pass, dz2, dcross, keep_a, send_a, vecs_a = run_middle(
        info, first, ctx2, out_grad, og_got, w2, w3, vec, fib
    )

    def key_value_sums(parts):
        bit = len(parts) // 2
        while bit > 1:
            arrived = [send_xor(parts[k | bit], "group", bit) for k in range(bit)]
            parts = [add(parts[k], arrived[k]) for k in range(bit)]
            bit //= 2
        return parts[0], send_xor(parts[1], "group", 1)

    dcross, *parts_a = point(dcross, *sum_over_cores(keep_a, send_a))
    part_a = sum_over_chips(parts_a)
    dq2, *dkvs2 = run_backward(info, q2, ctx2, lse2, dcross, kvs2, False)
    dq2, out_pass, *dkvs2 = point(dq2, out_pass, *dkvs2)
    own2, got2 = key_value_sums(dkvs2)
    dz1, dself, keep_b, send_b, vecs_b = run_after_cross(info, dz2, dq2, first, x, ctx1, w2, vec)
    dself, part_a, got2, out_pass = point(dself, part_a, got2, out_pass)
    sum_a = ReplicaSum(part_a)
    sum_a.start()
    out_got = swap(out_pass)
    enc_keep, enc_pass, keep_e, send_e, vecs_e = run_encoder_back(info, own2, got2, xe, w2)
    dself, enc_pass, *parts_b = point(
        dself,
        enc_pass,
        *sum_over_cores(jnp.concatenate([keep_b, keep_e], axis=1), jnp.concatenate([send_b, send_e], axis=1)),
    )
    part_b = sum_over_chips(parts_b)
    enc_got = swap(enc_pass)
    pairs = width // PAIR // 2
    dq1_a, *dkvs1_a = run_backward(info, q1, ctx1, lse1, dself, kvs1, True, 0, pairs)
    dself, sum_a.arrived, *dkvs1_a = point(dself, sum_a.arrived, *dkvs1_a)
    own1_a, got1_a = key_value_sums(dkvs1_a)
    sum_a.finish()
    sum_a.start()
    dq1_b, *dkvs1_b = run_backward(info, q1, ctx1, lse1, dself, kvs1, True, pairs, pairs)
    part_b, dq1_b, sum_a.arrived, *dkvs1_b = point(part_b, dq1_b, sum_a.arrived, *dkvs1_b)
    own1_b, got1_b = key_value_sums(dkvs1_b)
    sum_b = ReplicaSum(part_b)
    sum_b.start()
    sum_a.finish()
    sum_a.start()
    tgt_keep, tgt_pass, keep_c, send_c, vecs_c = run_target_back(
        info, dz1, (dq1_a, dq1_b), (own1_a, own1_b), (got1_a, got1_b), x, w1
    )

    vecs = (vecs_a + vecs_b + vecs_e + vecs_c).astype(BF16)
    by_owner = jnp.transpose(vecs.reshape(VEC_ROWS, size, part), (1, 0, 2))
    hidden_bias = vecs[FIB : FIB + chunks].reshape(size, chunks, part)
    by_owner = jnp.concatenate([by_owner[:, :FIB], hidden_bias, by_owner[:, FIB + chunks :]], axis=1)
    by_slot = butterfly(by_owner, place, size).reshape(size // 2, 2, VEC_ROWS * part // width, width)
    spare = -(3 * part + by_slot.shape[2]) % 32
    by_slot = jnp.pad(by_slot, ((0, 0), (0, 0), (0, spare), (0, 0)))
    keep_c = jnp.concatenate([keep_c, by_slot[:, 0]], axis=1)
    send_c = jnp.concatenate([send_c, by_slot[:, 1]], axis=1)
    tgt_pass, sum_a.arrived, sum_b.arrived, keep_c, send_c = point(
        tgt_pass, sum_a.arrived, sum_b.arrived, keep_c, send_c
    )

    def advance(*sums):
        for s in sums:
            s.finish()
            s.start()

    advance(sum_a, sum_b)
    tgt_pass, sum_a.arrived, sum_b.arrived, *parts_c = point(
        tgt_pass, sum_a.arrived, sum_b.arrived, *sum_over_cores(keep_c, send_c)
    )
    advance(sum_a, sum_b)
    tgt_pass, sum_a.arrived, sum_b.arrived, part_c = point(
        tgt_pass, sum_a.arrived, sum_b.arrived, sum_over_chips(parts_c)
    )
    advance(sum_a, sum_b)
    sum_c = ReplicaSum(part_c)
    sum_c.start()
    tgt_got = swap(tgt_pass)
    sum_b.arrived, sum_c.arrived = point(sum_b.arrived, sum_c.arrived)
    advance(sum_b, sum_c)
    sum_a.arrived, sum_b.arrived, sum_c.arrived = point(sum_a.arrived, sum_b.arrived, sum_c.arrived)
    sum_a.finish()
    advance(sum_b, sum_c)
    sum_c.arrived, = point(sum_c.arrived)
    advance(sum_c)
    while sum_a.steps:
        sum_a.start()
        sum_a.finish()
    sum_b.arrived, sum_c.arrived = point(sum_b.arrived, sum_c.arrived)
    sum_b.finish()
    while sum_b.steps:
        sum_b.start()
        sum_b.finish()
    sum_c.finish()
    while sum_c.steps:
        sum_c.start()
        sum_c.finish()

    def unswap(kept, arrived):
        return jnp.where(half == 0, jnp.stack([kept, arrived]), jnp.stack([arrived, kept]))

    a = sum_a.value.astype(F32)
    b = sum_b.value.astype(F32)
    c = sum_c.value.astype(F32)
    g_fi = jnp.transpose(a[: chunks * part].reshape(chunks, part, width), (1, 0, 2)).reshape(part, ff)
    g_fo = a[chunks * part : chunks * part + ffn_out.shape[0]]
    g_co = a[chunks * part + ffn_out.shape[0] :]
    g_so, g_cq, g_ck, g_cv = (b[i * part : (i + 1) * part] for i in range(4))
    g_sq, g_sk, g_sv = (c[i * part : (i + 1) * part] for i in range(3))
    g_vec = c[3 * part : 3 * part + VEC_ROWS * part // width].reshape(VEC_ROWS, part)
    return (
        unswap(out_keep, out_got),
        unswap(tgt_keep, tgt_got),
        unswap(enc_keep, enc_got),
        g_sq, g_sk, g_sv, g_so, g_vec[SBQ], g_vec[SBV], g_vec[SBO], g_vec[N1G], g_vec[N1B],
        g_cq, g_ck, g_cv, g_co, g_vec[CBQ], g_vec[CBV], g_vec[CBO], g_vec[N2G], g_vec[N2B],
        g_fi, g_vec[FIB : FIB + chunks].reshape(-1), g_fo, g_vec[FOB], g_vec[N3G], g_vec[N3B],
    )


def solution(mesh):
    seq, lens, mat, vec = P("replica", "group", None), P("replica"), P("group", None), P("group")
    layer = (mat,) * 4 + (vec,) * 5 + (mat,) * 4 + (vec,) * 5 + (mat, vec, mat, vec, vec, vec)
    in_specs = (seq, seq, lens, lens) + layer + (seq,)
    out_specs = (seq,) * 3 + layer
    return jax.shard_map(body, mesh=mesh, in_specs=in_specs, out_specs=out_specs, check_vma=False)
```

```python
import functools

import jax
import jax.numpy as jnp
import numpy as np
from jax import lax
from jax.experimental import pallas as pl
from jax.experimental.pallas import tpu as pltpu
from jax.sharding import PartitionSpec as P

F32 = jnp.float32
BF16 = jnp.bfloat16
HEADS = 8
PAIR = 128
HALF = 64
SCALE = 0.125
NEGATIVE = -1e30
EPSILON = 1e-5
LOG2E = 1.4426950408889634
VMEM_LIMIT = 56 << 20

(SBQ, SBV, SBO, N1G, N1B, CBQ, CBV, CBO, N2G, N2B, FOB, N3G, N3B, FIB) = range(14)
VEC_ROWS = 32
INFO_HEAD = 7

VMEM_SPEC = pl.BlockSpec(memory_space=pltpu.VMEM)
LOHI = True
ROW_SPLIT = 1
SMEM_SPEC = pl.BlockSpec(memory_space=pltpu.SMEM)


def nn(left, right):
    return lax.dot_general(left, right, (((1,), (0,)), ((), ())), preferred_element_type=F32)


def nt(left, right):
    return lax.dot_general(left, right, (((1,), (1,)), ((), ())), preferred_element_type=F32)


def tn(left, right):
    return lax.dot_general(left, right, (((0,), (0,)), ((), ())), preferred_element_type=F32)


def as_struct(shape, dtype):
    return jax.ShapeDtypeStruct(shape, dtype)


def cost(flops, nbytes):
    return pl.CostEstimate(flops=1000, bytes_accessed=1000, transcendentals=0)


def send_xor(value, axis, mask):
    size = lax.axis_size(axis)
    return lax.ppermute(value, axis, [(i, i ^ mask) for i in range(size)])


def gather_xor(value, axis, size):
    found = {0: value}
    bit = size // 2
    while bit:
        found.update({k | bit: send_xor(v, axis, bit) for k, v in list(found.items())})
        bit //= 2
    return [found[k] for k in range(size)]


def gather_even(value, axis, size):
    found = {0: value}
    bit = size // 2
    while bit > 1:
        found.update({k | bit: send_xor(v, axis, bit) for k, v in list(found.items())})
        bit //= 2
    return [found[k] for k in range(0, size, 2)]


def with_odd(evens, axis):
    odds = [send_xor(e, axis, 1) for e in evens]
    return [v for pair in zip(evens, odds) for v in pair]


def point(*values):
    return lax.optimization_barrier(values)


def group_table(size, rows):
    half = size // 2
    table = []
    for g in range(size):
        upper = g >= half
        low = min(g, size - 1 - g)
        row = [g, int(upper), low * rows, (size - 1 - low) * rows, 0, 0, 0]
        for k in range(half):
            d = min(g ^ k, size - 1 - (g ^ k))
            row += [d * rows, (size - 1 - d) * rows]

        def place(b):
            d = b if (b >= half) == upper else size - 1 - b
            return ((g ^ d) * 2 + int(b >= half)) * rows

        free = [(1, b) for b in range(half, size - 1 - low)] + [(0, b) for b in range(low)]
        row += [place(b) for b in range(half)]
        row += [s * rows for s, _ in free] + [place(b) for _, b in free]
        table.append(row)
    return np.asarray(table, np.int32)


def assemble(dest, refs, place, rows, source, index=None):
    for k, ref in enumerate(refs):
        start = pl.multiple_of((place ^ k) * rows, rows)
        block = ref[source : source + rows, :]
        if index is None:
            dest[pl.ds(start, rows), :] = block
        else:
            dest[index, pl.ds(start, rows), :] = block


def scatter_rows(slots, grad, place, rows, offset):
    for k, slot in enumerate(slots):
        start = pl.multiple_of((place ^ k) * rows, rows)
        slot[offset : offset + rows, :] = grad[pl.ds(start, rows), :].astype(BF16)


def norm(resid):
    centred = resid - jnp.mean(resid, axis=-1, keepdims=True)
    inverse = lax.rsqrt(jnp.mean(centred * centred, axis=-1, keepdims=True) + EPSILON)
    return centred * inverse, inverse


def norm_back(grad, normed, inverse, gain):
    scaled = grad * gain
    return inverse * (
        scaled
        - jnp.mean(scaled, axis=-1, keepdims=True)
        - normed * jnp.mean(scaled * normed, axis=-1, keepdims=True)
    )


def ordered(info, own, other):
    upper = info[1] == 1
    return jnp.where(upper, other, own), jnp.where(upper, own, other)


def row_sum(value):
    return jnp.sum(value, axis=0, keepdims=True)


def qkv_kernel(size, info, own, other, *rest):
    ws, (vec, x_out, q_out, kv_out, weight) = rest[:size], rest[size:]
    place, half = info[0], info[1]
    rows, width = other.shape
    part = width // size
    for i in range(3):
        assemble(weight, ws, place, part, i * part, i)
    x = jnp.concatenate(ordered(info, own[half], other[...]), axis=0)
    x_out[...] = x
    q_out[...] = ((nn(x, weight[0]) + vec[SBQ : SBQ + 1, :]) * SCALE).astype(BF16)
    kv_out[0] = nn(x, weight[1]).astype(BF16)
    kv_out[1] = (nn(x, weight[2]) + vec[SBV : SBV + 1, :]).astype(BF16)


def run_qkv(info, own, other, ws, vec):
    rows, width = other.shape
    tokens = 2 * rows
    return pl.pallas_call(
        functools.partial(qkv_kernel, len(ws)),
        out_shape=(
            as_struct((tokens, width), BF16),
            as_struct((tokens, width), BF16),
            as_struct((2, tokens, width), BF16),
        ),
        in_specs=[SMEM_SPEC] + [VMEM_SPEC] * (3 + len(ws)),
        out_specs=(VMEM_SPEC,) * 3,
        scratch_shapes=[pltpu.VMEM((3, width, width), BF16)],
        compiler_params=pltpu.CompilerParams(vmem_limit_bytes=VMEM_LIMIT),
        cost_estimate=cost(6 * tokens * width * width, 4e6),
        name="qkv",
    )(info, own, other, *ws, vec)


def first_pack_kernel(info, target, wq, wk, wv, w_out, other_out):
    part = wq.shape[0]
    for i, w in enumerate((wq, wk, wv)):
        w_out[i * part : (i + 1) * part] = w[...]
    other_out[...] = target[1 - info[1]]


def run_first_pack(info, target, ws):
    _, rows, width = target.shape
    return pl.pallas_call(
        first_pack_kernel,
        out_shape=(as_struct((3 * ws[0].shape[0], width), BF16), as_struct((rows, width), BF16)),
        in_specs=[SMEM_SPEC] + [VMEM_SPEC] * 4,
        out_specs=(VMEM_SPEC,) * 2,
        compiler_params=pltpu.CompilerParams(vmem_limit_bytes=VMEM_LIMIT),
        cost_estimate=cost(0, 0),
        name="first_pack",
    )(info, target, *ws)


def second_pack_kernel(info, encoder, og, w_in, w_out, *refs):
    ws, (w2_out, near_out, far_out, enc_out, og_out) = refs[:5], refs[5:]
    part, width = ws[0].shape
    for i, w in enumerate(ws):
        w2_out[i * part : (i + 1) * part] = w[...]
    enc_out[...] = encoder[1 - info[1]]
    og_out[...] = og[1 - info[1]]
    small, large = part // 2, w_out.shape[0] // 2
    chunks = w_in.shape[1] // width
    for which, out in enumerate((near_out, far_out)):
        at = pl.multiple_of((info[6] ^ which) * small, small)
        for c in range(chunks):
            out[c * small : (c + 1) * small] = w_in[pl.ds(at, small), c * width : (c + 1) * width]
        at = pl.multiple_of((info[6] ^ which) * large, large)
        out[chunks * small :] = w_out[pl.ds(at, large)]


def run_second_pack(info, encoder, og, w_in, w_out, ws):
    _, rows, width = encoder.shape
    block = as_struct((rows, width), BF16)
    half = as_struct((w_in.shape[0] // 2 * (w_in.shape[1] // width) + w_out.shape[0] // 2, width), BF16)
    return pl.pallas_call(
        second_pack_kernel,
        out_shape=(as_struct((5 * ws[0].shape[0], width), BF16), half, half, block, block),
        in_specs=[SMEM_SPEC] + [VMEM_SPEC] * 9,
        out_specs=(VMEM_SPEC,) * 5,
        compiler_params=pltpu.CompilerParams(vmem_limit_bytes=VMEM_LIMIT),
        cost_estimate=cost(0, 0),
        name="second_pack",
    )(info, encoder, og, w_in, w_out, *ws)


def cross_kv_kernel(size, info, own, other, *rest):
    ws, (vec, x_out, kv_out, weight) = rest[:size], rest[size:]
    place, half = info[0], info[1]
    rows, width = other.shape
    part = width // size
    for i in range(2):
        assemble(weight, ws, place, part, (2 + i) * part, i)
    x = jnp.concatenate(ordered(info, own[half], other[...]), axis=0)
    x_out[...] = x
    kv_out[0] = nn(x, weight[0]).astype(BF16)
    kv_out[1] = (nn(x, weight[1]) + vec[CBV : CBV + 1, :]).astype(BF16)


def run_cross_kv(info, own, other, ws, vec):
    rows, width = other.shape
    tokens = 2 * rows
    return pl.pallas_call(
        functools.partial(cross_kv_kernel, len(ws)),
        out_shape=(as_struct((tokens, width), BF16), as_struct((2, tokens, width), BF16)),
        in_specs=[SMEM_SPEC] + [VMEM_SPEC] * (3 + len(ws)),
        out_specs=(VMEM_SPEC,) * 2,
        scratch_shapes=[pltpu.VMEM((2, width, width), BF16)],
        compiler_params=pltpu.CompilerParams(vmem_limit_bytes=VMEM_LIMIT),
        cost_estimate=cost(4 * tokens * width * width, 4e6),
        name="cross_kv",
    )(info, own, other, *ws, vec)


def after_self_kernel(size, info, x_ref, ctx, *rest):
    ws, (vec, first_out, q_out, weight) = rest[:size], rest[size:]
    place = info[0]
    width = x_ref.shape[1]
    part = width // size
    for i in range(2):
        assemble(weight, ws, place, part, i * part, i)
    resid = x_ref[...].astype(F32) + nn(ctx[...], weight[0]) + vec[SBO : SBO + 1, :]
    normed, _ = norm(resid)
    first = (normed * vec[N1G : N1G + 1, :] + vec[N1B : N1B + 1, :]).astype(BF16)
    first_out[...] = first
    q_out[...] = ((nn(first, weight[1]) + vec[CBQ : CBQ + 1, :]) * SCALE).astype(BF16)


def run_after_self(info, x, ctx, ws, vec):
    tokens, width = x.shape
    return pl.pallas_call(
        functools.partial(after_self_kernel, len(ws)),
        out_shape=(as_struct((tokens, width), BF16),) * 2,
        in_specs=[SMEM_SPEC] + [VMEM_SPEC] * (3 + len(ws)),
        out_specs=(VMEM_SPEC,) * 2,
        scratch_shapes=[pltpu.VMEM((2, width, width), BF16)],
        compiler_params=pltpu.CompilerParams(vmem_limit_bytes=VMEM_LIMIT),
        cost_estimate=cost(4 * tokens * width * width, 4e6),
        name="after_self",
    )(info, x, ctx, *ws, vec)


def lanes_of(rows):
    return lax.broadcasted_iota(jnp.int32, (rows, PAIR), 1)


def lane_row(head):
    return ((lax.broadcasted_iota(jnp.int32, (1, PAIR), 1) // HALF) == head).astype(F32).astype(BF16)


def split3(value):
    a = value.astype(BF16)
    rest = value - a.astype(F32)
    b = rest.astype(BF16)
    c = (rest - b.astype(F32)).astype(BF16)
    return a, b, c


def lane_pieces(value, base, rows):
    lane = lanes_of(rows)
    a, b, c = (p.astype(F32) for p in split3(value))
    return jnp.where(lane == base, a, jnp.where(lane == base + 1, b, jnp.where(lane == base + 2, c, 0.0)))


def put_key_extras(kx, info, count, rows, limit, ones):
    for p in range(count):
        for slot in range(2):
            at = (2 * p + slot) * rows
            pos = info[INFO_HEAD + 2 * p + slot] + lax.broadcasted_iota(jnp.int32, (rows, PAIR), 0)
            lane = lanes_of(rows)
            for head in range(2):
                spare = HALF * (1 - head)
                extra = jnp.where((lane == spare) & (pos >= limit), NEGATIVE, 0.0)
                if ones:
                    extra = jnp.where((lane > spare) & (lane < spare + 4), 1.0, extra)
                kx[head, at : at + rows] = extra.astype(BF16)


def put_operands(dest, parts, head, extra):
    mine = lane_row(head)
    at = 0
    for part in parts:
        rows = part.shape[0]
        add_on = extra[at : at + rows] if extra.shape[0] > 1 else extra
        dest[head, at : at + rows] = part * mine + add_on
        at += rows


def one_lanes(head, first, last):
    lane = lax.broadcasted_iota(jnp.int32, (1, PAIR), 1) - HALF * (1 - head)
    return jnp.where((lane >= first) & (lane < last), 1.0, 0.0).astype(BF16)


def finish_rows(acc, top, head):
    rows = acc.shape[0]
    spare = HALF * (1 - head)
    total = acc[:, spare : spare + 1]
    return acc / total, lane_pieces(-(top + jnp.log(total)), spare + 1, rows)


def forward_operands(count, info, limit, q_ref, kvs, qa, ka, va, kx):
    rows = q_ref.shape[0] // 2

    @pl.when(pl.program_id(0) == 0)
    def _():
        put_key_extras(kx, info, count, rows, limit, False)

    for head in range(2):
        put_operands(qa, [q_ref[...]], head, one_lanes(head, 0, 1))
        put_operands(ka, [kv[0] for kv in kvs], head, kx.at[head])
        put_operands(va, [kv[1] for kv in kvs], head, one_lanes(head, 0, 1))


def weights_of(logits, top):
    return jnp.exp2((logits - top) * LOG2E).astype(BF16)


def store_heads(ctx_out, lse_out, cut, done):
    (context_a, pieces_a), (context_b, pieces_b) = done
    lane = lanes_of(context_a.shape[0])
    ctx_out[cut] = jnp.where(lane < HALF, context_a, context_b).astype(BF16)
    lse_out[cut] = (pieces_a + pieces_b).astype(BF16)


def cross_forward_kernel(count, info, q_ref, *rest):
    kvs, (ctx_out, lse_out, qa, ka, va, kx) = rest[:count], rest[count:]
    rows = q_ref.shape[0] // 2
    forward_operands(count, info, info[5], q_ref, kvs, qa, ka, va, kx)
    step = rows // ROW_SPLIT
    units = [(c, head) for c in range(2 * ROW_SPLIT) for head in range(2)]

    def logits_of(unit):
        c, head = unit
        return nt(qa[head, c * step : (c + 1) * step], ka[head])

    logits, weights, done = {0: logits_of(units[0])}, {}, {}
    for u in range(len(units) + 1):
        if u + 1 < len(units):
            logits[u + 1] = logits_of(units[u + 1])
        if u < len(units):
            now = logits.pop(u)
            top = jnp.max(now, axis=-1, keepdims=True)
            weights[u] = (weights_of(now, top), top)
        if u > 0:
            c, head = units[u - 1]
            probs, top = weights.pop(u - 1)
            done[head] = finish_rows(nn(probs, va[head]), top, head)
            if head == 1:
                store_heads(ctx_out, lse_out, slice(c * step, (c + 1) * step), (done[0], done[1]))


def causal_mask(rows, transposed):
    a = lax.broadcasted_iota(jnp.int32, (rows, rows), 0)
    b = lax.broadcasted_iota(jnp.int32, (rows, rows), 1)
    return a <= b if transposed else b <= a


def tile_rows(info, count, rows):
    base = INFO_HEAD + 2 * count

    def at(i):
        return pl.multiple_of(info[base + i], rows)

    fixed = [at(i) for i in range(count)]
    free = [(at(count + i), at(2 * count - 1 + i)) for i in range(count - 1)]
    return fixed, free


def self_forward_kernel(count, info, q_ref, *rest):
    kvs, (ctx_out, lse_out, qa, ka, va, kx) = rest[:count], rest[count:]
    rows = q_ref.shape[0] // 2
    low, high = slice(0, rows), slice(rows, 2 * rows)
    forward_operands(count, info, info[4], q_ref, kvs, qa, ka, va, kx)
    causal = causal_mask(rows, False)
    fixed, free = tile_rows(info, count, rows)
    key_cuts = [pl.ds(k, rows) for k in fixed] + [high]
    to_high = [q > 0 for q, _ in free]

    def widest(tile):
        return jnp.max(tile, axis=-1, keepdims=True)

    def products(head):
        def logits_of(q_cut, k_cut):
            return nt(qa[head, q_cut], ka[head, k_cut])

        tiles = [logits_of(high, k) for k in key_cuts]
        tile_low = logits_of(low, low)
        extra = [logits_of(pl.ds(q, rows), pl.ds(k, rows)) for q, k in free]
        return tiles, tile_low, extra

    def weigh(tiles, tile_low, extra):
        tiles[-1] = jnp.where(causal, tiles[-1], NEGATIVE)
        tile_low = jnp.where(causal, tile_low, NEGATIVE)
        top_high = widest(functools.reduce(jnp.maximum, tiles))
        top_low = widest(tile_low)
        for tile, is_high in zip(extra, to_high):
            top = widest(tile)
            top_high = jnp.where(is_high, jnp.maximum(top_high, top), top_high)
            top_low = jnp.where(is_high, top_low, jnp.maximum(top_low, top))
        free_weights = [
            weights_of(tile, jnp.where(is_high, top_high, top_low)) for tile, is_high in zip(extra, to_high)
        ]
        return [weights_of(t, top_high) for t in tiles], weights_of(tile_low, top_low), free_weights, top_high, top_low

    def contexts(head, tiles, tile_low, extra, top_high, top_low):
        acc_high = sum(nn(t, va[head, k]) for t, k in zip(tiles, key_cuts))
        acc_low = nn(tile_low, va[head, low])
        for tile, is_high, (_, k) in zip(extra, to_high, free):
            part = nn(tile, va[head, pl.ds(k, rows)])
            acc_high = acc_high + jnp.where(is_high, part, 0.0)
            acc_low = acc_low + jnp.where(is_high, 0.0, part)
        return finish_rows(acc_low, top_low, head), finish_rows(acc_high, top_high, head)

    first, second = products(0), products(1)
    first = weigh(*first)
    first = contexts(0, *first)
    second = contexts(1, *weigh(*second))
    store_heads(ctx_out, lse_out, low, (first[0], second[0]))
    store_heads(ctx_out, lse_out, high, (first[1], second[1]))


def attention_specs(count, tokens, first=0):
    wide = pl.BlockSpec((tokens, PAIR), lambda i: (0, i + first))
    kv = pl.BlockSpec((2, tokens, PAIR), lambda i: (0, 0, i + first))
    lse = pl.BlockSpec((None, tokens, PAIR), lambda i: (i + first, 0, 0))
    return wide, kv, lse


def run_forward(info, q, kvs, causal):
    tokens, width = q.shape
    count = len(kvs)
    keys = count * tokens
    pairs = width // PAIR
    wide, kv, lse = attention_specs(count, tokens)
    kernel = functools.partial(self_forward_kernel if causal else cross_forward_kernel, count)
    return pl.pallas_call(
        kernel,
        grid=(pairs,),
        out_shape=(as_struct((tokens, width), BF16), as_struct((pairs, tokens, PAIR), BF16)),
        in_specs=[SMEM_SPEC, wide] + [kv] * count,
        out_specs=(wide, lse),
        scratch_shapes=[
            pltpu.VMEM((2, tokens, PAIR), BF16),
            pltpu.VMEM((2, keys, PAIR), BF16),
            pltpu.VMEM((2, keys, PAIR), BF16),
            pltpu.VMEM((2, keys, PAIR), BF16),
        ],
        compiler_params=pltpu.CompilerParams(vmem_limit_bytes=VMEM_LIMIT),
        cost_estimate=cost(8e9, 4e6),
        name="self_forward" if causal else "cross_forward",
    )(info, q, *kvs)


def backward_operands(count, info, limit, q_ref, ctx, lse, grad, kvs, qa, ga, ka, va, kx):
    tokens = q_ref.shape[0]
    rows = tokens // 2

    @pl.when(pl.program_id(0) == 0)
    def _():
        put_key_extras(kx, info, count, rows, limit, True)

    lane = lanes_of(tokens)
    both = grad[...].astype(F32) * ctx[...].astype(F32)
    for head in range(2):
        mine = (lane // HALF) == head
        spare = HALF * (1 - head)
        far = lane_row(1 - head)
        delta = jnp.sum(jnp.where(mine, both, 0.0), axis=-1, keepdims=True)
        put_operands(qa, [q_ref[...]], head, lse[...] * far + one_lanes(head, 0, 1))
        put_operands(ga, [grad[...]], head, lane_pieces(-delta, spare, tokens).astype(BF16))
        put_operands(ka, [kv[0] for kv in kvs], head, kx.at[head])
        put_operands(va, [kv[1] for kv in kvs], head, one_lanes(head, 0, 3))


def in_stages(units, first, second, third):
    one, two = {0: first(units[0])}, {}
    for u in range(len(units) + 1):
        if u + 1 < len(units):
            one[u + 1] = first(units[u + 1])
        if u < len(units):
            two[u] = second(units[u], *one.pop(u))
        if u > 0:
            third(units[u - 1], *two.pop(u - 1))


def both_heads(a, b):
    return jnp.where(lanes_of(a.shape[0]) < HALF, a, b)


def cross_backward_kernel(count, info, q_ref, ctx, lse, grad, *rest):
    kvs, rest = rest[:count], rest[count:]
    dq_out, dkvs, (qa, ga, ka, va, kx) = rest[0], rest[1 : 1 + count], rest[1 + count :]
    tokens = q_ref.shape[0]
    rows = tokens // 2
    backward_operands(count, info, info[5], q_ref, ctx, lse, grad, kvs, qa, ga, ka, va, kx)
    dq, dk, dv = [0.0, 0.0], [None, None], [None, None]

    def products(unit):
        at, head = unit
        return nt(ka[head, at : at + rows], qa[head]), nt(va[head, at : at + rows], ga[head])

    def scores_of(unit, logits, grad_p):
        probs = jnp.exp2(logits * LOG2E)
        return probs.astype(BF16), (probs * grad_p).astype(BF16)

    def grads(unit, probs, scores):
        at, head = unit
        p, cut = at // tokens, slice(at % tokens, at % tokens + rows)
        dv[head] = nn(probs, grad[...])
        dk[head] = nn(scores, q_ref[...])
        dq[head] = dq[head] + tn(kvs[p][0, cut], scores)
        if head == 1:
            dkvs[p][0, cut] = both_heads(*dk).astype(BF16)
            dkvs[p][1, cut] = both_heads(*dv).astype(BF16)

    in_stages([(i * rows, head) for i in range(2 * count) for head in range(2)], products, scores_of, grads)
    top = lax.broadcasted_iota(jnp.int32, (PAIR, tokens), 0) < HALF
    dq_out[...] = jnp.where(top, dq[0], dq[1]).T.astype(BF16)


def self_backward_kernel(count, info, q_ref, ctx, lse, grad, *rest):
    kvs, rest = rest[:count], rest[count:]
    dq_out, dkvs, (qa, ga, ka, va, kx, k_all, parts, total) = rest[0], rest[1 : 1 + count], rest[1 + count :]
    tokens = q_ref.shape[0]
    rows = tokens // 2
    low, high = slice(0, rows), slice(rows, 2 * rows)
    backward_operands(count, info, info[4], q_ref, ctx, lse, grad, kvs, qa, ga, ka, va, kx)
    for p in range(count):
        k_all[p * tokens : (p + 1) * tokens] = kvs[p][0]
    causal = causal_mask(rows, True)
    fixed, free = tile_rows(info, count, rows)
    tiles = [(high, pl.ds(k, rows), False, None) for k in fixed]
    tiles += [(high, high, True, None), (low, low, True, None)]
    tiles += [(pl.ds(q, rows), pl.ds(k, rows), False, q > 0) for q, k in free]
    dq_low, dq_high = [0.0, 0.0], [0.0, 0.0]
    dk, dv = [None, None], [None, None]

    def products(unit):
        t, head = unit
        q_cut, k_cut = tiles[t][:2]
        return nt(ka[head, k_cut], qa[head, q_cut]), nt(va[head, k_cut], ga[head, q_cut])

    def scores_of(unit, logits, grad_p):
        if tiles[unit[0]][2]:
            logits = jnp.where(causal, logits, NEGATIVE)
        probs = jnp.exp2(logits * LOG2E)
        return probs.astype(BF16), (probs * grad_p).astype(BF16)

    def grads(unit, probs, scores):
        t, head = unit
        q_cut, k_cut, _, is_high = tiles[t]
        dv[head] = nn(probs, grad[q_cut])
        dk[head] = nn(scores, q_ref[q_cut])
        part = tn(k_all[k_cut], scores)
        if q_cut is high:
            dq_high[head] = dq_high[head] + part
        elif q_cut is low:
            dq_low[head] = dq_low[head] + part
        else:
            dq_high[head] = dq_high[head] + jnp.where(is_high, part, 0.0)
            dq_low[head] = dq_low[head] + jnp.where(is_high, 0.0, part)
        if head == 1:
            parts[0, t] = both_heads(*dk)
            parts[1, t] = both_heads(*dv)

    in_stages([(t, head) for t in range(len(tiles)) for head in range(2)], products, scores_of, grads)
    top = lax.broadcasted_iota(jnp.int32, (PAIR, rows), 0) < HALF
    dq_out[low] = jnp.where(top, *dq_low).T.astype(BF16)
    dq_out[high] = jnp.where(top, *dq_high).T.astype(BF16)
    total[...] = jnp.zeros_like(total)
    for i in range(2):
        total[i, high] = parts[i, count]
        total[i, low] = parts[i, count + 1]
    base = INFO_HEAD + 2 * count

    @pl.loop(0, 2 * count - 1)
    def _(t):
        is_free = (t >= count).astype(jnp.int32)
        at = pl.multiple_of(info[base + t + is_free * (count - 1)], rows)
        for i in range(2):
            total[i, pl.ds(at, rows)] += parts[i, t + 2 * is_free]

    for p in range(count):
        cut = slice(p * tokens, (p + 1) * tokens)
        for i in range(2):
            dkvs[p][i] = total[i, cut].astype(BF16)


def run_backward(info, q, ctx, lse, grad, kvs, causal, first=0, pairs=None):
    tokens, width = q.shape
    pairs = pairs or width // PAIR
    width = pairs * PAIR
    rows = tokens // 2
    count = len(kvs)
    keys = count * tokens
    wide, kv, lse_spec = attention_specs(count, tokens, first)
    wide_out, kv_out, _ = attention_specs(count, tokens)
    scratch = [pltpu.VMEM((2, tokens, PAIR), BF16)] * 2 + [pltpu.VMEM((2, keys, PAIR), BF16)] * 3
    if causal:
        scratch += [
            pltpu.VMEM((keys, PAIR), BF16),
            pltpu.VMEM((2, 2 * count + 1, rows, PAIR), F32),
            pltpu.VMEM((2, keys, PAIR), F32),
        ]
    return pl.pallas_call(
        functools.partial(self_backward_kernel if causal else cross_backward_kernel, count),
        grid=(pairs,),
        out_shape=(as_struct((tokens, width), BF16),) + (as_struct((2, tokens, width), BF16),) * count,
        in_specs=[SMEM_SPEC, wide, wide, lse_spec, wide] + [kv] * count,
        out_specs=(wide_out,) + (kv_out,) * count,
        scratch_shapes=scratch,
        compiler_params=pltpu.CompilerParams(vmem_limit_bytes=VMEM_LIMIT),
        cost_estimate=cost(2.5e9 * pairs, 6e6),
        name="self_backward" if causal else "cross_backward",
    )(info, q, ctx, lse, grad, *kvs)


def middle_kernel(size, info, first_ref, ctx, og_own, og_other, *rest):
    w2, w3, rest = rest[:size], rest[size : 3 * size], rest[3 * size :]
    vec, fib, keep_out, pass_out, dz2_out, dcross_out = rest[:6]
    slots, (vecs, co, fi, fo, pre, scr, wide) = rest[6 : 6 + size], rest[6 + size :]
    place, half = info[0], info[1]
    tokens, width = first_ref.shape
    rows = tokens // 2
    part = width // size
    hidden_part = fo.shape[0] // size
    chunks = fi.shape[1] // width
    assemble(co, w2, place, part, 4 * part)
    for i, ref in enumerate(w3):
        owner, which = place ^ (i // 2), info[6] ^ (i % 2)
        small, large = part // 2, hidden_part // 2
        start = pl.multiple_of(owner * part + which * small, small)
        for c in range(chunks):
            fi[pl.ds(start, small), c * width : (c + 1) * width] = ref[c * small : (c + 1) * small, :]
        start = pl.multiple_of(owner * hidden_part + which * large, large)
        fo[pl.ds(start, large), :] = ref[chunks * small :, :]

    def vector(i):
        return vec[i : i + 1, :]

    resid2 = first_ref[...].astype(F32) + nn(ctx[...], co[...]) + vector(CBO)
    normed2, inverse2 = norm(resid2)
    second = (normed2 * vector(N2G) + vector(N2B)).astype(BF16)
    branch = jnp.zeros((tokens, width), F32)
    for c in range(chunks):
        cut = slice(c * width, (c + 1) * width)
        value = nn(second, fi[:, cut]) + fib[:, cut]
        pre[:, cut] = value
        hidden = (value * (0.5 * jnp.tanh(0.5 * value) + 0.5)).astype(BF16)
        scr[:, cut] = hidden
        branch = branch + nn(hidden, fo[cut])
    resid3 = second.astype(F32) + branch + vector(FOB)
    normed3, inverse3 = norm(resid3)
    out = (normed3 * vector(N3G) + vector(N3B)).astype(BF16)
    keep_out[...], pass_out[...] = ordered(info, out[:rows], out[rows:])

    live = info[4]
    iota = lax.broadcasted_iota(jnp.int32, (rows, 1), 0)
    low, high = ordered(info, og_own[half], og_other[...])
    grad3 = jnp.concatenate(
        [
            jnp.where(iota + info[2] < live, low.astype(F32), 0.0),
            jnp.where(iota + info[3] < live, high.astype(F32), 0.0),
        ],
        axis=0,
    )
    dz3 = norm_back(grad3, normed3, inverse3, vector(N3G))
    vecs[...] = jnp.zeros_like(vecs)
    vecs[N3G : N3G + 1] = row_sum(grad3 * normed3)
    vecs[N3B : N3B + 1] = row_sum(grad3)
    dy = dz3.astype(BF16)
    vecs[FOB : FOB + 1] = row_sum(dy.astype(F32))
    dsecond = dz3
    for c in range(chunks):
        cut = slice(c * width, (c + 1) * width)
        wide[...] = tn(scr[:, cut], dy)
        for b in range(width // min(hidden_part, width)):
            row = c * width + b * hidden_part
            owner = row // hidden_part
            block = wide[b * hidden_part : (b + 1) * hidden_part].astype(BF16)
            for k, slot in enumerate(slots):

                @pl.when((place ^ owner) == k)
                def _():
                    slot[chunks * part : chunks * part + hidden_part, :] = block

        value = pre[:, cut]
        sig = 0.5 * jnp.tanh(0.5 * value) + 0.5
        dpre = (nt(dy, fo[cut]) * (sig * (1.0 + value * (1.0 - sig)))).astype(BF16)
        vecs[FIB + c : FIB + c + 1] = row_sum(dpre.astype(F32))
        dsecond = dsecond + nt(dpre, fi[:, cut])
        wide[...] = tn(second, dpre)
        scatter_rows(slots, wide, place, part, c * part)
    dz2 = norm_back(dsecond, normed2, inverse2, vector(N2G))
    vecs[N2G : N2G + 1] = row_sum(dsecond * normed2)
    vecs[N2B : N2B + 1] = row_sum(dsecond)
    dz2_out[...] = dz2
    da2 = dz2.astype(BF16)
    vecs[CBO : CBO + 1] = row_sum(da2.astype(F32))
    dcross_out[...] = nt(da2, co[...]).astype(BF16)
    wide[...] = tn(ctx[...], da2)
    scatter_rows(slots, wide, place, part, chunks * part + hidden_part)


def run_middle(info, first, ctx, og_own, og_other, w2, w3, vec, fib):
    tokens, width = first.shape
    size = len(w2)
    part = width // size
    ff = fib.shape[1]
    grad_rows = (ff // width) * part + ff // size + part
    pack = as_struct((grad_rows, width), BF16)
    return pl.pallas_call(
        functools.partial(middle_kernel, size),
        out_shape=(
            as_struct((tokens // 2, width), BF16),
            as_struct((tokens // 2, width), BF16),
            as_struct((tokens, width), F32),
            as_struct((tokens, width), BF16),
            *(pack,) * size,
            as_struct((VEC_ROWS, width), F32),
        ),
        in_specs=[SMEM_SPEC] + [VMEM_SPEC] * (4 + 3 * size + 2),
        out_specs=(VMEM_SPEC,) * (5 + size),
        scratch_shapes=[
            pltpu.VMEM((width, width), BF16),
            pltpu.VMEM((width, ff), BF16),
            pltpu.VMEM((ff, width), BF16),
            pltpu.VMEM((tokens, ff), F32),
            pltpu.VMEM((tokens, ff), BF16),
            pltpu.VMEM((width, width), F32),
        ],
        compiler_params=pltpu.CompilerParams(vmem_limit_bytes=VMEM_LIMIT),
        cost_estimate=cost(12 * tokens * width * ff, 2e7),
        name="middle",
    )(info, first, ctx, og_own, og_other, *w2, *w3, vec, fib)


def after_cross_kernel(size, info, dz2, dq, first_ref, x_ref, ctx, *rest):
    w2, rest = rest[:size], rest[size:]
    vec, dz1_out, dself_out = rest[:3]
    slots, (vecs, weight, wide) = rest[3 : 3 + size], rest[3 + size :]
    place = info[0]
    width = x_ref.shape[1]
    part = width // size
    for i in range(2):
        assemble(weight, w2, place, part, i * part, i)

    def vector(i):
        return vec[i : i + 1, :]

    vecs[...] = jnp.zeros_like(vecs)
    dfirst = dz2[...] + SCALE * nt(dq[...], weight[1])
    resid = x_ref[...].astype(F32) + nn(ctx[...], weight[0]) + vector(SBO)
    normed, inverse = norm(resid)
    dz1 = norm_back(dfirst, normed, inverse, vector(N1G))
    vecs[N1G : N1G + 1] = row_sum(dfirst * normed)
    vecs[N1B : N1B + 1] = row_sum(dfirst)
    vecs[CBQ : CBQ + 1] = row_sum(dq[...].astype(F32)) * SCALE
    dz1_out[...] = dz1
    da1 = dz1.astype(BF16)
    vecs[SBO : SBO + 1] = row_sum(da1.astype(F32))
    dself_out[...] = nt(da1, weight[0]).astype(BF16)
    wide[...] = tn(ctx[...], da1)
    scatter_rows(slots, wide, place, part, 0)
    wide[...] = tn(first_ref[...], dq[...]) * SCALE
    scatter_rows(slots, wide, place, part, part)


def run_after_cross(info, dz2, dq, first, x, ctx, w2, vec):
    tokens, width = x.shape
    size = len(w2)
    pack = as_struct((2 * (width // size), width), BF16)
    return pl.pallas_call(
        functools.partial(after_cross_kernel, size),
        out_shape=(
            as_struct((tokens, width), F32),
            as_struct((tokens, width), BF16),
            *(pack,) * size,
            as_struct((VEC_ROWS, width), F32),
        ),
        in_specs=[SMEM_SPEC] + [VMEM_SPEC] * (6 + size),
        out_specs=(VMEM_SPEC,) * (3 + size),
        scratch_shapes=[pltpu.VMEM((2, width, width), BF16), pltpu.VMEM((width, width), F32)],
        compiler_params=pltpu.CompilerParams(vmem_limit_bytes=VMEM_LIMIT),
        cost_estimate=cost(10 * tokens * width * width, 8e6),
        name="after_cross",
    )(info, dz2, dq, first, x, ctx, *w2, vec)


def encoder_back_kernel(size, info, own, got, x_ref, *rest):
    w2, given, rest = rest[:size], rest[size : 2 * size], rest[2 * size :]
    keep_out, pass_out = rest[:2]
    slots, (vecs, weight, wide) = rest[2 : 2 + size], rest[2 + size :]
    place = info[0]
    width = x_ref.shape[1]
    rows = x_ref.shape[0] // 2
    part = width // size
    for i in range(2):
        assemble(weight, w2, place, part, (2 + i) * part, i)
    vecs[...] = jnp.zeros_like(vecs)
    for slot, ref in zip(slots, given):
        slot[: 2 * part, :] = ref[...]
    total = None
    for i in range(2):
        grad = (own[i].astype(F32) + got[i].astype(F32)).astype(BF16)
        if i == 1:
            vecs[CBV : CBV + 1] = row_sum(grad.astype(F32))
        wide[...] = tn(x_ref[...], grad)
        scatter_rows(slots, wide, place, part, (2 + i) * part)
        term = nt(grad, weight[i])
        total = term if total is None else total + term
    total = total.astype(BF16)
    keep_out[...], pass_out[...] = ordered(info, total[:rows], total[rows:])


def run_encoder_back(info, own, got, x, w2, given):
    tokens, width = x.shape
    size = len(w2)
    pack = as_struct((4 * (width // size), width), BF16)
    return pl.pallas_call(
        functools.partial(encoder_back_kernel, size),
        out_shape=(
            as_struct((tokens // 2, width), BF16),
            as_struct((tokens // 2, width), BF16),
            *(pack,) * size,
            as_struct((VEC_ROWS, width), F32),
        ),
        in_specs=[SMEM_SPEC] + [VMEM_SPEC] * (3 + 2 * size),
        out_specs=(VMEM_SPEC,) * (3 + size),
        scratch_shapes=[pltpu.VMEM((2, width, width), BF16), pltpu.VMEM((width, width), F32)],
        compiler_params=pltpu.CompilerParams(vmem_limit_bytes=VMEM_LIMIT),
        cost_estimate=cost(8 * tokens * width * width, 8e6),
        name="encoder_back",
    )(info, own, got, x, *w2, *given)


def side_by_side(refs):
    return jnp.concatenate([ref[...] for ref in refs], axis=-1)


def target_back_kernel(size, hidden, info, dz1, dq_a, dq_b, own_a, own_b, got_a, got_b, x_ref, *rest):
    w1, others, rest = rest[:size], rest[size : size + 3], rest[size + 3 :]
    keep_out, pass_out = rest[:2]
    slots, (vecs, by_owner, weight, wide) = rest[2 : 2 + size], rest[2 + size :]
    place = info[0]
    width = x_ref.shape[1]
    rows = x_ref.shape[0] // 2
    part = width // size
    for i in range(3):
        assemble(weight, w1, place, part, i * part, i)
    vecs[...] = others[0][...] + others[1][...] + others[2][...]
    dq = side_by_side((dq_a, dq_b))
    vecs[SBQ : SBQ + 1] = row_sum(dq.astype(F32)) * SCALE
    total = dz1[...] + SCALE * nt(dq, weight[0])
    wide[...] = tn(x_ref[...], dq) * SCALE
    scatter_rows(slots, wide, place, part, 0)
    for i in range(2):
        own = side_by_side((own_a.at[i], own_b.at[i])).astype(F32)
        grad = (own + side_by_side((got_a.at[i], got_b.at[i])).astype(F32)).astype(BF16)
        if i == 1:
            vecs[SBV : SBV + 1] = row_sum(grad.astype(F32))
        wide[...] = tn(x_ref[...], grad)
        scatter_rows(slots, wide, place, part, (1 + i) * part)
        total = total + nt(grad, weight[1 + i])
    total = total.astype(BF16)
    keep_out[...], pass_out[...] = ordered(info, total[:rows], total[rows:])
    chunks = hidden // width
    for j in range(size):
        by_owner[j] = jnp.zeros((VEC_ROWS, width), F32)
        by_owner[j, :, :part] = vecs[:, j * part : (j + 1) * part]
        for i in range(chunks):
            at = (j * chunks + i) * part
            row = FIB + at // width
            by_owner[j, FIB + i : FIB + i + 1, :part] = vecs[row : row + 1, at % width : at % width + part]
    for k, slot in enumerate(slots):
        slot[3 * part :, :] = by_owner[place ^ k].astype(BF16)


def run_target_back(hidden, info, dz1, dqs, owns, gots, x, w1, others):
    tokens, width = x.shape
    size = len(w1)
    pack = as_struct((3 * (width // size) + VEC_ROWS, width), BF16)
    return pl.pallas_call(
        functools.partial(target_back_kernel, size, hidden),
        out_shape=(
            as_struct((tokens // 2, width), BF16),
            as_struct((tokens // 2, width), BF16),
            *(pack,) * size,
        ),
        in_specs=[SMEM_SPEC] + [VMEM_SPEC] * (11 + size),
        out_specs=(VMEM_SPEC,) * (2 + size),
        scratch_shapes=[
            pltpu.VMEM((VEC_ROWS, width), F32),
            pltpu.VMEM((size, VEC_ROWS, width), F32),
            pltpu.VMEM((3, width, width), BF16), pltpu.VMEM((width, width), F32),
        ],
        compiler_params=pltpu.CompilerParams(vmem_limit_bytes=VMEM_LIMIT),
        cost_estimate=cost(12 * tokens * width * width, 8e6),
        name="target_back",
    )(info, dz1, *dqs, *owns, *gots, x, *w1, *others)


def add(left, right):
    return (left.astype(F32) + right.astype(F32)).astype(BF16)


class GroupSum:
    def __init__(self, slots):
        self.keep = slots[0::2]
        self.own, *self.far = [send_xor(v, "group", 1) for v in slots[1::2]]

    def start(self):
        parts = [None] + [add(k, f) for k, f in zip(self.keep[1:], self.far)]
        mask, self.arrived = 2, []
        while len(parts) > 1:
            arrived = [send_xor(p, "group", mask) for p in parts[1::2]]
            self.arrived.append(arrived[0])
            parts = [None] + [add(a, b) for a, b in zip(parts[2::2], arrived[1:])]
            mask *= 2

    def addends(self):
        return [self.keep[0], self.own, *self.arrived]

    def finish(self):
        return functools.reduce(lambda a, b: a + b, [v.astype(F32) for v in self.addends()]).astype(BF16)


def piece_shape(rows, width, size):
    return rows // 2, 2 * width // size


def pieces_kernel(count, *refs):
    addends, (out,) = refs[:count], refs[count:]
    size, rows, lanes = out.shape
    total = functools.reduce(lambda a, b: a + b, [v[...].astype(F32) for v in addends]).astype(BF16)
    for j in range(size):
        row, lane = (j % 2) * rows, (j // 2) * lanes
        out[j] = total[row : row + rows, lane : lane + lanes]


def run_pieces(addends, size):
    rows, width = addends[0].shape
    return pl.pallas_call(
        functools.partial(pieces_kernel, len(addends)),
        out_shape=as_struct((size, *piece_shape(rows, width, size)), BF16),
        in_specs=[VMEM_SPEC] * len(addends),
        out_specs=VMEM_SPEC,
        compiler_params=pltpu.CompilerParams(vmem_limit_bytes=VMEM_LIMIT),
        cost_estimate=cost(0, 0),
        name="pieces",
    )(*addends)


def sum_pieces_kernel(parts, out):
    total = parts[0].astype(F32)
    for j in range(1, parts.shape[0]):
        total = total + parts[j].astype(F32)
    for j in range(parts.shape[0]):
        out[j] = total.astype(BF16)


def run_sum_pieces(parts):
    return pl.pallas_call(
        sum_pieces_kernel,
        out_shape=as_struct(parts.shape, BF16),
        in_specs=[VMEM_SPEC],
        out_specs=VMEM_SPEC,
        compiler_params=pltpu.CompilerParams(vmem_limit_bytes=VMEM_LIMIT),
        cost_estimate=cost(0, 0),
        name="sum_pieces",
    )(parts)


def whole_kernel(cuts, parts, *outs):
    size, rows, lanes = parts.shape
    for (start, stop), out in zip(cuts, outs):
        for j in range(size):
            row, lane = (j % 2) * rows, (j // 2) * lanes
            low, high = max(start, row), min(stop, row + rows)
            if low < high:
                block = parts[j, low - row : high - row].astype(F32)
                out[low - start : high - start, lane : lane + lanes] = block


def run_whole(parts, cuts):
    size, _, lanes = parts.shape
    width = lanes * size // 2
    return pl.pallas_call(
        functools.partial(whole_kernel, cuts),
        out_shape=tuple(as_struct((stop - start, width), F32) for start, stop in cuts),
        in_specs=[VMEM_SPEC],
        out_specs=(VMEM_SPEC,) * len(cuts),
        compiler_params=pltpu.CompilerParams(vmem_limit_bytes=VMEM_LIMIT),
        cost_estimate=cost(0, 0),
        name="whole",
    )(parts)


def exchange(parts):
    return lax.all_to_all(parts, "replica", 0, 0)


def halves(value, dim):
    cut = value.shape[dim] // 2
    return lax.slice_in_dim(value, 0, cut, axis=dim), lax.slice_in_dim(value, cut, 2 * cut, axis=dim)


class ReplicaSum:
    def __init__(self, value):
        self.value = value
        self.size = lax.axis_size("replica")
        self.place = lax.axis_index("replica")
        masks = [1 << i for i in range(self.size.bit_length() - 1)]
        self.steps = [(m, True) for m in masks] + [(m, False) for m in reversed(masks)]
        self.dims = {}

    def start(self):
        mask, down = self.steps[0]
        up = (self.place & mask) != 0
        if down:
            dim = 0 if mask == 1 else 1
            if self.value.shape[dim] % 2:
                dim = 1 - dim
            self.dims[mask] = dim
            low, high = halves(self.value, dim)
            self.value = jnp.where(up, high, low)
            self.arrived = send_xor(jnp.where(up, low, high), "replica", mask)
        else:
            self.arrived = send_xor(self.value, "replica", mask)

    def finish(self):
        mask, down = self.steps.pop(0)
        if down:
            self.value = add(self.value, self.arrived)
        else:
            up = (self.place & mask) != 0
            dim = self.dims[mask]
            self.value = jnp.where(
                up,
                jnp.concatenate([self.arrived, self.value], axis=dim),
                jnp.concatenate([self.value, self.arrived], axis=dim),
            )


def butterfly(stacked, place, size):
    bit = 1
    while bit < size:
        order = np.arange(size) ^ bit
        flipped = jnp.stack([stacked[int(i)] for i in order])
        stacked = jnp.where((place & bit) != 0, flipped, stacked)
        bit *= 2
    return stacked


def body(
    target, encoder, target_len, encoder_len,
    self_wq, self_wk, self_wv, self_wo, self_bq, self_bv, self_bo, norm1_gain, norm1_bias,
    cross_wq, cross_wk, cross_wv, cross_wo, cross_bq, cross_bv, cross_bo, norm2_gain, norm2_bias,
    ffn_in, ffn_in_bias, ffn_out, ffn_out_bias, norm3_gain, norm3_bias, out_grad,
):
    size = lax.axis_size("group")
    place = lax.axis_index("group")
    _, rows, width = target.shape
    part = width // size
    ff = ffn_in.shape[1]
    chunks = ff // width
    half = (place >= size // 2).astype(jnp.int32)
    table = jnp.asarray(group_table(size, rows))
    side = lax.axis_index("replica") & 1
    lengths = jnp.append(jnp.stack([target_len, encoder_len])[:, half], side)
    info = lax.dynamic_update_slice(table[place], lengths, (4,))
    mirror = [(i, size - 1 - i) for i in range(size)]

    def swap(value):
        return lax.ppermute(value, "group", mirror)

    w1_own, target_half = run_first_pack(info, target, (self_wq, self_wk, self_wv))
    w1 = gather_even(w1_own, "group", size)
    target_got = swap(target_half)
    matrices = (encoder, out_grad, ffn_in, ffn_out, self_wo, cross_wq, cross_wk, cross_wv, cross_wo)
    vectors = (
        self_bq, self_bv, self_bo, norm1_gain, norm1_bias, cross_bq, cross_bv, cross_bo,
        norm2_gain, norm2_bias, ffn_out_bias, norm3_gain, norm3_bias, ffn_in_bias,
    )
    w1_odd, *late = point(send_xor(w1_own, "group", 1), *matrices, *vectors)
    matrices, vectors = late[: len(matrices)], late[len(matrices) :]
    w2_own, *w3_own, encoder_half, og_half = run_second_pack(info, *matrices[:4], matrices[4:])
    vec_own = jnp.concatenate([v.reshape(-1, part) for v in vectors])
    vec_own = jnp.pad(vec_own, ((0, VEC_ROWS - vec_own.shape[0]), (0, 0)))
    vec_odd = send_xor(vec_own, "group", 1)
    vec_pairs = gather_even(jnp.concatenate([vec_own, vec_odd]), "group", size)
    vec_all = jnp.stack(vec_pairs).reshape(size, VEC_ROWS, part)
    vec_all = butterfly(vec_all, place, size)
    vec = jnp.transpose(vec_all, (1, 0, 2)).reshape(VEC_ROWS, width).astype(F32)
    fib = vec_all[:, FIB : FIB + chunks].reshape(1, ff).astype(F32)
    target_got, encoder_half, *w1 = point(target_got, encoder_half, *w1)
    encoder_got = swap(encoder_half)
    w1 = [v for e, o in zip(w1, [w1_odd] + [send_xor(e, "group", 1) for e in w1[1:]]) for v in (e, o)]

    x, q1, kv1 = run_qkv(info, target, target_got, w1, vec)
    kv1, w2_own, encoder_got = point(kv1, w2_own, encoder_got)
    w2 = gather_even(w2_own, "group", size)
    kvs1 = gather_xor(kv1, "group", size // 2)
    ctx1, lse1 = run_forward(info, q1, kvs1, True)
    ctx1, w3_near, w3_far, *w2 = point(ctx1, *w3_own, *w2)
    w2 = with_odd(w2, "group")
    w3_even = gather_even(w3_near, "group", size)[1:]
    w3_odd = [send_xor(w, "group", 1) for w in (w3_near, w3_far)]
    xe, kv2 = run_cross_kv(info, encoder, encoder_got, w2, vec)
    kv2, ctx1 = point(kv2, ctx1)
    kvs2 = gather_xor(kv2, "group", size // 2)
    first, q2 = run_after_self(info, x, ctx1, w2, vec)
    q2, og_half, *w3_even = point(q2, og_half, *w3_even)
    w3_other = [send_xor(w, "replica", 1) for w in w3_even]
    og_got = swap(og_half)
    w3_pass = [send_xor(w, "group", 1) for w in w3_even]
    ctx2, lse2 = run_forward(info, q2, kvs2, False)
    ctx2, og_got, *w3_other = point(ctx2, og_got, *w3_other)
    w3 = [*w3_own, *w3_odd]
    for near, far, passed in zip(w3_even, w3_other, w3_pass):
        w3 += [near, far, passed, send_xor(far, "group", 1)]
    out_keep, out_pass, dz2, dcross, *slots_a, vecs_a = run_middle(
        info, first, ctx2, out_grad, og_got, w2, w3, vec, fib
    )

    def key_value_sums(parts):
        bit = len(parts) // 2
        while bit > 1:
            arrived = [send_xor(parts[k | bit], "group", bit) for k in range(bit)]
            parts = [add(parts[k], arrived[k]) for k in range(bit)]
            bit //= 2
        return parts[0], send_xor(parts[1], "group", 1)

    group_a = GroupSum(slots_a)
    dcross, *group_a.far = point(dcross, *group_a.far)
    group_a.start()
    dq2, *dkvs2 = run_backward(info, q2, ctx2, lse2, dcross, kvs2, False)
    dq2, out_pass, *dkvs2 = point(dq2, out_pass, *dkvs2)
    own2, got2 = key_value_sums(dkvs2)
    dz1, dself, *slots_b, vecs_b = run_after_cross(info, dz2, dq2, first, x, ctx1, w2, vec)
    dself, got2, out_pass, group_a.own, *group_a.arrived = point(
        dself, got2, out_pass, group_a.own, *group_a.arrived
    )
    sum_a = ReplicaSum(group_a.finish())
    sum_a.start()
    out_got = swap(out_pass)
    enc_keep, enc_pass, *slots_b, vecs_e = run_encoder_back(info, own2, got2, xe, w2, slots_b)
    group_b = GroupSum(slots_b)
    dself, enc_pass, sum_a.arrived, *group_b.far = point(dself, enc_pass, sum_a.arrived, *group_b.far)
    group_b.start()
    sum_a.finish()
    sum_a.start()
    enc_got = swap(enc_pass)
    pairs = width // PAIR // 2
    dq1_a, *dkvs1_a = run_backward(info, q1, ctx1, lse1, dself, kvs1, True, 0, pairs)
    dself, sum_a.arrived, *dkvs1_a = point(dself, sum_a.arrived, *dkvs1_a)
    own1_a, got1_a = key_value_sums(dkvs1_a)
    sum_a.finish()
    sum_a.start()
    dq1_b, *dkvs1_b = run_backward(info, q1, ctx1, lse1, dself, kvs1, True, pairs, pairs)
    hops = len(group_b.arrived)
    group_b.own, dq1_b, sum_a.arrived, *moved = point(
        group_b.own, dq1_b, sum_a.arrived, *group_b.arrived, *dkvs1_b
    )
    group_b.arrived, dkvs1_b = moved[:hops], moved[hops:]
    own1_b, got1_b = key_value_sums(dkvs1_b)
    sum_b = ReplicaSum(group_b.finish())
    sum_b.start()
    sum_a.finish()
    sum_a.start()
    tgt_keep, tgt_pass, *slots_c = run_target_back(
        ff, info, dz1, (dq1_a, dq1_b), (own1_a, own1_b), (got1_a, got1_b), x, w1, (vecs_a, vecs_b, vecs_e)
    )

    tgt_pass, sum_a.arrived, sum_b.arrived, *slots_c = point(tgt_pass, sum_a.arrived, sum_b.arrived, *slots_c)

    def advance(*sums):
        for s in sums:
            if s.steps:
                s.finish()
            if s.steps:
                s.start()

    def behind(*values):
        *values, sum_a.value, sum_b.value = point(*values, sum_a.value, sum_b.value)
        return values

    group_c = GroupSum(slots_c)
    group_c.far = behind(*group_c.far)
    group_c.start()
    advance(sum_a, sum_b)
    sum_a.arrived, sum_b.arrived = point(sum_a.arrived, sum_b.arrived)
    advance(sum_a, sum_b)
    group_c.own, *group_c.arrived = behind(group_c.own, *group_c.arrived)
    pieces_c = run_pieces(group_c.addends(), lax.axis_size("replica"))
    parts_c = exchange(pieces_c)
    tgt_got = swap(tgt_pass)
    sum_a.arrived, sum_b.arrived = point(sum_a.arrived, sum_b.arrived)
    advance(sum_a, sum_b)
    parts_c, tgt_got = behind(parts_c, tgt_got)
    parts_c = exchange(run_sum_pieces(parts_c))
    sum_a.arrived, sum_b.arrived = point(sum_a.arrived, sum_b.arrived)
    while sum_a.steps or sum_b.steps:
        advance(sum_a, sum_b)
    parts_c, *_ = behind(parts_c)
    cuts = tuple((i * part, (i + 1) * part) for i in range(3)) + ((3 * part, 3 * part + VEC_ROWS),)
    g_sq, g_sk, g_sv, g_vec = run_whole(parts_c, cuts)

    def unswap(kept, arrived):
        return jnp.where(half == 0, jnp.stack([kept, arrived]), jnp.stack([arrived, kept]))

    a = sum_a.value.astype(F32)
    b = sum_b.value.astype(F32)
    g_fi = jnp.transpose(a[: chunks * part].reshape(chunks, part, width), (1, 0, 2)).reshape(part, ff)
    g_fo = a[chunks * part : chunks * part + ffn_out.shape[0]]
    g_co = a[chunks * part + ffn_out.shape[0] :]
    g_so, g_cq, g_ck, g_cv = (b[i * part : (i + 1) * part] for i in range(4))
    g_vec = g_vec[:, :part]
    return (
        unswap(out_keep, out_got),
        unswap(tgt_keep, tgt_got),
        unswap(enc_keep, enc_got),
        g_sq, g_sk, g_sv, g_so, g_vec[SBQ], g_vec[SBV], g_vec[SBO], g_vec[N1G], g_vec[N1B],
        g_cq, g_ck, g_cv, g_co, g_vec[CBQ], g_vec[CBV], g_vec[CBO], g_vec[N2G], g_vec[N2B],
        g_fi, g_vec[FIB : FIB + chunks].reshape(-1), g_fo, g_vec[FOB], g_vec[N3G], g_vec[N3B],
    )


def solution(mesh):
    seq, lens, mat, vec = P("replica", "group", None), P("replica"), P("group", None), P("group")
    layer = (mat,) * 4 + (vec,) * 5 + (mat,) * 4 + (vec,) * 5 + (mat, vec, mat, vec, vec, vec)
    in_specs = (seq, seq, lens, lens) + layer + (seq,)
    out_specs = (seq,) * 3 + layer
    return jax.shard_map(body, mesh=mesh, in_specs=in_specs, out_specs=out_specs, check_vma=False)
```

```python
import functools

import jax
import jax.numpy as jnp
import numpy as np
from jax import lax
from jax.experimental import pallas as pl
from jax.experimental.pallas import tpu as pltpu
from jax.sharding import PartitionSpec as P

F32 = jnp.float32
BF16 = jnp.bfloat16
HEADS = 8
PAIR = 128
HALF = 64
SCALE = 0.125
NEGATIVE = -1e30
EPSILON = 1e-5
LOG2E = 1.4426950408889634
DENSE_LIMIT = 20 << 20
FULL_LIMIT = 56 << 20
MIDDLE_LIMIT = 40 << 20

(SBQ, SBV, SBO, N1G, N1B, CBQ, CBV, CBO, N2G, N2B, FOB, N3G, N3B, FIB) = range(14)
VEC_ROWS = 32
INFO_HEAD = 7

VMEM_SPEC = pl.BlockSpec(memory_space=pltpu.VMEM)
LOHI = True
ROW_SPLIT = 1
SMEM_SPEC = pl.BlockSpec(memory_space=pltpu.SMEM)


def nn(left, right):
    return lax.dot_general(left, right, (((1,), (0,)), ((), ())), preferred_element_type=F32)


def nt(left, right):
    return lax.dot_general(left, right, (((1,), (1,)), ((), ())), preferred_element_type=F32)


def tn(left, right):
    return lax.dot_general(left, right, (((0,), (0,)), ((), ())), preferred_element_type=F32)


def as_struct(shape, dtype):
    return jax.ShapeDtypeStruct(shape, dtype)


def cost(flops, nbytes):
    return pl.CostEstimate(flops=1000, bytes_accessed=1000, transcendentals=0)


def send_xor(value, axis, mask):
    size = lax.axis_size(axis)
    return lax.ppermute(value, axis, [(i, i ^ mask) for i in range(size)])


def gather_xor(value, axis, size):
    found = {0: value}
    bit = size // 2
    while bit:
        found.update({k | bit: send_xor(v, axis, bit) for k, v in list(found.items())})
        bit //= 2
    return [found[k] for k in range(size)]


def gather_even(value, axis, size):
    found = {0: value}
    bit = size // 2
    while bit > 1:
        found.update({k | bit: send_xor(v, axis, bit) for k, v in list(found.items())})
        bit //= 2
    return [found[k] for k in range(0, size, 2)]


def with_odd(evens, axis):
    odds = [send_xor(e, axis, 1) for e in evens]
    return [v for pair in zip(evens, odds) for v in pair]


def point(*values):
    return lax.optimization_barrier(values)


def group_table(size, rows):
    half = size // 2
    table = []
    for g in range(size):
        upper = g >= half
        low = min(g, size - 1 - g)
        row = [g, int(upper), low * rows, (size - 1 - low) * rows, 0, 0, 0]
        for k in range(half):
            d = min(g ^ k, size - 1 - (g ^ k))
            row += [d * rows, (size - 1 - d) * rows]

        def place(b):
            d = b if (b >= half) == upper else size - 1 - b
            return ((g ^ d) * 2 + int(b >= half)) * rows

        free = [(1, b) for b in range(half, size - 1 - low)] + [(0, b) for b in range(low)]
        row += [place(b) for b in range(half)]
        row += [s * rows for s, _ in free] + [place(b) for _, b in free]
        table.append(row)
    return np.asarray(table, np.int32)


def assemble(dest, refs, place, rows, source, index=None):
    for k, ref in enumerate(refs):
        start = pl.multiple_of((place ^ k) * rows, rows)
        block = ref[source : source + rows, :]
        if index is None:
            dest[pl.ds(start, rows), :] = block
        else:
            dest[index, pl.ds(start, rows), :] = block


def scatter_rows(slots, grad, place, rows, offset):
    for k, slot in enumerate(slots):
        start = pl.multiple_of((place ^ k) * rows, rows)
        slot[offset : offset + rows, :] = grad[pl.ds(start, rows), :].astype(BF16)


def norm(resid):
    centred = resid - jnp.mean(resid, axis=-1, keepdims=True)
    inverse = lax.rsqrt(jnp.mean(centred * centred, axis=-1, keepdims=True) + EPSILON)
    return centred * inverse, inverse


def norm_back(grad, normed, inverse, gain):
    scaled = grad * gain
    return inverse * (
        scaled
        - jnp.mean(scaled, axis=-1, keepdims=True)
        - normed * jnp.mean(scaled * normed, axis=-1, keepdims=True)
    )


def ordered(info, own, other):
    upper = info[1] == 1
    return jnp.where(upper, other, own), jnp.where(upper, own, other)


def row_sum(value):
    return jnp.sum(value, axis=0, keepdims=True)


def qkv_kernel(size, info, own, other, *rest):
    ws, (vec, x_out, q_out, kv_out, weight) = rest[:size], rest[size:]
    place, half = info[0], info[1]
    rows, width = other.shape
    part = width // size
    for i in range(3):
        assemble(weight, ws, place, part, i * part, i)
    x = jnp.concatenate(ordered(info, own[half], other[...]), axis=0)
    x_out[...] = x
    q_out[...] = ((nn(x, weight[0]) + vec[SBQ : SBQ + 1, :]) * SCALE).astype(BF16)
    kv_out[0] = nn(x, weight[1]).astype(BF16)
    kv_out[1] = (nn(x, weight[2]) + vec[SBV : SBV + 1, :]).astype(BF16)


def run_qkv(info, own, other, ws, vec):
    rows, width = other.shape
    tokens = 2 * rows
    return pl.pallas_call(
        functools.partial(qkv_kernel, len(ws)),
        out_shape=(
            as_struct((tokens, width), BF16),
            as_struct((tokens, width), BF16),
            as_struct((2, tokens, width), BF16),
        ),
        in_specs=[SMEM_SPEC] + [VMEM_SPEC] * (3 + len(ws)),
        out_specs=(VMEM_SPEC,) * 3,
        scratch_shapes=[pltpu.VMEM((3, width, width), BF16)],
        compiler_params=pltpu.CompilerParams(vmem_limit_bytes=DENSE_LIMIT),
        cost_estimate=cost(6 * tokens * width * width, 4e6),
        name="qkv",
    )(info, own, other, *ws, vec)


def first_pack_kernel(info, target, wq, wk, wv, w_out, other_out):
    part = wq.shape[0]
    for i, w in enumerate((wq, wk, wv)):
        w_out[i * part : (i + 1) * part] = w[...]
    other_out[...] = target[1 - info[1]]


def run_first_pack(info, target, ws):
    _, rows, width = target.shape
    return pl.pallas_call(
        first_pack_kernel,
        out_shape=(as_struct((3 * ws[0].shape[0], width), BF16), as_struct((rows, width), BF16)),
        in_specs=[SMEM_SPEC] + [VMEM_SPEC] * 4,
        out_specs=(VMEM_SPEC,) * 2,
        compiler_params=pltpu.CompilerParams(vmem_limit_bytes=FULL_LIMIT),
        cost_estimate=cost(0, 0),
        name="first_pack",
    )(info, target, *ws)


def second_pack_kernel(info, encoder, og, w_in, w_out, *refs):
    ws, (w2_out, near_out, far_out, enc_out, og_out) = refs[:5], refs[5:]
    part, width = ws[0].shape
    for i, w in enumerate(ws):
        w2_out[i * part : (i + 1) * part] = w[...]
    enc_out[...] = encoder[1 - info[1]]
    og_out[...] = og[1 - info[1]]
    small, large = part // 2, w_out.shape[0] // 2
    chunks = w_in.shape[1] // width
    for which, out in enumerate((near_out, far_out)):
        at = pl.multiple_of((info[6] ^ which) * small, small)
        for c in range(chunks):
            out[c * small : (c + 1) * small] = w_in[pl.ds(at, small), c * width : (c + 1) * width]
        at = pl.multiple_of((info[6] ^ which) * large, large)
        out[chunks * small :] = w_out[pl.ds(at, large)]


def run_second_pack(info, encoder, og, w_in, w_out, ws):
    _, rows, width = encoder.shape
    block = as_struct((rows, width), BF16)
    half = as_struct((w_in.shape[0] // 2 * (w_in.shape[1] // width) + w_out.shape[0] // 2, width), BF16)
    return pl.pallas_call(
        second_pack_kernel,
        out_shape=(as_struct((5 * ws[0].shape[0], width), BF16), half, half, block, block),
        in_specs=[SMEM_SPEC] + [VMEM_SPEC] * 9,
        out_specs=(VMEM_SPEC,) * 5,
        compiler_params=pltpu.CompilerParams(vmem_limit_bytes=FULL_LIMIT),
        cost_estimate=cost(0, 0),
        name="second_pack",
    )(info, encoder, og, w_in, w_out, *ws)


def cross_kv_kernel(size, info, own, other, *rest):
    ws, (vec, x_out, kv_out, weight) = rest[:size], rest[size:]
    place, half = info[0], info[1]
    rows, width = other.shape
    part = width // size
    for i in range(2):
        assemble(weight, ws, place, part, (2 + i) * part, i)
    x = jnp.concatenate(ordered(info, own[half], other[...]), axis=0)
    x_out[...] = x
    kv_out[0] = nn(x, weight[0]).astype(BF16)
    kv_out[1] = (nn(x, weight[1]) + vec[CBV : CBV + 1, :]).astype(BF16)


def run_cross_kv(info, own, other, ws, vec):
    rows, width = other.shape
    tokens = 2 * rows
    return pl.pallas_call(
        functools.partial(cross_kv_kernel, len(ws)),
        out_shape=(as_struct((tokens, width), BF16), as_struct((2, tokens, width), BF16)),
        in_specs=[SMEM_SPEC] + [VMEM_SPEC] * (3 + len(ws)),
        out_specs=(VMEM_SPEC,) * 2,
        scratch_shapes=[pltpu.VMEM((2, width, width), BF16)],
        compiler_params=pltpu.CompilerParams(vmem_limit_bytes=DENSE_LIMIT),
        cost_estimate=cost(4 * tokens * width * width, 4e6),
        name="cross_kv",
    )(info, own, other, *ws, vec)


def after_self_kernel(size, info, x_ref, ctx, *rest):
    ws, (vec, first_out, q_out, weight) = rest[:size], rest[size:]
    place = info[0]
    width = x_ref.shape[1]
    part = width // size
    for i in range(2):
        assemble(weight, ws, place, part, i * part, i)
    resid = x_ref[...].astype(F32) + nn(ctx[...], weight[0]) + vec[SBO : SBO + 1, :]
    normed, _ = norm(resid)
    first = (normed * vec[N1G : N1G + 1, :] + vec[N1B : N1B + 1, :]).astype(BF16)
    first_out[...] = first
    q_out[...] = ((nn(first, weight[1]) + vec[CBQ : CBQ + 1, :]) * SCALE).astype(BF16)


def run_after_self(info, x, ctx, ws, vec):
    tokens, width = x.shape
    return pl.pallas_call(
        functools.partial(after_self_kernel, len(ws)),
        out_shape=(as_struct((tokens, width), BF16),) * 2,
        in_specs=[SMEM_SPEC] + [VMEM_SPEC] * (3 + len(ws)),
        out_specs=(VMEM_SPEC,) * 2,
        scratch_shapes=[pltpu.VMEM((2, width, width), BF16)],
        compiler_params=pltpu.CompilerParams(vmem_limit_bytes=DENSE_LIMIT),
        cost_estimate=cost(4 * tokens * width * width, 4e6),
        name="after_self",
    )(info, x, ctx, *ws, vec)


def lanes_of(rows):
    return lax.broadcasted_iota(jnp.int32, (rows, PAIR), 1)


def lane_row(head):
    return ((lax.broadcasted_iota(jnp.int32, (1, PAIR), 1) // HALF) == head).astype(F32).astype(BF16)


def split3(value):
    a = value.astype(BF16)
    rest = value - a.astype(F32)
    b = rest.astype(BF16)
    c = (rest - b.astype(F32)).astype(BF16)
    return a, b, c


def lane_pieces(value, base, rows):
    lane = lanes_of(rows)
    a, b, c = (p.astype(F32) for p in split3(value))
    return jnp.where(lane == base, a, jnp.where(lane == base + 1, b, jnp.where(lane == base + 2, c, 0.0)))


def put_key_extras(kx, info, count, rows, limit, ones):
    for p in range(count):
        for slot in range(2):
            at = (2 * p + slot) * rows
            pos = info[INFO_HEAD + 2 * p + slot] + lax.broadcasted_iota(jnp.int32, (rows, PAIR), 0)
            lane = lanes_of(rows)
            for head in range(2):
                spare = HALF * (1 - head)
                extra = jnp.where((lane == spare) & (pos >= limit), NEGATIVE, 0.0)
                if ones:
                    extra = jnp.where((lane > spare) & (lane < spare + 4), 1.0, extra)
                kx[head, at : at + rows] = extra.astype(BF16)


def put_operands(dest, parts, head, extra):
    mine = lane_row(head)
    at = 0
    for part in parts:
        rows = part.shape[0]
        add_on = extra[at : at + rows] if extra.shape[0] > 1 else extra
        dest[head, at : at + rows] = part * mine + add_on
        at += rows


def one_lanes(head, first, last):
    lane = lax.broadcasted_iota(jnp.int32, (1, PAIR), 1) - HALF * (1 - head)
    return jnp.where((lane >= first) & (lane < last), 1.0, 0.0).astype(BF16)


def finish_rows(acc, top, head):
    rows = acc.shape[0]
    spare = HALF * (1 - head)
    total = acc[:, spare : spare + 1]
    return acc / total, lane_pieces(-(top + jnp.log(total)), spare + 1, rows)


def forward_operands(count, info, limit, q_ref, kvs, qa, ka, va, kx):
    rows = q_ref.shape[0] // 2

    @pl.when(pl.program_id(0) == 0)
    def _():
        put_key_extras(kx, info, count, rows, limit, False)

    for head in range(2):
        put_operands(qa, [q_ref[...]], head, one_lanes(head, 0, 1))
        put_operands(ka, [kv[0] for kv in kvs], head, kx.at[head])
        put_operands(va, [kv[1] for kv in kvs], head, one_lanes(head, 0, 1))


def weights_of(logits, top):
    return jnp.exp2((logits - top) * LOG2E).astype(BF16)


def store_heads(ctx_out, lse_out, cut, done):
    (context_a, pieces_a), (context_b, pieces_b) = done
    lane = lanes_of(context_a.shape[0])
    ctx_out[cut] = jnp.where(lane < HALF, context_a, context_b).astype(BF16)
    lse_out[cut] = (pieces_a + pieces_b).astype(BF16)


def cross_forward_kernel(count, info, q_ref, *rest):
    kvs, (ctx_out, lse_out, qa, ka, va, kx) = rest[:count], rest[count:]
    rows = q_ref.shape[0] // 2
    forward_operands(count, info, info[5], q_ref, kvs, qa, ka, va, kx)
    step = rows // ROW_SPLIT
    units = [(c, head) for c in range(2 * ROW_SPLIT) for head in range(2)]

    def logits_of(unit):
        c, head = unit
        return nt(qa[head, c * step : (c + 1) * step], ka[head])

    logits, weights, done = {0: logits_of(units[0])}, {}, {}
    for u in range(len(units) + 1):
        if u + 1 < len(units):
            logits[u + 1] = logits_of(units[u + 1])
        if u < len(units):
            now = logits.pop(u)
            top = jnp.max(now, axis=-1, keepdims=True)
            weights[u] = (weights_of(now, top), top)
        if u > 0:
            c, head = units[u - 1]
            probs, top = weights.pop(u - 1)
            done[head] = finish_rows(nn(probs, va[head]), top, head)
            if head == 1:
                store_heads(ctx_out, lse_out, slice(c * step, (c + 1) * step), (done[0], done[1]))


def causal_mask(rows, transposed):
    a = lax.broadcasted_iota(jnp.int32, (rows, rows), 0)
    b = lax.broadcasted_iota(jnp.int32, (rows, rows), 1)
    return a <= b if transposed else b <= a


def tile_rows(info, count, rows):
    base = INFO_HEAD + 2 * count

    def at(i):
        return pl.multiple_of(info[base + i], rows)

    fixed = [at(i) for i in range(count)]
    free = [(at(count + i), at(2 * count - 1 + i)) for i in range(count - 1)]
    return fixed, free


def self_forward_kernel(count, info, q_ref, *rest):
    kvs, (ctx_out, lse_out, qa, ka, va, kx) = rest[:count], rest[count:]
    rows = q_ref.shape[0] // 2
    low, high = slice(0, rows), slice(rows, 2 * rows)
    forward_operands(count, info, info[4], q_ref, kvs, qa, ka, va, kx)
    causal = causal_mask(rows, False)
    fixed, free = tile_rows(info, count, rows)
    key_cuts = [pl.ds(k, rows) for k in fixed] + [high]
    to_high = [q > 0 for q, _ in free]

    def widest(tile):
        return jnp.max(tile, axis=-1, keepdims=True)

    def products(head):
        def logits_of(q_cut, k_cut):
            return nt(qa[head, q_cut], ka[head, k_cut])

        tiles = [logits_of(high, k) for k in key_cuts]
        tile_low = logits_of(low, low)
        extra = [logits_of(pl.ds(q, rows), pl.ds(k, rows)) for q, k in free]
        return tiles, tile_low, extra

    def weigh(tiles, tile_low, extra):
        tiles[-1] = jnp.where(causal, tiles[-1], NEGATIVE)
        tile_low = jnp.where(causal, tile_low, NEGATIVE)
        top_high = widest(functools.reduce(jnp.maximum, tiles))
        top_low = widest(tile_low)
        for tile, is_high in zip(extra, to_high):
            top = widest(tile)
            top_high = jnp.where(is_high, jnp.maximum(top_high, top), top_high)
            top_low = jnp.where(is_high, top_low, jnp.maximum(top_low, top))
        free_weights = [
            weights_of(tile, jnp.where(is_high, top_high, top_low)) for tile, is_high in zip(extra, to_high)
        ]
        return [weights_of(t, top_high) for t in tiles], weights_of(tile_low, top_low), free_weights, top_high, top_low

    def contexts(head, tiles, tile_low, extra, top_high, top_low):
        acc_high = sum(nn(t, va[head, k]) for t, k in zip(tiles, key_cuts))
        acc_low = nn(tile_low, va[head, low])
        for tile, is_high, (_, k) in zip(extra, to_high, free):
            part = nn(tile, va[head, pl.ds(k, rows)])
            acc_high = acc_high + jnp.where(is_high, part, 0.0)
            acc_low = acc_low + jnp.where(is_high, 0.0, part)
        return finish_rows(acc_low, top_low, head), finish_rows(acc_high, top_high, head)

    first, second = products(0), products(1)
    first = weigh(*first)
    first = contexts(0, *first)
    second = contexts(1, *weigh(*second))
    store_heads(ctx_out, lse_out, low, (first[0], second[0]))
    store_heads(ctx_out, lse_out, high, (first[1], second[1]))


def attention_limit(keys):
    return (10 << 20) + keys * (12 << 10)


def attention_specs(count, tokens, first=0):
    wide = pl.BlockSpec((tokens, PAIR), lambda i: (0, i + first))
    kv = pl.BlockSpec((2, tokens, PAIR), lambda i: (0, 0, i + first))
    lse = pl.BlockSpec((None, tokens, PAIR), lambda i: (i + first, 0, 0))
    return wide, kv, lse


def run_forward(info, q, kvs, causal):
    tokens, width = q.shape
    count = len(kvs)
    keys = count * tokens
    pairs = width // PAIR
    wide, kv, lse = attention_specs(count, tokens)
    kernel = functools.partial(self_forward_kernel if causal else cross_forward_kernel, count)
    return pl.pallas_call(
        kernel,
        grid=(pairs,),
        out_shape=(as_struct((tokens, width), BF16), as_struct((pairs, tokens, PAIR), BF16)),
        in_specs=[SMEM_SPEC, wide] + [kv] * count,
        out_specs=(wide, lse),
        scratch_shapes=[
            pltpu.VMEM((2, tokens, PAIR), BF16),
            pltpu.VMEM((2, keys, PAIR), BF16),
            pltpu.VMEM((2, keys, PAIR), BF16),
            pltpu.VMEM((2, keys, PAIR), BF16),
        ],
        compiler_params=pltpu.CompilerParams(vmem_limit_bytes=attention_limit(keys)),
        cost_estimate=cost(8e9, 4e6),
        name="self_forward" if causal else "cross_forward",
    )(info, q, *kvs)


def backward_operands(count, info, limit, q_ref, ctx, lse, grad, kvs, qa, ga, ka, va, kx):
    tokens = q_ref.shape[0]
    rows = tokens // 2

    @pl.when(pl.program_id(0) == 0)
    def _():
        put_key_extras(kx, info, count, rows, limit, True)

    lane = lanes_of(tokens)
    both = grad[...].astype(F32) * ctx[...].astype(F32)
    for head in range(2):
        mine = (lane // HALF) == head
        spare = HALF * (1 - head)
        far = lane_row(1 - head)
        delta = jnp.sum(jnp.where(mine, both, 0.0), axis=-1, keepdims=True)
        put_operands(qa, [q_ref[...]], head, lse[...] * far + one_lanes(head, 0, 1))
        put_operands(ga, [grad[...]], head, lane_pieces(-delta, spare, tokens).astype(BF16))
        put_operands(ka, [kv[0] for kv in kvs], head, kx.at[head])
        put_operands(va, [kv[1] for kv in kvs], head, one_lanes(head, 0, 3))


def in_stages(units, first, second, third):
    one, two = {0: first(units[0])}, {}
    for u in range(len(units) + 1):
        if u + 1 < len(units):
            one[u + 1] = first(units[u + 1])
        if u < len(units):
            two[u] = second(units[u], *one.pop(u))
        if u > 0:
            third(units[u - 1], *two.pop(u - 1))


def both_heads(a, b):
    return jnp.where(lanes_of(a.shape[0]) < HALF, a, b)


def cross_backward_kernel(count, info, q_ref, ctx, lse, grad, *rest):
    kvs, rest = rest[:count], rest[count:]
    dq_out, dkvs, (qa, ga, ka, va, kx) = rest[0], rest[1 : 1 + count], rest[1 + count :]
    tokens = q_ref.shape[0]
    rows = tokens // 2
    backward_operands(count, info, info[5], q_ref, ctx, lse, grad, kvs, qa, ga, ka, va, kx)
    dq, dk, dv = [0.0, 0.0], [None, None], [None, None]

    def products(unit):
        at, head = unit
        return nt(ka[head, at : at + rows], qa[head]), nt(va[head, at : at + rows], ga[head])

    def scores_of(unit, logits, grad_p):
        probs = jnp.exp2(logits * LOG2E)
        return probs.astype(BF16), (probs * grad_p).astype(BF16)

    def grads(unit, probs, scores):
        at, head = unit
        p, cut = at // tokens, slice(at % tokens, at % tokens + rows)
        dv[head] = nn(probs, grad[...])
        dk[head] = nn(scores, q_ref[...])
        dq[head] = dq[head] + tn(kvs[p][0, cut], scores)
        if head == 1:
            dkvs[p][0, cut] = both_heads(*dk).astype(BF16)
            dkvs[p][1, cut] = both_heads(*dv).astype(BF16)

    in_stages([(i * rows, head) for i in range(2 * count) for head in range(2)], products, scores_of, grads)
    top = lax.broadcasted_iota(jnp.int32, (PAIR, tokens), 0) < HALF
    dq_out[...] = jnp.where(top, dq[0], dq[1]).T.astype(BF16)


def self_backward_kernel(count, info, q_ref, ctx, lse, grad, *rest):
    kvs, rest = rest[:count], rest[count:]
    dq_out, dkvs, (qa, ga, ka, va, kx, k_all, parts, total) = rest[0], rest[1 : 1 + count], rest[1 + count :]
    tokens = q_ref.shape[0]
    rows = tokens // 2
    low, high = slice(0, rows), slice(rows, 2 * rows)
    backward_operands(count, info, info[4], q_ref, ctx, lse, grad, kvs, qa, ga, ka, va, kx)
    for p in range(count):
        k_all[p * tokens : (p + 1) * tokens] = kvs[p][0]
    causal = causal_mask(rows, True)
    fixed, free = tile_rows(info, count, rows)
    tiles = [(high, pl.ds(k, rows), False, None) for k in fixed]
    tiles += [(high, high, True, None), (low, low, True, None)]
    tiles += [(pl.ds(q, rows), pl.ds(k, rows), False, q > 0) for q, k in free]
    dq_low, dq_high = [0.0, 0.0], [0.0, 0.0]
    dk, dv = [None, None], [None, None]

    def products(unit):
        t, head = unit
        q_cut, k_cut = tiles[t][:2]
        return nt(ka[head, k_cut], qa[head, q_cut]), nt(va[head, k_cut], ga[head, q_cut])

    def scores_of(unit, logits, grad_p):
        if tiles[unit[0]][2]:
            logits = jnp.where(causal, logits, NEGATIVE)
        probs = jnp.exp2(logits * LOG2E)
        return probs.astype(BF16), (probs * grad_p).astype(BF16)

    def grads(unit, probs, scores):
        t, head = unit
        q_cut, k_cut, _, is_high = tiles[t]
        dv[head] = nn(probs, grad[q_cut])
        dk[head] = nn(scores, q_ref[q_cut])
        part = tn(k_all[k_cut], scores)
        if q_cut is high:
            dq_high[head] = dq_high[head] + part
        elif q_cut is low:
            dq_low[head] = dq_low[head] + part
        else:
            dq_high[head] = dq_high[head] + jnp.where(is_high, part, 0.0)
            dq_low[head] = dq_low[head] + jnp.where(is_high, 0.0, part)
        if head == 1:
            parts[0, t] = both_heads(*dk)
            parts[1, t] = both_heads(*dv)

    in_stages([(t, head) for t in range(len(tiles)) for head in range(2)], products, scores_of, grads)
    top = lax.broadcasted_iota(jnp.int32, (PAIR, rows), 0) < HALF
    dq_out[low] = jnp.where(top, *dq_low).T.astype(BF16)
    dq_out[high] = jnp.where(top, *dq_high).T.astype(BF16)
    total[...] = jnp.zeros_like(total)
    for i in range(2):
        total[i, high] = parts[i, count]
        total[i, low] = parts[i, count + 1]
    base = INFO_HEAD + 2 * count

    @pl.loop(0, 2 * count - 1)
    def _(t):
        is_free = (t >= count).astype(jnp.int32)
        at = pl.multiple_of(info[base + t + is_free * (count - 1)], rows)
        for i in range(2):
            total[i, pl.ds(at, rows)] += parts[i, t + 2 * is_free]

    for p in range(count):
        cut = slice(p * tokens, (p + 1) * tokens)
        for i in range(2):
            dkvs[p][i] = total[i, cut].astype(BF16)


def run_backward(info, q, ctx, lse, grad, kvs, causal, first=0, pairs=None):
    tokens, width = q.shape
    pairs = pairs or width // PAIR
    width = pairs * PAIR
    rows = tokens // 2
    count = len(kvs)
    keys = count * tokens
    wide, kv, lse_spec = attention_specs(count, tokens, first)
    wide_out, kv_out, _ = attention_specs(count, tokens)
    scratch = [pltpu.VMEM((2, tokens, PAIR), BF16)] * 2 + [pltpu.VMEM((2, keys, PAIR), BF16)] * 3
    if causal:
        scratch += [
            pltpu.VMEM((keys, PAIR), BF16),
            pltpu.VMEM((2, 2 * count + 1, rows, PAIR), F32),
            pltpu.VMEM((2, keys, PAIR), F32),
        ]
    return pl.pallas_call(
        functools.partial(self_backward_kernel if causal else cross_backward_kernel, count),
        grid=(pairs,),
        out_shape=(as_struct((tokens, width), BF16),) + (as_struct((2, tokens, width), BF16),) * count,
        in_specs=[SMEM_SPEC, wide, wide, lse_spec, wide] + [kv] * count,
        out_specs=(wide_out,) + (kv_out,) * count,
        scratch_shapes=scratch,
        compiler_params=pltpu.CompilerParams(vmem_limit_bytes=FULL_LIMIT),
        cost_estimate=cost(2.5e9 * pairs, 6e6),
        name="self_backward" if causal else "cross_backward",
    )(info, q, ctx, lse, grad, *kvs)


def middle_kernel(size, info, first_ref, ctx, og_own, og_other, *rest):
    w2, w3, rest = rest[:size], rest[size : 3 * size], rest[3 * size :]
    vec, fib, keep_out, pass_out, dz2_out, dcross_out = rest[:6]
    slots, (vecs, co, fi, fo, slope, scr, wide, grad_out) = rest[6 : 6 + size], rest[6 + size :]
    place, half = info[0], info[1]
    tokens, width = first_ref.shape
    rows = tokens // 2
    part = width // size
    hidden_part = fo.shape[0] // size
    chunks = fi.shape[1] // width
    assemble(co, w2, place, part, 4 * part)
    for i, ref in enumerate(w3):
        owner, which = place ^ (i // 2), info[6] ^ (i % 2)
        small, large = part // 2, hidden_part // 2
        start = pl.multiple_of(owner * part + which * small, small)
        for c in range(chunks):
            fi[pl.ds(start, small), c * width : (c + 1) * width] = ref[c * small : (c + 1) * small, :]
        start = pl.multiple_of(owner * hidden_part + which * large, large)
        fo[pl.ds(start, large), :] = ref[chunks * small :, :]

    def vector(i):
        return vec[i : i + 1, :]

    resid2 = first_ref[...].astype(F32) + nn(ctx[...], co[...]) + vector(CBO)
    normed2, inverse2 = norm(resid2)
    second = (normed2 * vector(N2G) + vector(N2B)).astype(BF16)
    sums = [0.0]

    def forward_product(c):
        return (nn(second, fi[:, c * width : (c + 1) * width]),)

    def activate(c, value):
        cut = slice(c * width, (c + 1) * width)
        value = value + fib[:, cut]
        sig = 0.5 * jnp.tanh(0.5 * value) + 0.5
        slope[:, cut] = sig * (1.0 + value * (1.0 - sig))
        hidden = (value * sig).astype(BF16)
        scr[:, cut] = hidden
        return (hidden,)

    def add_branch(c, hidden):
        sums[0] = sums[0] + nn(hidden, fo[c * width : (c + 1) * width])

    in_stages(range(chunks), forward_product, activate, add_branch)
    branch = sums[0]
    resid3 = second.astype(F32) + branch + vector(FOB)
    normed3, inverse3 = norm(resid3)
    out = (normed3 * vector(N3G) + vector(N3B)).astype(BF16)
    keep_out[...], pass_out[...] = ordered(info, out[:rows], out[rows:])

    live = info[4]
    iota = lax.broadcasted_iota(jnp.int32, (rows, 1), 0)
    low, high = ordered(info, og_own[half], og_other[...])
    grad3 = jnp.concatenate(
        [
            jnp.where(iota + info[2] < live, low.astype(F32), 0.0),
            jnp.where(iota + info[3] < live, high.astype(F32), 0.0),
        ],
        axis=0,
    )
    dz3 = norm_back(grad3, normed3, inverse3, vector(N3G))
    vecs[...] = jnp.zeros_like(vecs)
    vecs[N3G : N3G + 1] = row_sum(grad3 * normed3)
    vecs[N3B : N3B + 1] = row_sum(grad3)
    dy = dz3.astype(BF16)
    vecs[FOB : FOB + 1] = row_sum(dy.astype(F32))
    second_t = second.T
    sums = [dz3]

    def backward_products(c):
        cut = slice(c * width, (c + 1) * width)
        grad_out[cut] = tn(scr[:, cut], dy).astype(BF16)
        return (nt(dy, fo[cut]),)

    def slope_back(c, grad):
        dpre = (grad * slope[:, c * width : (c + 1) * width]).astype(BF16)
        vecs[FIB + c : FIB + c + 1] = row_sum(dpre.astype(F32))
        return (dpre,)

    def input_grads(c, dpre):
        sums[0] = sums[0] + nt(dpre, fi[:, c * width : (c + 1) * width])
        wide[...] = nn(second_t, dpre)
        scatter_rows(slots, wide, place, part, c * part)

    in_stages(range(chunks), backward_products, slope_back, input_grads)
    dsecond = sums[0]
    for k, slot in enumerate(slots):
        start = pl.multiple_of((place ^ k) * hidden_part, hidden_part)
        slot[chunks * part : chunks * part + hidden_part, :] = grad_out[pl.ds(start, hidden_part), :]
    dz2 = norm_back(dsecond, normed2, inverse2, vector(N2G))
    vecs[N2G : N2G + 1] = row_sum(dsecond * normed2)
    vecs[N2B : N2B + 1] = row_sum(dsecond)
    dz2_out[...] = dz2
    da2 = dz2.astype(BF16)
    vecs[CBO : CBO + 1] = row_sum(da2.astype(F32))
    dcross_out[...] = nt(da2, co[...]).astype(BF16)
    wide[...] = tn(ctx[...], da2)
    scatter_rows(slots, wide, place, part, chunks * part + hidden_part)


def run_middle(info, first, ctx, og_own, og_other, w2, w3, vec, fib):
    tokens, width = first.shape
    size = len(w2)
    part = width // size
    ff = fib.shape[1]
    grad_rows = (ff // width) * part + ff // size + part
    pack = as_struct((grad_rows, width), BF16)
    return pl.pallas_call(
        functools.partial(middle_kernel, size),
        out_shape=(
            as_struct((tokens // 2, width), BF16),
            as_struct((tokens // 2, width), BF16),
            as_struct((tokens, width), F32),
            as_struct((tokens, width), BF16),
            *(pack,) * size,
            as_struct((VEC_ROWS, width), F32),
        ),
        in_specs=[SMEM_SPEC] + [VMEM_SPEC] * (4 + 3 * size + 2),
        out_specs=(VMEM_SPEC,) * (5 + size),
        scratch_shapes=[
            pltpu.VMEM((width, width), BF16),
            pltpu.VMEM((width, ff), BF16),
            pltpu.VMEM((ff, width), BF16),
            pltpu.VMEM((tokens, ff), F32),
            pltpu.VMEM((tokens, ff), BF16),
            pltpu.VMEM((width, width), F32),
            pltpu.VMEM((ff, width), BF16),
        ],
        compiler_params=pltpu.CompilerParams(vmem_limit_bytes=MIDDLE_LIMIT),
        cost_estimate=cost(12 * tokens * width * ff, 2e7),
        name="middle",
    )(info, first, ctx, og_own, og_other, *w2, *w3, vec, fib)


def after_cross_kernel(size, info, dz2, dq, first_ref, x_ref, ctx, *rest):
    w2, rest = rest[:size], rest[size:]
    vec, dz1_out, dself_out = rest[:3]
    slots, (vecs, weight, wide) = rest[3 : 3 + size], rest[3 + size :]
    place = info[0]
    width = x_ref.shape[1]
    part = width // size
    for i in range(2):
        assemble(weight, w2, place, part, i * part, i)

    def vector(i):
        return vec[i : i + 1, :]

    vecs[...] = jnp.zeros_like(vecs)
    dfirst = dz2[...] + SCALE * nt(dq[...], weight[1])
    resid = x_ref[...].astype(F32) + nn(ctx[...], weight[0]) + vector(SBO)
    normed, inverse = norm(resid)
    dz1 = norm_back(dfirst, normed, inverse, vector(N1G))
    vecs[N1G : N1G + 1] = row_sum(dfirst * normed)
    vecs[N1B : N1B + 1] = row_sum(dfirst)
    vecs[CBQ : CBQ + 1] = row_sum(dq[...].astype(F32)) * SCALE
    dz1_out[...] = dz1
    da1 = dz1.astype(BF16)
    vecs[SBO : SBO + 1] = row_sum(da1.astype(F32))
    dself_out[...] = nt(da1, weight[0]).astype(BF16)
    wide[...] = tn(ctx[...], da1)
    scatter_rows(slots, wide, place, part, 0)
    wide[...] = tn(first_ref[...], dq[...]) * SCALE
    scatter_rows(slots, wide, place, part, part)


def run_after_cross(info, dz2, dq, first, x, ctx, w2, vec):
    tokens, width = x.shape
    size = len(w2)
    pack = as_struct((2 * (width // size), width), BF16)
    return pl.pallas_call(
        functools.partial(after_cross_kernel, size),
        out_shape=(
            as_struct((tokens, width), F32),
            as_struct((tokens, width), BF16),
            *(pack,) * size,
            as_struct((VEC_ROWS, width), F32),
        ),
        in_specs=[SMEM_SPEC] + [VMEM_SPEC] * (6 + size),
        out_specs=(VMEM_SPEC,) * (3 + size),
        scratch_shapes=[pltpu.VMEM((2, width, width), BF16), pltpu.VMEM((width, width), F32)],
        compiler_params=pltpu.CompilerParams(vmem_limit_bytes=FULL_LIMIT),
        cost_estimate=cost(10 * tokens * width * width, 8e6),
        name="after_cross",
    )(info, dz2, dq, first, x, ctx, *w2, vec)


def encoder_back_kernel(size, info, own, got, x_ref, *rest):
    w2, given, rest = rest[:size], rest[size : 2 * size], rest[2 * size :]
    keep_out, pass_out = rest[:2]
    slots, (vecs, weight, wide) = rest[2 : 2 + size], rest[2 + size :]
    place = info[0]
    width = x_ref.shape[1]
    rows = x_ref.shape[0] // 2
    part = width // size
    for i in range(2):
        assemble(weight, w2, place, part, (2 + i) * part, i)
    vecs[...] = jnp.zeros_like(vecs)
    for slot, ref in zip(slots, given):
        slot[: 2 * part, :] = ref[...]
    total = None
    for i in range(2):
        grad = (own[i].astype(F32) + got[i].astype(F32)).astype(BF16)
        if i == 1:
            vecs[CBV : CBV + 1] = row_sum(grad.astype(F32))
        wide[...] = tn(x_ref[...], grad)
        scatter_rows(slots, wide, place, part, (2 + i) * part)
        term = nt(grad, weight[i])
        total = term if total is None else total + term
    total = total.astype(BF16)
    keep_out[...], pass_out[...] = ordered(info, total[:rows], total[rows:])


def run_encoder_back(info, own, got, x, w2, given):
    tokens, width = x.shape
    size = len(w2)
    pack = as_struct((4 * (width // size), width), BF16)
    return pl.pallas_call(
        functools.partial(encoder_back_kernel, size),
        out_shape=(
            as_struct((tokens // 2, width), BF16),
            as_struct((tokens // 2, width), BF16),
            *(pack,) * size,
            as_struct((VEC_ROWS, width), F32),
        ),
        in_specs=[SMEM_SPEC] + [VMEM_SPEC] * (3 + 2 * size),
        out_specs=(VMEM_SPEC,) * (3 + size),
        scratch_shapes=[pltpu.VMEM((2, width, width), BF16), pltpu.VMEM((width, width), F32)],
        compiler_params=pltpu.CompilerParams(vmem_limit_bytes=FULL_LIMIT),
        cost_estimate=cost(8 * tokens * width * width, 8e6),
        name="encoder_back",
    )(info, own, got, x, *w2, *given)


def side_by_side(refs):
    return jnp.concatenate([ref[...] for ref in refs], axis=-1)


def target_back_kernel(size, hidden, info, dz1, dq_a, dq_b, own_a, own_b, got_a, got_b, x_ref, *rest):
    w1, others, rest = rest[:size], rest[size : size + 3], rest[size + 3 :]
    keep_out, pass_out = rest[:2]
    slots, (vecs, by_owner, weight, wide) = rest[2 : 2 + size], rest[2 + size :]
    place = info[0]
    width = x_ref.shape[1]
    rows = x_ref.shape[0] // 2
    part = width // size
    for i in range(3):
        assemble(weight, w1, place, part, i * part, i)
    vecs[...] = others[0][...] + others[1][...] + others[2][...]
    dq = side_by_side((dq_a, dq_b))
    vecs[SBQ : SBQ + 1] = row_sum(dq.astype(F32)) * SCALE
    total = dz1[...] + SCALE * nt(dq, weight[0])
    wide[...] = tn(x_ref[...], dq) * SCALE
    scatter_rows(slots, wide, place, part, 0)
    for i in range(2):
        own = side_by_side((own_a.at[i], own_b.at[i])).astype(F32)
        grad = (own + side_by_side((got_a.at[i], got_b.at[i])).astype(F32)).astype(BF16)
        if i == 1:
            vecs[SBV : SBV + 1] = row_sum(grad.astype(F32))
        wide[...] = tn(x_ref[...], grad)
        scatter_rows(slots, wide, place, part, (1 + i) * part)
        total = total + nt(grad, weight[1 + i])
    total = total.astype(BF16)
    keep_out[...], pass_out[...] = ordered(info, total[:rows], total[rows:])
    chunks = hidden // width
    for j in range(size):
        by_owner[j] = jnp.zeros((VEC_ROWS, width), F32)
        by_owner[j, :, :part] = vecs[:, j * part : (j + 1) * part]
        for i in range(chunks):
            at = (j * chunks + i) * part
            row = FIB + at // width
            by_owner[j, FIB + i : FIB + i + 1, :part] = vecs[row : row + 1, at % width : at % width + part]
    for k, slot in enumerate(slots):
        slot[3 * part :, :] = by_owner[place ^ k].astype(BF16)


def run_target_back(hidden, info, dz1, dqs, owns, gots, x, w1, others):
    tokens, width = x.shape
    size = len(w1)
    pack = as_struct((3 * (width // size) + VEC_ROWS, width), BF16)
    return pl.pallas_call(
        functools.partial(target_back_kernel, size, hidden),
        out_shape=(
            as_struct((tokens // 2, width), BF16),
            as_struct((tokens // 2, width), BF16),
            *(pack,) * size,
        ),
        in_specs=[SMEM_SPEC] + [VMEM_SPEC] * (11 + size),
        out_specs=(VMEM_SPEC,) * (2 + size),
        scratch_shapes=[
            pltpu.VMEM((VEC_ROWS, width), F32),
            pltpu.VMEM((size, VEC_ROWS, width), F32),
            pltpu.VMEM((3, width, width), BF16), pltpu.VMEM((width, width), F32),
        ],
        compiler_params=pltpu.CompilerParams(vmem_limit_bytes=DENSE_LIMIT),
        cost_estimate=cost(12 * tokens * width * width, 8e6),
        name="target_back",
    )(info, dz1, *dqs, *owns, *gots, x, *w1, *others)


def add(left, right):
    return (left.astype(F32) + right.astype(F32)).astype(BF16)


class GroupSum:
    def __init__(self, slots):
        self.keep = slots[0::2]
        self.own, *self.far = [send_xor(v, "group", 1) for v in slots[1::2]]

    def start(self):
        parts = [None] + [add(k, f) for k, f in zip(self.keep[1:], self.far)]
        mask, self.arrived = 2, []
        while len(parts) > 1:
            arrived = [send_xor(p, "group", mask) for p in parts[1::2]]
            self.arrived.append(arrived[0])
            parts = [None] + [add(a, b) for a, b in zip(parts[2::2], arrived[1:])]
            mask *= 2

    def addends(self):
        return [self.keep[0], self.own, *self.arrived]

    def finish(self):
        return functools.reduce(lambda a, b: a + b, [v.astype(F32) for v in self.addends()]).astype(BF16)


def piece_shape(rows, width, size):
    return rows // 2, 2 * width // size


def pieces_kernel(count, *refs):
    addends, (out,) = refs[:count], refs[count:]
    size, rows, lanes = out.shape
    total = functools.reduce(lambda a, b: a + b, [v[...].astype(F32) for v in addends]).astype(BF16)
    for j in range(size):
        row, lane = (j % 2) * rows, (j // 2) * lanes
        out[j] = total[row : row + rows, lane : lane + lanes]


def run_pieces(addends, size):
    rows, width = addends[0].shape
    return pl.pallas_call(
        functools.partial(pieces_kernel, len(addends)),
        out_shape=as_struct((size, *piece_shape(rows, width, size)), BF16),
        in_specs=[VMEM_SPEC] * len(addends),
        out_specs=VMEM_SPEC,
        compiler_params=pltpu.CompilerParams(vmem_limit_bytes=DENSE_LIMIT),
        cost_estimate=cost(0, 0),
        name="pieces",
    )(*addends)


def sum_pieces_kernel(parts, out):
    total = parts[0].astype(F32)
    for j in range(1, parts.shape[0]):
        total = total + parts[j].astype(F32)
    for j in range(parts.shape[0]):
        out[j] = total.astype(BF16)


def run_sum_pieces(parts):
    return pl.pallas_call(
        sum_pieces_kernel,
        out_shape=as_struct(parts.shape, BF16),
        in_specs=[VMEM_SPEC],
        out_specs=VMEM_SPEC,
        compiler_params=pltpu.CompilerParams(vmem_limit_bytes=DENSE_LIMIT),
        cost_estimate=cost(0, 0),
        name="sum_pieces",
    )(parts)


def whole_kernel(cuts, part, chunks, parts, *refs):
    *outs, full = refs
    size, rows, lanes = parts.shape
    for j in range(size):
        row, lane = (j % 2) * rows, (j // 2) * lanes
        full[row : row + rows, lane : lane + lanes] = parts[j].astype(F32)
    for (start, stop), out in zip(cuts, outs):
        out[...] = full[start:stop]
    base = cuts[-1][1]
    for i in range(FIB):
        outs[len(cuts) + i][...] = full[base + i : base + i + 1, :part]
    for i in range(chunks):
        outs[-1][:, i * part : (i + 1) * part] = full[base + FIB + i : base + FIB + i + 1, :part]


def run_whole(parts, cuts, part, chunks):
    size, rows, lanes = parts.shape
    width = lanes * size // 2
    shapes = [(stop - start, width) for start, stop in cuts] + [(1, part)] * FIB + [(1, chunks * part)]
    return pl.pallas_call(
        functools.partial(whole_kernel, cuts, part, chunks),
        out_shape=tuple(as_struct(shape, F32) for shape in shapes),
        in_specs=[VMEM_SPEC],
        out_specs=(VMEM_SPEC,) * len(shapes),
        scratch_shapes=[pltpu.VMEM((2 * rows, width), F32)],
        compiler_params=pltpu.CompilerParams(vmem_limit_bytes=DENSE_LIMIT),
        cost_estimate=cost(0, 0),
        name="whole",
    )(parts)


def exchange(parts):
    return lax.all_to_all(parts, "replica", 0, 0)


def halves(value, dim):
    cut = value.shape[dim] // 2
    return lax.slice_in_dim(value, 0, cut, axis=dim), lax.slice_in_dim(value, cut, 2 * cut, axis=dim)


class ReplicaSum:
    def __init__(self, value, whole=1):
        self.value = value
        self.size = lax.axis_size("replica")
        self.place = lax.axis_index("replica")
        masks = [1 << i for i in range(self.size.bit_length() - 1)]
        last = len(masks) - whole
        self.steps = [(m, "halve") for m in masks[:last]] + [(m, "whole") for m in masks[last:]]
        self.steps += [(m, "gather") for m in reversed(masks[:last])]
        self.dims = {}

    def start(self):
        mask, kind = self.steps[0]
        give = self.value
        if kind == "halve":
            up = (self.place & mask) != 0
            dim = 0 if mask == 1 else 1
            self.dims[mask] = dim
            low, high = halves(self.value, dim)
            self.value = jnp.where(up, high, low)
            give = jnp.where(up, low, high)
        self.arrived = send_xor(give, "replica", mask)

    def finish(self):
        mask, kind = self.steps.pop(0)
        if kind == "gather":
            up = (self.place & mask) != 0
            dim = self.dims[mask]
            self.value = jnp.where(
                up,
                jnp.concatenate([self.arrived, self.value], axis=dim),
                jnp.concatenate([self.value, self.arrived], axis=dim),
            )
        else:
            self.value = add(self.value, self.arrived)


def butterfly(stacked, place, size):
    bit = 1
    while bit < size:
        order = np.arange(size) ^ bit
        flipped = jnp.stack([stacked[int(i)] for i in order])
        stacked = jnp.where((place & bit) != 0, flipped, stacked)
        bit *= 2
    return stacked


def body(
    target, encoder, target_len, encoder_len,
    self_wq, self_wk, self_wv, self_wo, self_bq, self_bv, self_bo, norm1_gain, norm1_bias,
    cross_wq, cross_wk, cross_wv, cross_wo, cross_bq, cross_bv, cross_bo, norm2_gain, norm2_bias,
    ffn_in, ffn_in_bias, ffn_out, ffn_out_bias, norm3_gain, norm3_bias, out_grad,
):
    size = lax.axis_size("group")
    place = lax.axis_index("group")
    _, rows, width = target.shape
    part = width // size
    ff = ffn_in.shape[1]
    chunks = ff // width
    half = (place >= size // 2).astype(jnp.int32)
    table = jnp.asarray(group_table(size, rows))
    side = lax.axis_index("replica") & 1
    lengths = jnp.append(jnp.stack([target_len, encoder_len])[:, half], side)
    info = lax.dynamic_update_slice(table[place], lengths, (4,))
    mirror = [(i, size - 1 - i) for i in range(size)]

    def swap(value):
        return lax.ppermute(value, "group", mirror)

    w1_own, target_half = run_first_pack(info, target, (self_wq, self_wk, self_wv))
    w1 = gather_even(w1_own, "group", size)
    target_got = swap(target_half)
    matrices = (encoder, out_grad, ffn_in, ffn_out, self_wo, cross_wq, cross_wk, cross_wv, cross_wo)
    vectors = (
        self_bq, self_bv, self_bo, norm1_gain, norm1_bias, cross_bq, cross_bv, cross_bo,
        norm2_gain, norm2_bias, ffn_out_bias, norm3_gain, norm3_bias, ffn_in_bias,
    )
    w1_odd, *late = point(send_xor(w1_own, "group", 1), *matrices, *vectors)
    matrices, vectors = late[: len(matrices)], late[len(matrices) :]
    w2_own, *w3_own, encoder_half, og_half = run_second_pack(info, *matrices[:4], matrices[4:])
    vec_own = jnp.concatenate([v.reshape(-1, part) for v in vectors])
    vec_own = jnp.pad(vec_own, ((0, VEC_ROWS - vec_own.shape[0]), (0, 0)))
    vec_odd = send_xor(vec_own, "group", 1)
    vec_pairs = gather_even(jnp.concatenate([vec_own, vec_odd]), "group", size)
    vec_all = jnp.stack(vec_pairs).reshape(size, VEC_ROWS, part)
    vec_all = butterfly(vec_all, place, size)
    vec = jnp.transpose(vec_all, (1, 0, 2)).reshape(VEC_ROWS, width).astype(F32)
    fib = vec_all[:, FIB : FIB + chunks].reshape(1, ff).astype(F32)
    target_got, encoder_half, *w1 = point(target_got, encoder_half, *w1)
    encoder_got = swap(encoder_half)
    w1 = [v for e, o in zip(w1, [w1_odd] + [send_xor(e, "group", 1) for e in w1[1:]]) for v in (e, o)]

    x, q1, kv1 = run_qkv(info, target, target_got, w1, vec)
    kv1, w2_own, encoder_got = point(kv1, w2_own, encoder_got)
    w2 = gather_even(w2_own, "group", size)
    kvs1 = gather_xor(kv1, "group", size // 2)
    ctx1, lse1 = run_forward(info, q1, kvs1, True)
    ctx1, w3_near, w3_far, *w2 = point(ctx1, *w3_own, *w2)
    w2 = with_odd(w2, "group")
    w3_even = gather_even(w3_near, "group", size)[1:]
    w3_odd = [send_xor(w, "group", 1) for w in (w3_near, w3_far)]
    xe, kv2 = run_cross_kv(info, encoder, encoder_got, w2, vec)
    kv2, ctx1 = point(kv2, ctx1)
    kvs2 = gather_xor(kv2, "group", size // 2)
    first, q2 = run_after_self(info, x, ctx1, w2, vec)
    q2, og_half, *w3_even = point(q2, og_half, *w3_even)
    w3_other = [send_xor(w, "replica", 1) for w in w3_even]
    og_got = swap(og_half)
    w3_pass = [send_xor(w, "group", 1) for w in w3_even]
    ctx2, lse2 = run_forward(info, q2, kvs2, False)
    ctx2, og_got, *w3_other = point(ctx2, og_got, *w3_other)
    w3 = [*w3_own, *w3_odd]
    for near, far, passed in zip(w3_even, w3_other, w3_pass):
        w3 += [near, far, passed, send_xor(far, "group", 1)]
    out_keep, out_pass, dz2, dcross, *slots_a, vecs_a = run_middle(
        info, first, ctx2, out_grad, og_got, w2, w3, vec, fib
    )

    def key_value_sums(parts):
        bit = len(parts) // 2
        while bit > 1:
            arrived = [send_xor(parts[k | bit], "group", bit) for k in range(bit)]
            parts = [add(parts[k], arrived[k]) for k in range(bit)]
            bit //= 2
        return parts[0], send_xor(parts[1], "group", 1)

    group_a = GroupSum(slots_a)
    dcross, *group_a.far = point(dcross, *group_a.far)
    group_a.start()
    dq2, *dkvs2 = run_backward(info, q2, ctx2, lse2, dcross, kvs2, False)
    dq2, out_pass, *dkvs2 = point(dq2, out_pass, *dkvs2)
    own2, got2 = key_value_sums(dkvs2)
    dz1, dself, *slots_b, vecs_b = run_after_cross(info, dz2, dq2, first, x, ctx1, w2, vec)
    dself, got2, out_pass, group_a.own, *group_a.arrived = point(
        dself, got2, out_pass, group_a.own, *group_a.arrived
    )
    sum_a = ReplicaSum(group_a.finish(), 0)
    sum_a.start()
    out_got = swap(out_pass)
    enc_keep, enc_pass, *slots_b, vecs_e = run_encoder_back(info, own2, got2, xe, w2, slots_b)
    group_b = GroupSum(slots_b)
    dself, enc_pass, *group_b.far = point(dself, enc_pass, *group_b.far)
    group_b.start()
    enc_got = swap(enc_pass)
    pairs = width // PAIR // 2
    dq1_a, *dkvs1_a = run_backward(info, q1, ctx1, lse1, dself, kvs1, True, 0, pairs)
    dself, sum_a.arrived, *dkvs1_a = point(dself, sum_a.arrived, *dkvs1_a)
    own1_a, got1_a = key_value_sums(dkvs1_a)
    sum_a.finish()
    sum_a.start()
    dq1_b, *dkvs1_b = run_backward(info, q1, ctx1, lse1, dself, kvs1, True, pairs, pairs)
    hops = len(group_b.arrived)
    group_b.own, dq1_b, sum_a.arrived, *moved = point(
        group_b.own, dq1_b, sum_a.arrived, *group_b.arrived, *dkvs1_b
    )
    group_b.arrived, dkvs1_b = moved[:hops], moved[hops:]
    own1_b, got1_b = key_value_sums(dkvs1_b)
    sum_b = ReplicaSum(group_b.finish())
    sum_b.start()
    sum_a.finish()
    sum_a.start()
    tgt_keep, tgt_pass, *slots_c = run_target_back(
        ff, info, dz1, (dq1_a, dq1_b), (own1_a, own1_b), (got1_a, got1_b), x, w1, (vecs_a, vecs_b, vecs_e)
    )

    tgt_pass, sum_a.arrived, sum_b.arrived, *slots_c = point(tgt_pass, sum_a.arrived, sum_b.arrived, *slots_c)

    def advance(*sums):
        for s in sums:
            if s.steps:
                s.finish()
            if s.steps:
                s.start()

    def behind(*values):
        *values, sum_a.value, sum_b.value = point(*values, sum_a.value, sum_b.value)
        return values

    group_c = GroupSum(slots_c)
    group_c.far = behind(*group_c.far)
    group_c.start()
    advance(sum_a, sum_b)
    sum_a.arrived, sum_b.arrived = point(sum_a.arrived, sum_b.arrived)
    advance(sum_a, sum_b)
    group_c.own, *group_c.arrived = behind(group_c.own, *group_c.arrived)
    parts_c = exchange(run_pieces(group_c.addends(), lax.axis_size("replica")))
    tgt_got = swap(tgt_pass)
    sum_a.arrived, sum_b.arrived = point(sum_a.arrived, sum_b.arrived)
    advance(sum_a, sum_b)
    parts_c, tgt_got = behind(parts_c, tgt_got)
    parts_c = exchange(run_sum_pieces(parts_c))
    while sum_a.steps or sum_b.steps:
        advance(sum_a, sum_b)
    a = sum_a.value.astype(F32)
    g_fi = jnp.transpose(a[: chunks * part].reshape(chunks, part, width), (1, 0, 2)).reshape(part, ff)
    g_fo = a[chunks * part : chunks * part + ffn_out.shape[0]]
    g_co = a[chunks * part + ffn_out.shape[0] :]

    def unswap(kept, arrived):
        return jnp.where(half == 0, jnp.stack([kept, arrived]), jnp.stack([arrived, kept]))

    outputs = (unswap(out_keep, out_got), unswap(tgt_keep, tgt_got), unswap(enc_keep, enc_got))
    g_fi, g_fo, g_co, out, grad_tgt, grad_enc, parts_c = point(g_fi, g_fo, g_co, *outputs, parts_c)
    cuts = tuple((i * part, (i + 1) * part) for i in range(3))
    g_sq, g_sk, g_sv, *g_vec = run_whole(parts_c, cuts, part, chunks)
    g_vec = [v.reshape(-1) for v in g_vec]
    b = sum_b.value.astype(F32)
    g_so, g_cq, g_ck, g_cv = (b[i * part : (i + 1) * part] for i in range(4))
    return (
        out, grad_tgt, grad_enc,
        g_sq, g_sk, g_sv, g_so, g_vec[SBQ], g_vec[SBV], g_vec[SBO], g_vec[N1G], g_vec[N1B],
        g_cq, g_ck, g_cv, g_co, g_vec[CBQ], g_vec[CBV], g_vec[CBO], g_vec[N2G], g_vec[N2B],
        g_fi, g_vec[FIB], g_fo, g_vec[FOB], g_vec[N3G], g_vec[N3B],
    )


def solution(mesh):
    seq, lens, mat, vec = P("replica", "group", None), P("replica"), P("group", None), P("group")
    layer = (mat,) * 4 + (vec,) * 5 + (mat,) * 4 + (vec,) * 5 + (mat, vec, mat, vec, vec, vec)
    in_specs = (seq, seq, lens, lens) + layer + (seq,)
    out_specs = (seq,) * 3 + layer
    return jax.shard_map(body, mesh=mesh, in_specs=in_specs, out_specs=out_specs, check_vma=False)
```

```python
import functools

import jax
import jax.numpy as jnp
import numpy as np
from jax import lax
from jax.experimental import pallas as pl
from jax.experimental.pallas import tpu as pltpu
from jax.sharding import PartitionSpec as P

F32 = jnp.float32
BF16 = jnp.bfloat16
HEADS = 8
PAIR = 128
HALF = 64
SCALE = 0.125
NEGATIVE = -1e30
EPSILON = 1e-5
LOG2E = 1.4426950408889634
DENSE_LIMIT = 20 << 20
FULL_LIMIT = 56 << 20
MIDDLE_LIMIT = 40 << 20

(SBQ, SBV, SBO, N1G, N1B, CBQ, CBV, CBO, N2G, N2B, FOB, N3G, N3B, FIB) = range(14)
VEC_ROWS = 32
INFO_HEAD = 7

VMEM_SPEC = pl.BlockSpec(memory_space=pltpu.VMEM)
LOHI = True
ROW_SPLIT = 1
SMEM_SPEC = pl.BlockSpec(memory_space=pltpu.SMEM)


def nn(left, right):
    return lax.dot_general(left, right, (((1,), (0,)), ((), ())), preferred_element_type=F32)


def nt(left, right):
    return lax.dot_general(left, right, (((1,), (1,)), ((), ())), preferred_element_type=F32)


def tn(left, right):
    return lax.dot_general(left, right, (((0,), (0,)), ((), ())), preferred_element_type=F32)


def as_struct(shape, dtype):
    return jax.ShapeDtypeStruct(shape, dtype)


def cost(flops, nbytes):
    return pl.CostEstimate(flops=1000, bytes_accessed=1000, transcendentals=0)


def send_xor(value, axis, mask):
    size = lax.axis_size(axis)
    return lax.ppermute(value, axis, [(i, i ^ mask) for i in range(size)])


def gather_xor(value, axis, size):
    found = {0: value}
    bit = size // 2
    while bit:
        found.update({k | bit: send_xor(v, axis, bit) for k, v in list(found.items())})
        bit //= 2
    return [found[k] for k in range(size)]


def gather_even(value, axis, size):
    found = {0: value}
    bit = size // 2
    while bit > 1:
        found.update({k | bit: send_xor(v, axis, bit) for k, v in list(found.items())})
        bit //= 2
    return [found[k] for k in range(0, size, 2)]


def with_odd(evens, axis):
    odds = [send_xor(e, axis, 1) for e in evens]
    return [v for pair in zip(evens, odds) for v in pair]


def point(*values):
    return lax.optimization_barrier(values)


def group_table(size, rows):
    half = size // 2
    table = []
    for g in range(size):
        upper = g >= half
        low = min(g, size - 1 - g)
        row = [g, int(upper), low * rows, (size - 1 - low) * rows, 0, 0, 0]
        for k in range(half):
            d = min(g ^ k, size - 1 - (g ^ k))
            row += [d * rows, (size - 1 - d) * rows]

        def place(b):
            d = b if (b >= half) == upper else size - 1 - b
            return ((g ^ d) * 2 + int(b >= half)) * rows

        free = [(1, b) for b in range(half, size - 1 - low)] + [(0, b) for b in range(low)]
        row += [place(b) for b in range(half)]
        row += [s * rows for s, _ in free] + [place(b) for _, b in free]
        table.append(row)
    return np.asarray(table, np.int32)


def assemble(dest, refs, place, rows, source, index=None):
    for k, ref in enumerate(refs):
        start = pl.multiple_of((place ^ k) * rows, rows)
        block = ref[source : source + rows, :]
        if index is None:
            dest[pl.ds(start, rows), :] = block
        else:
            dest[index, pl.ds(start, rows), :] = block


def scatter_rows(slots, grad, place, rows, offset):
    for k, slot in enumerate(slots):
        start = pl.multiple_of((place ^ k) * rows, rows)
        slot[offset : offset + rows, :] = grad[pl.ds(start, rows), :].astype(BF16)


def norm(resid):
    centred = resid - jnp.mean(resid, axis=-1, keepdims=True)
    inverse = lax.rsqrt(jnp.mean(centred * centred, axis=-1, keepdims=True) + EPSILON)
    return centred * inverse, inverse


def norm_back(grad, normed, inverse, gain):
    scaled = grad * gain
    return inverse * (
        scaled
        - jnp.mean(scaled, axis=-1, keepdims=True)
        - normed * jnp.mean(scaled * normed, axis=-1, keepdims=True)
    )


def ordered(info, own, other):
    upper = info[1] == 1
    return jnp.where(upper, other, own), jnp.where(upper, own, other)


def row_sum(value):
    return jnp.sum(value, axis=0, keepdims=True)


def qkv_kernel(size, info, own, other, *rest):
    ws, (vec, x_out, q_out, kv_out, weight) = rest[:size], rest[size:]
    place, half = info[0], info[1]
    rows, width = other.shape
    part = width // size
    for i in range(3):
        assemble(weight, ws, place, part, i * part, i)
    x = jnp.concatenate(ordered(info, own[half], other[...]), axis=0)
    x_out[...] = x
    q_out[...] = ((nn(x, weight[0]) + vec[SBQ : SBQ + 1, :]) * SCALE).astype(BF16)
    kv_out[0] = nn(x, weight[1]).astype(BF16)
    kv_out[1] = (nn(x, weight[2]) + vec[SBV : SBV + 1, :]).astype(BF16)


def run_qkv(info, own, other, ws, vec):
    rows, width = other.shape
    tokens = 2 * rows
    return pl.pallas_call(
        functools.partial(qkv_kernel, len(ws)),
        out_shape=(
            as_struct((tokens, width), BF16),
            as_struct((tokens, width), BF16),
            as_struct((2, tokens, width), BF16),
        ),
        in_specs=[SMEM_SPEC] + [VMEM_SPEC] * (3 + len(ws)),
        out_specs=(VMEM_SPEC,) * 3,
        scratch_shapes=[pltpu.VMEM((3, width, width), BF16)],
        compiler_params=pltpu.CompilerParams(vmem_limit_bytes=DENSE_LIMIT),
        cost_estimate=cost(6 * tokens * width * width, 4e6),
        name="qkv",
    )(info, own, other, *ws, vec)


def first_pack_kernel(info, target, wq, wk, wv, w_out, other_out):
    part = wq.shape[0]
    for i, w in enumerate((wq, wk, wv)):
        w_out[i * part : (i + 1) * part] = w[...]
    other_out[...] = target[1 - info[1]]


def run_first_pack(info, target, ws):
    _, rows, width = target.shape
    return pl.pallas_call(
        first_pack_kernel,
        out_shape=(as_struct((3 * ws[0].shape[0], width), BF16), as_struct((rows, width), BF16)),
        in_specs=[SMEM_SPEC] + [VMEM_SPEC] * 4,
        out_specs=(VMEM_SPEC,) * 2,
        compiler_params=pltpu.CompilerParams(vmem_limit_bytes=FULL_LIMIT),
        cost_estimate=cost(0, 0),
        name="first_pack",
    )(info, target, *ws)


def second_pack_kernel(info, encoder, og, w_in, w_out, *refs):
    ws, (w2_out, near_out, far_out, enc_out, og_out) = refs[:5], refs[5:]
    part, width = ws[0].shape
    for i, w in enumerate(ws):
        w2_out[i * part : (i + 1) * part] = w[...]
    enc_out[...] = encoder[1 - info[1]]
    og_out[...] = og[1 - info[1]]
    small, large = part // 2, w_out.shape[0] // 2
    chunks = w_in.shape[1] // width
    for which, out in enumerate((near_out, far_out)):
        at = pl.multiple_of((info[6] ^ which) * small, small)
        for c in range(chunks):
            out[c * small : (c + 1) * small] = w_in[pl.ds(at, small), c * width : (c + 1) * width]
        at = pl.multiple_of((info[6] ^ which) * large, large)
        out[chunks * small :] = w_out[pl.ds(at, large)]


def run_second_pack(info, encoder, og, w_in, w_out, ws):
    _, rows, width = encoder.shape
    block = as_struct((rows, width), BF16)
    half = as_struct((w_in.shape[0] // 2 * (w_in.shape[1] // width) + w_out.shape[0] // 2, width), BF16)
    return pl.pallas_call(
        second_pack_kernel,
        out_shape=(as_struct((5 * ws[0].shape[0], width), BF16), half, half, block, block),
        in_specs=[SMEM_SPEC] + [VMEM_SPEC] * 9,
        out_specs=(VMEM_SPEC,) * 5,
        compiler_params=pltpu.CompilerParams(vmem_limit_bytes=FULL_LIMIT),
        cost_estimate=cost(0, 0),
        name="second_pack",
    )(info, encoder, og, w_in, w_out, *ws)


def cross_kv_kernel(size, info, own, other, *rest):
    ws, (vec, x_out, kv_out, weight) = rest[:size], rest[size:]
    place, half = info[0], info[1]
    rows, width = other.shape
    part = width // size
    for i in range(2):
        assemble(weight, ws, place, part, (2 + i) * part, i)
    x = jnp.concatenate(ordered(info, own[half], other[...]), axis=0)
    x_out[...] = x
    kv_out[0] = nn(x, weight[0]).astype(BF16)
    kv_out[1] = (nn(x, weight[1]) + vec[CBV : CBV + 1, :]).astype(BF16)


def run_cross_kv(info, own, other, ws, vec):
    rows, width = other.shape
    tokens = 2 * rows
    return pl.pallas_call(
        functools.partial(cross_kv_kernel, len(ws)),
        out_shape=(as_struct((tokens, width), BF16), as_struct((2, tokens, width), BF16)),
        in_specs=[SMEM_SPEC] + [VMEM_SPEC] * (3 + len(ws)),
        out_specs=(VMEM_SPEC,) * 2,
        scratch_shapes=[pltpu.VMEM((2, width, width), BF16)],
        compiler_params=pltpu.CompilerParams(vmem_limit_bytes=DENSE_LIMIT),
        cost_estimate=cost(4 * tokens * width * width, 4e6),
        name="cross_kv",
    )(info, own, other, *ws, vec)


def after_self_kernel(size, info, x_ref, ctx, *rest):
    ws, (vec, first_out, q_out, weight) = rest[:size], rest[size:]
    place = info[0]
    width = x_ref.shape[1]
    part = width // size
    for i in range(2):
        assemble(weight, ws, place, part, i * part, i)
    resid = x_ref[...].astype(F32) + nn(ctx[...], weight[0]) + vec[SBO : SBO + 1, :]
    normed, _ = norm(resid)
    first = (normed * vec[N1G : N1G + 1, :] + vec[N1B : N1B + 1, :]).astype(BF16)
    first_out[...] = first
    q_out[...] = ((nn(first, weight[1]) + vec[CBQ : CBQ + 1, :]) * SCALE).astype(BF16)


def run_after_self(info, x, ctx, ws, vec):
    tokens, width = x.shape
    return pl.pallas_call(
        functools.partial(after_self_kernel, len(ws)),
        out_shape=(as_struct((tokens, width), BF16),) * 2,
        in_specs=[SMEM_SPEC] + [VMEM_SPEC] * (3 + len(ws)),
        out_specs=(VMEM_SPEC,) * 2,
        scratch_shapes=[pltpu.VMEM((2, width, width), BF16)],
        compiler_params=pltpu.CompilerParams(vmem_limit_bytes=DENSE_LIMIT),
        cost_estimate=cost(4 * tokens * width * width, 4e6),
        name="after_self",
    )(info, x, ctx, *ws, vec)


def lanes_of(rows):
    return lax.broadcasted_iota(jnp.int32, (rows, PAIR), 1)


def lane_row(head):
    return ((lax.broadcasted_iota(jnp.int32, (1, PAIR), 1) // HALF) == head).astype(F32).astype(BF16)


def split3(value):
    a = value.astype(BF16)
    rest = value - a.astype(F32)
    b = rest.astype(BF16)
    c = (rest - b.astype(F32)).astype(BF16)
    return a, b, c


def lane_pieces(value, base, rows):
    lane = lanes_of(rows)
    a, b, c = (p.astype(F32) for p in split3(value))
    return jnp.where(lane == base, a, jnp.where(lane == base + 1, b, jnp.where(lane == base + 2, c, 0.0)))


def put_key_extras(kx, info, count, rows, limit, ones):
    for p in range(count):
        for slot in range(2):
            at = (2 * p + slot) * rows
            pos = info[INFO_HEAD + 2 * p + slot] + lax.broadcasted_iota(jnp.int32, (rows, PAIR), 0)
            lane = lanes_of(rows)
            for head in range(2):
                spare = HALF * (1 - head)
                extra = jnp.where((lane == spare) & (pos >= limit), NEGATIVE, 0.0)
                if ones:
                    extra = jnp.where((lane > spare) & (lane < spare + 4), 1.0, extra)
                kx[head, at : at + rows] = extra.astype(BF16)


def put_operands(dest, parts, head, extra):
    mine = lane_row(head)
    at = 0
    for part in parts:
        rows = part.shape[0]
        add_on = extra[at : at + rows] if extra.shape[0] > 1 else extra
        dest[head, at : at + rows] = part * mine + add_on
        at += rows


def one_lanes(head, first, last):
    lane = lax.broadcasted_iota(jnp.int32, (1, PAIR), 1) - HALF * (1 - head)
    return jnp.where((lane >= first) & (lane < last), 1.0, 0.0).astype(BF16)


def finish_rows(acc, top, head):
    rows = acc.shape[0]
    spare = HALF * (1 - head)
    total = acc[:, spare : spare + 1]
    return acc / total, lane_pieces(-(top + jnp.log(total)), spare + 1, rows)


def forward_operands(count, info, limit, q_ref, kvs, qa, ka, va, kx):
    rows = q_ref.shape[0] // 2

    @pl.when(pl.program_id(0) == 0)
    def _():
        put_key_extras(kx, info, count, rows, limit, False)

    for head in range(2):
        put_operands(qa, [q_ref[...]], head, one_lanes(head, 0, 1))
        put_operands(ka, [kv[0] for kv in kvs], head, kx.at[head])
        put_operands(va, [kv[1] for kv in kvs], head, one_lanes(head, 0, 1))


def weights_of(logits, top):
    return jnp.exp2((logits - top) * LOG2E).astype(BF16)


def store_heads(ctx_out, lse_out, cut, done):
    (context_a, pieces_a), (context_b, pieces_b) = done
    lane = lanes_of(context_a.shape[0])
    ctx_out[cut] = jnp.where(lane < HALF, context_a, context_b).astype(BF16)
    lse_out[cut] = (pieces_a + pieces_b).astype(BF16)


def cross_forward_kernel(count, info, q_ref, *rest):
    kvs, (ctx_out, lse_out, qa, ka, va, kx) = rest[:count], rest[count:]
    rows = q_ref.shape[0] // 2
    forward_operands(count, info, info[5], q_ref, kvs, qa, ka, va, kx)
    step = rows // ROW_SPLIT
    units = [(c, head) for c in range(2 * ROW_SPLIT) for head in range(2)]

    def logits_of(unit):
        c, head = unit
        return nt(qa[head, c * step : (c + 1) * step], ka[head])

    logits, weights, done = {0: logits_of(units[0])}, {}, {}
    for u in range(len(units) + 1):
        if u + 1 < len(units):
            logits[u + 1] = logits_of(units[u + 1])
        if u < len(units):
            now = logits.pop(u)
            top = jnp.max(now, axis=-1, keepdims=True)
            weights[u] = (weights_of(now, top), top)
        if u > 0:
            c, head = units[u - 1]
            probs, top = weights.pop(u - 1)
            done[head] = finish_rows(nn(probs, va[head]), top, head)
            if head == 1:
                store_heads(ctx_out, lse_out, slice(c * step, (c + 1) * step), (done[0], done[1]))


def causal_mask(rows, transposed):
    a = lax.broadcasted_iota(jnp.int32, (rows, rows), 0)
    b = lax.broadcasted_iota(jnp.int32, (rows, rows), 1)
    return a <= b if transposed else b <= a


def tile_rows(info, count, rows):
    base = INFO_HEAD + 2 * count

    def at(i):
        return pl.multiple_of(info[base + i], rows)

    fixed = [at(i) for i in range(count)]
    free = [(at(count + i), at(2 * count - 1 + i)) for i in range(count - 1)]
    return fixed, free


def self_forward_kernel(count, info, q_ref, *rest):
    kvs, (ctx_out, lse_out, qa, ka, va, kx) = rest[:count], rest[count:]
    rows = q_ref.shape[0] // 2
    low, high = slice(0, rows), slice(rows, 2 * rows)
    forward_operands(count, info, info[4], q_ref, kvs, qa, ka, va, kx)
    causal = causal_mask(rows, False)
    fixed, free = tile_rows(info, count, rows)
    key_cuts = [pl.ds(k, rows) for k in fixed] + [high]
    to_high = [q > 0 for q, _ in free]

    def widest(tile):
        return jnp.max(tile, axis=-1, keepdims=True)

    def products(head):
        def logits_of(q_cut, k_cut):
            return nt(qa[head, q_cut], ka[head, k_cut])

        tiles = [logits_of(high, k) for k in key_cuts]
        tile_low = logits_of(low, low)
        extra = [logits_of(pl.ds(q, rows), pl.ds(k, rows)) for q, k in free]
        return tiles, tile_low, extra

    def weigh(tiles, tile_low, extra):
        tiles[-1] = jnp.where(causal, tiles[-1], NEGATIVE)
        tile_low = jnp.where(causal, tile_low, NEGATIVE)
        top_high = widest(functools.reduce(jnp.maximum, tiles))
        top_low = widest(tile_low)
        for tile, is_high in zip(extra, to_high):
            top = widest(tile)
            top_high = jnp.where(is_high, jnp.maximum(top_high, top), top_high)
            top_low = jnp.where(is_high, top_low, jnp.maximum(top_low, top))
        free_weights = [
            weights_of(tile, jnp.where(is_high, top_high, top_low)) for tile, is_high in zip(extra, to_high)
        ]
        return [weights_of(t, top_high) for t in tiles], weights_of(tile_low, top_low), free_weights, top_high, top_low

    def contexts(head, tiles, tile_low, extra, top_high, top_low):
        acc_high = sum(nn(t, va[head, k]) for t, k in zip(tiles, key_cuts))
        acc_low = nn(tile_low, va[head, low])
        for tile, is_high, (_, k) in zip(extra, to_high, free):
            part = nn(tile, va[head, pl.ds(k, rows)])
            acc_high = acc_high + jnp.where(is_high, part, 0.0)
            acc_low = acc_low + jnp.where(is_high, 0.0, part)
        return finish_rows(acc_low, top_low, head), finish_rows(acc_high, top_high, head)

    first, second = products(0), products(1)
    first = weigh(*first)
    first = contexts(0, *first)
    second = contexts(1, *weigh(*second))
    store_heads(ctx_out, lse_out, low, (first[0], second[0]))
    store_heads(ctx_out, lse_out, high, (first[1], second[1]))


def attention_limit(keys):
    return (10 << 20) + keys * (12 << 10)


def attention_specs(count, tokens, first=0):
    wide = pl.BlockSpec((tokens, PAIR), lambda i: (0, i + first))
    kv = pl.BlockSpec((2, tokens, PAIR), lambda i: (0, 0, i + first))
    lse = pl.BlockSpec((None, tokens, PAIR), lambda i: (i + first, 0, 0))
    return wide, kv, lse


def run_forward(info, q, kvs, causal):
    tokens, width = q.shape
    count = len(kvs)
    keys = count * tokens
    pairs = width // PAIR
    wide, kv, lse = attention_specs(count, tokens)
    kernel = functools.partial(self_forward_kernel if causal else cross_forward_kernel, count)
    return pl.pallas_call(
        kernel,
        grid=(pairs,),
        out_shape=(as_struct((tokens, width), BF16), as_struct((pairs, tokens, PAIR), BF16)),
        in_specs=[SMEM_SPEC, wide] + [kv] * count,
        out_specs=(wide, lse),
        scratch_shapes=[
            pltpu.VMEM((2, tokens, PAIR), BF16),
            pltpu.VMEM((2, keys, PAIR), BF16),
            pltpu.VMEM((2, keys, PAIR), BF16),
            pltpu.VMEM((2, keys, PAIR), BF16),
        ],
        compiler_params=pltpu.CompilerParams(vmem_limit_bytes=attention_limit(keys)),
        cost_estimate=cost(8e9, 4e6),
        name="self_forward" if causal else "cross_forward",
    )(info, q, *kvs)


def backward_operands(count, info, limit, q_ref, ctx, lse, grad, kvs, qa, ga, ka, va, kx):
    tokens = q_ref.shape[0]
    rows = tokens // 2

    @pl.when(pl.program_id(0) == 0)
    def _():
        put_key_extras(kx, info, count, rows, limit, True)

    lane = lanes_of(tokens)
    both = grad[...].astype(F32) * ctx[...].astype(F32)
    for head in range(2):
        mine = (lane // HALF) == head
        spare = HALF * (1 - head)
        far = lane_row(1 - head)
        delta = jnp.sum(jnp.where(mine, both, 0.0), axis=-1, keepdims=True)
        put_operands(qa, [q_ref[...]], head, lse[...] * far + one_lanes(head, 0, 1))
        put_operands(ga, [grad[...]], head, lane_pieces(-delta, spare, tokens).astype(BF16))
        put_operands(ka, [kv[0] for kv in kvs], head, kx.at[head])
        put_operands(va, [kv[1] for kv in kvs], head, one_lanes(head, 0, 3))


def in_stages(units, first, second, third):
    one, two = {0: first(units[0])}, {}
    for u in range(len(units) + 1):
        if u + 1 < len(units):
            one[u + 1] = first(units[u + 1])
        if u < len(units):
            two[u] = second(units[u], *one.pop(u))
        if u > 0:
            third(units[u - 1], *two.pop(u - 1))


def both_heads(a, b):
    return jnp.where(lanes_of(a.shape[0]) < HALF, a, b)


def cross_backward_kernel(count, info, q_ref, ctx, lse, grad, *rest):
    kvs, rest = rest[:count], rest[count:]
    dq_out, dkvs, (qa, ga, ka, va, kx) = rest[0], rest[1 : 1 + count], rest[1 + count :]
    tokens = q_ref.shape[0]
    rows = tokens // 2
    backward_operands(count, info, info[5], q_ref, ctx, lse, grad, kvs, qa, ga, ka, va, kx)
    dq, dk, dv = [0.0, 0.0], [None, None], [None, None]

    def products(unit):
        at, head = unit
        return nt(ka[head, at : at + rows], qa[head]), nt(va[head, at : at + rows], ga[head])

    def scores_of(unit, logits, grad_p):
        probs = jnp.exp2(logits * LOG2E)
        return probs.astype(BF16), (probs * grad_p).astype(BF16)

    def grads(unit, probs, scores):
        at, head = unit
        p, cut = at // tokens, slice(at % tokens, at % tokens + rows)
        dv[head] = nn(probs, grad[...])
        dk[head] = nn(scores, q_ref[...])
        dq[head] = dq[head] + tn(kvs[p][0, cut], scores)
        if head == 1:
            dkvs[p][0, cut] = both_heads(*dk).astype(BF16)
            dkvs[p][1, cut] = both_heads(*dv).astype(BF16)

    in_stages([(i * rows, head) for i in range(2 * count) for head in range(2)], products, scores_of, grads)
    top = lax.broadcasted_iota(jnp.int32, (PAIR, tokens), 0) < HALF
    dq_out[...] = jnp.where(top, dq[0], dq[1]).T.astype(BF16)


def self_backward_kernel(count, info, q_ref, ctx, lse, grad, *rest):
    kvs, rest = rest[:count], rest[count:]
    dq_out, dkvs, (qa, ga, ka, va, kx, k_all, parts, total) = rest[0], rest[1 : 1 + count], rest[1 + count :]
    tokens = q_ref.shape[0]
    rows = tokens // 2
    low, high = slice(0, rows), slice(rows, 2 * rows)
    backward_operands(count, info, info[4], q_ref, ctx, lse, grad, kvs, qa, ga, ka, va, kx)
    for p in range(count):
        k_all[p * tokens : (p + 1) * tokens] = kvs[p][0]
    causal = causal_mask(rows, True)
    fixed, free = tile_rows(info, count, rows)
    tiles = [(high, pl.ds(k, rows), False, None) for k in fixed]
    tiles += [(high, high, True, None), (low, low, True, None)]
    tiles += [(pl.ds(q, rows), pl.ds(k, rows), False, q > 0) for q, k in free]
    dq_low, dq_high = [0.0, 0.0], [0.0, 0.0]
    dk, dv = [None, None], [None, None]

    def products(unit):
        t, head = unit
        q_cut, k_cut = tiles[t][:2]
        return nt(ka[head, k_cut], qa[head, q_cut]), nt(va[head, k_cut], ga[head, q_cut])

    def scores_of(unit, logits, grad_p):
        if tiles[unit[0]][2]:
            logits = jnp.where(causal, logits, NEGATIVE)
        probs = jnp.exp2(logits * LOG2E)
        return probs.astype(BF16), (probs * grad_p).astype(BF16)

    def grads(unit, probs, scores):
        t, head = unit
        q_cut, k_cut, _, is_high = tiles[t]
        dv[head] = nn(probs, grad[q_cut])
        dk[head] = nn(scores, q_ref[q_cut])
        part = tn(k_all[k_cut], scores)
        if q_cut is high:
            dq_high[head] = dq_high[head] + part
        elif q_cut is low:
            dq_low[head] = dq_low[head] + part
        else:
            dq_high[head] = dq_high[head] + jnp.where(is_high, part, 0.0)
            dq_low[head] = dq_low[head] + jnp.where(is_high, 0.0, part)
        if head == 1:
            parts[0, t] = both_heads(*dk)
            parts[1, t] = both_heads(*dv)

    in_stages([(t, head) for t in range(len(tiles)) for head in range(2)], products, scores_of, grads)
    top = lax.broadcasted_iota(jnp.int32, (PAIR, rows), 0) < HALF
    dq_out[low] = jnp.where(top, *dq_low).T.astype(BF16)
    dq_out[high] = jnp.where(top, *dq_high).T.astype(BF16)
    total[...] = jnp.zeros_like(total)
    for i in range(2):
        total[i, high] = parts[i, count]
        total[i, low] = parts[i, count + 1]
    base = INFO_HEAD + 2 * count

    @pl.loop(0, 2 * count - 1)
    def _(t):
        is_free = (t >= count).astype(jnp.int32)
        at = pl.multiple_of(info[base + t + is_free * (count - 1)], rows)
        for i in range(2):
            total[i, pl.ds(at, rows)] += parts[i, t + 2 * is_free]

    for p in range(count):
        cut = slice(p * tokens, (p + 1) * tokens)
        for i in range(2):
            dkvs[p][i] = total[i, cut].astype(BF16)


def run_backward(info, q, ctx, lse, grad, kvs, causal, first=0, pairs=None):
    tokens, width = q.shape
    pairs = pairs or width // PAIR
    width = pairs * PAIR
    rows = tokens // 2
    count = len(kvs)
    keys = count * tokens
    wide, kv, lse_spec = attention_specs(count, tokens, first)
    wide_out, kv_out, _ = attention_specs(count, tokens)
    scratch = [pltpu.VMEM((2, tokens, PAIR), BF16)] * 2 + [pltpu.VMEM((2, keys, PAIR), BF16)] * 3
    if causal:
        scratch += [
            pltpu.VMEM((keys, PAIR), BF16),
            pltpu.VMEM((2, 2 * count + 1, rows, PAIR), F32),
            pltpu.VMEM((2, keys, PAIR), F32),
        ]
    return pl.pallas_call(
        functools.partial(self_backward_kernel if causal else cross_backward_kernel, count),
        grid=(pairs,),
        out_shape=(as_struct((tokens, width), BF16),) + (as_struct((2, tokens, width), BF16),) * count,
        in_specs=[SMEM_SPEC, wide, wide, lse_spec, wide] + [kv] * count,
        out_specs=(wide_out,) + (kv_out,) * count,
        scratch_shapes=scratch,
        compiler_params=pltpu.CompilerParams(vmem_limit_bytes=FULL_LIMIT if causal else attention_limit(keys)),
        cost_estimate=cost(2.5e9 * pairs, 6e6),
        name="self_backward" if causal else "cross_backward",
    )(info, q, ctx, lse, grad, *kvs)


def middle_kernel(size, info, first_ref, ctx, og_own, og_other, *rest):
    w2, w3, rest = rest[:size], rest[size : 3 * size], rest[3 * size :]
    vec, fib, keep_out, pass_out, dz2_out, dcross_out = rest[:6]
    slots, (vecs, co, fi, fo, slope, scr, wide, grad_out) = rest[6 : 6 + size], rest[6 + size :]
    place, half = info[0], info[1]
    tokens, width = first_ref.shape
    rows = tokens // 2
    part = width // size
    hidden_part = fo.shape[0] // size
    chunks = fi.shape[1] // width
    assemble(co, w2, place, part, 4 * part)
    for i, ref in enumerate(w3):
        owner, which = place ^ (i // 2), info[6] ^ (i % 2)
        small, large = part // 2, hidden_part // 2
        start = pl.multiple_of(owner * part + which * small, small)
        for c in range(chunks):
            fi[pl.ds(start, small), c * width : (c + 1) * width] = ref[c * small : (c + 1) * small, :]
        start = pl.multiple_of(owner * hidden_part + which * large, large)
        fo[pl.ds(start, large), :] = ref[chunks * small :, :]

    def vector(i):
        return vec[i : i + 1, :]

    resid2 = first_ref[...].astype(F32) + nn(ctx[...], co[...]) + vector(CBO)
    normed2, inverse2 = norm(resid2)
    second = (normed2 * vector(N2G) + vector(N2B)).astype(BF16)
    sums = [0.0]

    def forward_product(c):
        return (nn(second, fi[:, c * width : (c + 1) * width]),)

    def activate(c, value):
        cut = slice(c * width, (c + 1) * width)
        value = value + fib[:, cut]
        sig = 0.5 * jnp.tanh(0.5 * value) + 0.5
        slope[:, cut] = sig * (1.0 + value * (1.0 - sig))
        hidden = (value * sig).astype(BF16)
        scr[:, cut] = hidden
        return (hidden,)

    def add_branch(c, hidden):
        sums[0] = sums[0] + nn(hidden, fo[c * width : (c + 1) * width])

    in_stages(range(chunks), forward_product, activate, add_branch)
    branch = sums[0]
    resid3 = second.astype(F32) + branch + vector(FOB)
    normed3, inverse3 = norm(resid3)
    out = (normed3 * vector(N3G) + vector(N3B)).astype(BF16)
    keep_out[...], pass_out[...] = ordered(info, out[:rows], out[rows:])

    live = info[4]
    iota = lax.broadcasted_iota(jnp.int32, (rows, 1), 0)
    low, high = ordered(info, og_own[half], og_other[...])
    grad3 = jnp.concatenate(
        [
            jnp.where(iota + info[2] < live, low.astype(F32), 0.0),
            jnp.where(iota + info[3] < live, high.astype(F32), 0.0),
        ],
        axis=0,
    )
    dz3 = norm_back(grad3, normed3, inverse3, vector(N3G))
    vecs[...] = jnp.zeros_like(vecs)
    vecs[N3G : N3G + 1] = row_sum(grad3 * normed3)
    vecs[N3B : N3B + 1] = row_sum(grad3)
    dy = dz3.astype(BF16)
    vecs[FOB : FOB + 1] = row_sum(dy.astype(F32))
    second_t = second.T
    sums = [dz3]

    def backward_products(c):
        cut = slice(c * width, (c + 1) * width)
        grad_out[cut] = tn(scr[:, cut], dy).astype(BF16)
        return (nt(dy, fo[cut]),)

    def slope_back(c, grad):
        dpre = (grad * slope[:, c * width : (c + 1) * width]).astype(BF16)
        vecs[FIB + c : FIB + c + 1] = row_sum(dpre.astype(F32))
        return (dpre,)

    def input_grads(c, dpre):
        sums[0] = sums[0] + nt(dpre, fi[:, c * width : (c + 1) * width])
        wide[...] = nn(second_t, dpre)
        scatter_rows(slots, wide, place, part, c * part)

    in_stages(range(chunks), backward_products, slope_back, input_grads)
    dsecond = sums[0]
    for k, slot in enumerate(slots):
        start = pl.multiple_of((place ^ k) * hidden_part, hidden_part)
        slot[chunks * part : chunks * part + hidden_part, :] = grad_out[pl.ds(start, hidden_part), :]
    dz2 = norm_back(dsecond, normed2, inverse2, vector(N2G))
    vecs[N2G : N2G + 1] = row_sum(dsecond * normed2)
    vecs[N2B : N2B + 1] = row_sum(dsecond)
    dz2_out[...] = dz2
    da2 = dz2.astype(BF16)
    vecs[CBO : CBO + 1] = row_sum(da2.astype(F32))
    dcross_out[...] = nt(da2, co[...]).astype(BF16)
    wide[...] = tn(ctx[...], da2)
    scatter_rows(slots, wide, place, part, chunks * part + hidden_part)


def run_middle(info, first, ctx, og_own, og_other, w2, w3, vec, fib):
    tokens, width = first.shape
    size = len(w2)
    part = width // size
    ff = fib.shape[1]
    grad_rows = (ff // width) * part + ff // size + part
    pack = as_struct((grad_rows, width), BF16)
    return pl.pallas_call(
        functools.partial(middle_kernel, size),
        out_shape=(
            as_struct((tokens // 2, width), BF16),
            as_struct((tokens // 2, width), BF16),
            as_struct((tokens, width), F32),
            as_struct((tokens, width), BF16),
            *(pack,) * size,
            as_struct((VEC_ROWS, width), F32),
        ),
        in_specs=[SMEM_SPEC] + [VMEM_SPEC] * (4 + 3 * size + 2),
        out_specs=(VMEM_SPEC,) * (5 + size),
        scratch_shapes=[
            pltpu.VMEM((width, width), BF16),
            pltpu.VMEM((width, ff), BF16),
            pltpu.VMEM((ff, width), BF16),
            pltpu.VMEM((tokens, ff), F32),
            pltpu.VMEM((tokens, ff), BF16),
            pltpu.VMEM((width, width), F32),
            pltpu.VMEM((ff, width), BF16),
        ],
        compiler_params=pltpu.CompilerParams(vmem_limit_bytes=MIDDLE_LIMIT),
        cost_estimate=cost(12 * tokens * width * ff, 2e7),
        name="middle",
    )(info, first, ctx, og_own, og_other, *w2, *w3, vec, fib)


def after_cross_kernel(size, info, dz2, dq, first_ref, x_ref, ctx, *rest):
    w2, rest = rest[:size], rest[size:]
    vec, dz1_out, dself_out = rest[:3]
    slots, (vecs, weight, wide) = rest[3 : 3 + size], rest[3 + size :]
    place = info[0]
    width = x_ref.shape[1]
    part = width // size
    for i in range(2):
        assemble(weight, w2, place, part, i * part, i)

    def vector(i):
        return vec[i : i + 1, :]

    vecs[...] = jnp.zeros_like(vecs)
    dfirst = dz2[...] + SCALE * nt(dq[...], weight[1])
    resid = x_ref[...].astype(F32) + nn(ctx[...], weight[0]) + vector(SBO)
    normed, inverse = norm(resid)
    dz1 = norm_back(dfirst, normed, inverse, vector(N1G))
    vecs[N1G : N1G + 1] = row_sum(dfirst * normed)
    vecs[N1B : N1B + 1] = row_sum(dfirst)
    vecs[CBQ : CBQ + 1] = row_sum(dq[...].astype(F32)) * SCALE
    dz1_out[...] = dz1
    da1 = dz1.astype(BF16)
    vecs[SBO : SBO + 1] = row_sum(da1.astype(F32))
    dself_out[...] = nt(da1, weight[0]).astype(BF16)
    wide[...] = tn(ctx[...], da1)
    scatter_rows(slots, wide, place, part, 0)
    wide[...] = tn(first_ref[...], dq[...]) * SCALE
    scatter_rows(slots, wide, place, part, part)


def run_after_cross(info, dz2, dq, first, x, ctx, w2, vec):
    tokens, width = x.shape
    size = len(w2)
    pack = as_struct((2 * (width // size), width), BF16)
    return pl.pallas_call(
        functools.partial(after_cross_kernel, size),
        out_shape=(
            as_struct((tokens, width), F32),
            as_struct((tokens, width), BF16),
            *(pack,) * size,
            as_struct((VEC_ROWS, width), F32),
        ),
        in_specs=[SMEM_SPEC] + [VMEM_SPEC] * (6 + size),
        out_specs=(VMEM_SPEC,) * (3 + size),
        scratch_shapes=[pltpu.VMEM((2, width, width), BF16), pltpu.VMEM((width, width), F32)],
        compiler_params=pltpu.CompilerParams(vmem_limit_bytes=FULL_LIMIT),
        cost_estimate=cost(10 * tokens * width * width, 8e6),
        name="after_cross",
    )(info, dz2, dq, first, x, ctx, *w2, vec)


def encoder_back_kernel(size, info, own, got, x_ref, *rest):
    w2, given, rest = rest[:size], rest[size : 2 * size], rest[2 * size :]
    keep_out, pass_out = rest[:2]
    slots, (vecs, weight, wide) = rest[2 : 2 + size], rest[2 + size :]
    place = info[0]
    width = x_ref.shape[1]
    rows = x_ref.shape[0] // 2
    part = width // size
    for i in range(2):
        assemble(weight, w2, place, part, (2 + i) * part, i)
    vecs[...] = jnp.zeros_like(vecs)
    for slot, ref in zip(slots, given):
        slot[: 2 * part, :] = ref[...]
    total = None
    for i in range(2):
        grad = (own[i].astype(F32) + got[i].astype(F32)).astype(BF16)
        if i == 1:
            vecs[CBV : CBV + 1] = row_sum(grad.astype(F32))
        wide[...] = tn(x_ref[...], grad)
        scatter_rows(slots, wide, place, part, (2 + i) * part)
        term = nt(grad, weight[i])
        total = term if total is None else total + term
    total = total.astype(BF16)
    keep_out[...], pass_out[...] = ordered(info, total[:rows], total[rows:])


def run_encoder_back(info, own, got, x, w2, given):
    tokens, width = x.shape
    size = len(w2)
    pack = as_struct((4 * (width // size), width), BF16)
    return pl.pallas_call(
        functools.partial(encoder_back_kernel, size),
        out_shape=(
            as_struct((tokens // 2, width), BF16),
            as_struct((tokens // 2, width), BF16),
            *(pack,) * size,
            as_struct((VEC_ROWS, width), F32),
        ),
        in_specs=[SMEM_SPEC] + [VMEM_SPEC] * (3 + 2 * size),
        out_specs=(VMEM_SPEC,) * (3 + size),
        scratch_shapes=[pltpu.VMEM((2, width, width), BF16), pltpu.VMEM((width, width), F32)],
        compiler_params=pltpu.CompilerParams(vmem_limit_bytes=FULL_LIMIT),
        cost_estimate=cost(8 * tokens * width * width, 8e6),
        name="encoder_back",
    )(info, own, got, x, *w2, *given)


def side_by_side(refs):
    return jnp.concatenate([ref[...] for ref in refs], axis=-1)


def target_back_kernel(size, hidden, info, dz1, dq_a, dq_b, own_a, own_b, got_a, got_b, x_ref, *rest):
    w1, others, rest = rest[:size], rest[size : size + 3], rest[size + 3 :]
    keep_out, pass_out = rest[:2]
    slots, (vecs, by_owner, weight, wide) = rest[2 : 2 + size], rest[2 + size :]
    place = info[0]
    width = x_ref.shape[1]
    rows = x_ref.shape[0] // 2
    part = width // size
    for i in range(3):
        assemble(weight, w1, place, part, i * part, i)
    vecs[...] = others[0][...] + others[1][...] + others[2][...]
    dq = side_by_side((dq_a, dq_b))
    vecs[SBQ : SBQ + 1] = row_sum(dq.astype(F32)) * SCALE
    total = dz1[...] + SCALE * nt(dq, weight[0])
    wide[...] = tn(x_ref[...], dq) * SCALE
    scatter_rows(slots, wide, place, part, 0)
    for i in range(2):
        own = side_by_side((own_a.at[i], own_b.at[i])).astype(F32)
        grad = (own + side_by_side((got_a.at[i], got_b.at[i])).astype(F32)).astype(BF16)
        if i == 1:
            vecs[SBV : SBV + 1] = row_sum(grad.astype(F32))
        wide[...] = tn(x_ref[...], grad)
        scatter_rows(slots, wide, place, part, (1 + i) * part)
        total = total + nt(grad, weight[1 + i])
    total = total.astype(BF16)
    keep_out[...], pass_out[...] = ordered(info, total[:rows], total[rows:])
    chunks = hidden // width
    for j in range(size):
        by_owner[j] = jnp.zeros((VEC_ROWS, width), F32)
        by_owner[j, :, :part] = vecs[:, j * part : (j + 1) * part]
        for i in range(chunks):
            at = (j * chunks + i) * part
            row = FIB + at // width
            by_owner[j, FIB + i : FIB + i + 1, :part] = vecs[row : row + 1, at % width : at % width + part]
    for k, slot in enumerate(slots):
        slot[3 * part :, :] = by_owner[place ^ k].astype(BF16)


def run_target_back(hidden, info, dz1, dqs, owns, gots, x, w1, others):
    tokens, width = x.shape
    size = len(w1)
    pack = as_struct((3 * (width // size) + VEC_ROWS, width), BF16)
    return pl.pallas_call(
        functools.partial(target_back_kernel, size, hidden),
        out_shape=(
            as_struct((tokens // 2, width), BF16),
            as_struct((tokens // 2, width), BF16),
            *(pack,) * size,
        ),
        in_specs=[SMEM_SPEC] + [VMEM_SPEC] * (11 + size),
        out_specs=(VMEM_SPEC,) * (2 + size),
        scratch_shapes=[
            pltpu.VMEM((VEC_ROWS, width), F32),
            pltpu.VMEM((size, VEC_ROWS, width), F32),
            pltpu.VMEM((3, width, width), BF16), pltpu.VMEM((width, width), F32),
        ],
        compiler_params=pltpu.CompilerParams(vmem_limit_bytes=DENSE_LIMIT),
        cost_estimate=cost(12 * tokens * width * width, 8e6),
        name="target_back",
    )(info, dz1, *dqs, *owns, *gots, x, *w1, *others)


def add(left, right):
    return (left.astype(F32) + right.astype(F32)).astype(BF16)


class GroupSum:
    def __init__(self, slots):
        self.keep = slots[0::2]
        self.own, *self.far = [send_xor(v, "group", 1) for v in slots[1::2]]

    def start(self):
        parts = [None] + [add(k, f) for k, f in zip(self.keep[1:], self.far)]
        mask, self.arrived = 2, []
        while len(parts) > 1:
            arrived = [send_xor(p, "group", mask) for p in parts[1::2]]
            self.arrived.append(arrived[0])
            parts = [None] + [add(a, b) for a, b in zip(parts[2::2], arrived[1:])]
            mask *= 2

    def addends(self):
        return [self.keep[0], self.own, *self.arrived]

    def finish(self):
        return functools.reduce(lambda a, b: a + b, [v.astype(F32) for v in self.addends()]).astype(BF16)


def piece_shape(rows, width, size):
    return rows // 2, 2 * width // size


def pieces_kernel(count, *refs):
    addends, (out,) = refs[:count], refs[count:]
    size, rows, lanes = out.shape
    total = functools.reduce(lambda a, b: a + b, [v[...].astype(F32) for v in addends]).astype(BF16)
    for j in range(size):
        row, lane = (j % 2) * rows, (j // 2) * lanes
        out[j] = total[row : row + rows, lane : lane + lanes]


def run_pieces(addends, size):
    rows, width = addends[0].shape
    return pl.pallas_call(
        functools.partial(pieces_kernel, len(addends)),
        out_shape=as_struct((size, *piece_shape(rows, width, size)), BF16),
        in_specs=[VMEM_SPEC] * len(addends),
        out_specs=VMEM_SPEC,
        compiler_params=pltpu.CompilerParams(vmem_limit_bytes=DENSE_LIMIT),
        cost_estimate=cost(0, 0),
        name="pieces",
    )(*addends)


def sum_pieces_kernel(parts, out):
    total = parts[0].astype(F32)
    for j in range(1, parts.shape[0]):
        total = total + parts[j].astype(F32)
    for j in range(parts.shape[0]):
        out[j] = total.astype(BF16)


def run_sum_pieces(parts):
    return pl.pallas_call(
        sum_pieces_kernel,
        out_shape=as_struct(parts.shape, BF16),
        in_specs=[VMEM_SPEC],
        out_specs=VMEM_SPEC,
        compiler_params=pltpu.CompilerParams(vmem_limit_bytes=DENSE_LIMIT),
        cost_estimate=cost(0, 0),
        name="sum_pieces",
    )(parts)


def whole_kernel(cuts, part, chunks, parts, *refs):
    *outs, full = refs
    size, rows, lanes = parts.shape
    for j in range(size):
        row, lane = (j % 2) * rows, (j // 2) * lanes
        full[row : row + rows, lane : lane + lanes] = parts[j].astype(F32)
    for (start, stop), out in zip(cuts, outs):
        out[...] = full[start:stop]
    base = cuts[-1][1]
    for i in range(FIB):
        outs[len(cuts) + i][...] = full[base + i : base + i + 1, :part]
    for i in range(chunks):
        outs[-1][:, i * part : (i + 1) * part] = full[base + FIB + i : base + FIB + i + 1, :part]


def run_whole(parts, cuts, part, chunks):
    size, rows, lanes = parts.shape
    width = lanes * size // 2
    shapes = [(stop - start, width) for start, stop in cuts] + [(1, part)] * FIB + [(1, chunks * part)]
    return pl.pallas_call(
        functools.partial(whole_kernel, cuts, part, chunks),
        out_shape=tuple(as_struct(shape, F32) for shape in shapes),
        in_specs=[VMEM_SPEC],
        out_specs=(VMEM_SPEC,) * len(shapes),
        scratch_shapes=[pltpu.VMEM((2 * rows, width), F32)],
        compiler_params=pltpu.CompilerParams(vmem_limit_bytes=DENSE_LIMIT),
        cost_estimate=cost(0, 0),
        name="whole",
    )(parts)


def exchange(parts):
    return lax.all_to_all(parts, "replica", 0, 0)


def halves(value, dim):
    cut = value.shape[dim] // 2
    return lax.slice_in_dim(value, 0, cut, axis=dim), lax.slice_in_dim(value, cut, 2 * cut, axis=dim)


class ReplicaSum:
    def __init__(self, value, whole=1):
        self.value = value
        self.size = lax.axis_size("replica")
        self.place = lax.axis_index("replica")
        masks = [1 << i for i in range(self.size.bit_length() - 1)]
        last = len(masks) - whole
        self.steps = [(m, "halve") for m in masks[:last]] + [(m, "whole") for m in masks[last:]]
        self.steps += [(m, "gather") for m in reversed(masks[:last])]
        self.dims = {}

    def start(self):
        mask, kind = self.steps[0]
        give = self.value
        if kind == "halve":
            up = (self.place & mask) != 0
            dim = 0 if mask == 1 else 1
            self.dims[mask] = dim
            low, high = halves(self.value, dim)
            self.value = jnp.where(up, high, low)
            give = jnp.where(up, low, high)
        self.arrived = send_xor(give, "replica", mask)

    def finish(self):
        mask, kind = self.steps.pop(0)
        if kind == "gather":
            up = (self.place & mask) != 0
            dim = self.dims[mask]
            self.value = jnp.where(
                up,
                jnp.concatenate([self.arrived, self.value], axis=dim),
                jnp.concatenate([self.value, self.arrived], axis=dim),
            )
        else:
            self.value = add(self.value, self.arrived)


def butterfly(stacked, place, size):
    bit = 1
    while bit < size:
        order = np.arange(size) ^ bit
        flipped = jnp.stack([stacked[int(i)] for i in order])
        stacked = jnp.where((place & bit) != 0, flipped, stacked)
        bit *= 2
    return stacked


def body(
    target, encoder, target_len, encoder_len,
    self_wq, self_wk, self_wv, self_wo, self_bq, self_bv, self_bo, norm1_gain, norm1_bias,
    cross_wq, cross_wk, cross_wv, cross_wo, cross_bq, cross_bv, cross_bo, norm2_gain, norm2_bias,
    ffn_in, ffn_in_bias, ffn_out, ffn_out_bias, norm3_gain, norm3_bias, out_grad,
):
    size = lax.axis_size("group")
    place = lax.axis_index("group")
    _, rows, width = target.shape
    part = width // size
    ff = ffn_in.shape[1]
    chunks = ff // width
    half = (place >= size // 2).astype(jnp.int32)
    table = jnp.asarray(group_table(size, rows))
    side = lax.axis_index("replica") & 1
    lengths = jnp.append(jnp.stack([target_len, encoder_len])[:, half], side)
    info = lax.dynamic_update_slice(table[place], lengths, (4,))
    mirror = [(i, size - 1 - i) for i in range(size)]

    def swap(value):
        return lax.ppermute(value, "group", mirror)

    w1_own, target_half = run_first_pack(info, target, (self_wq, self_wk, self_wv))
    w1 = gather_even(w1_own, "group", size)
    target_got = swap(target_half)
    matrices = (encoder, out_grad, ffn_in, ffn_out, self_wo, cross_wq, cross_wk, cross_wv, cross_wo)
    vectors = (
        self_bq, self_bv, self_bo, norm1_gain, norm1_bias, cross_bq, cross_bv, cross_bo,
        norm2_gain, norm2_bias, ffn_out_bias, norm3_gain, norm3_bias, ffn_in_bias,
    )
    w1_odd, *late = point(send_xor(w1_own, "group", 1), *matrices, *vectors)
    matrices, vectors = late[: len(matrices)], late[len(matrices) :]
    w2_own, *w3_own, encoder_half, og_half = run_second_pack(info, *matrices[:4], matrices[4:])
    encoder_half, *vectors = point(encoder_half, *vectors)
    vec_own = jnp.concatenate([v.reshape(-1, part) for v in vectors])
    vec_own = jnp.pad(vec_own, ((0, VEC_ROWS - vec_own.shape[0]), (0, 0)))
    vec_odd = send_xor(vec_own, "group", 1)
    vec_pairs = gather_even(jnp.concatenate([vec_own, vec_odd]), "group", size)
    vec_all = jnp.stack(vec_pairs).reshape(size, VEC_ROWS, part)
    vec_all = butterfly(vec_all, place, size)
    vec = jnp.transpose(vec_all, (1, 0, 2)).reshape(VEC_ROWS, width).astype(F32)
    fib = vec_all[:, FIB : FIB + chunks].reshape(1, ff).astype(F32)
    target_got, encoder_half, *w1 = point(target_got, encoder_half, *w1)
    encoder_got = swap(encoder_half)
    w1 = [v for e, o in zip(w1, [w1_odd] + [send_xor(e, "group", 1) for e in w1[1:]]) for v in (e, o)]

    x, q1, kv1 = run_qkv(info, target, target_got, w1, vec)
    kv1, w2_own, encoder_got = point(kv1, w2_own, encoder_got)
    w2 = gather_even(w2_own, "group", size)
    kvs1 = gather_xor(kv1, "group", size // 2)
    ctx1, lse1 = run_forward(info, q1, kvs1, True)
    ctx1, w3_near, w3_far, *w2 = point(ctx1, *w3_own, *w2)
    w2 = with_odd(w2, "group")
    w3_even = gather_even(w3_near, "group", size)[1:]
    w3_odd = [send_xor(w, "group", 1) for w in (w3_near, w3_far)]
    xe, kv2 = run_cross_kv(info, encoder, encoder_got, w2, vec)
    kv2, ctx1 = point(kv2, ctx1)
    kvs2 = gather_xor(kv2, "group", size // 2)
    first, q2 = run_after_self(info, x, ctx1, w2, vec)
    q2, og_half, *w3_even = point(q2, og_half, *w3_even)
    w3_other = [send_xor(w, "replica", 1) for w in w3_even]
    og_got = swap(og_half)
    w3_pass = [send_xor(w, "group", 1) for w in w3_even]
    ctx2, lse2 = run_forward(info, q2, kvs2, False)
    ctx2, og_got, *w3_other = point(ctx2, og_got, *w3_other)
    w3 = [*w3_own, *w3_odd]
    for near, far, passed in zip(w3_even, w3_other, w3_pass):
        w3 += [near, far, passed, send_xor(far, "group", 1)]
    out_keep, out_pass, dz2, dcross, *slots_a, vecs_a = run_middle(
        info, first, ctx2, out_grad, og_got, w2, w3, vec, fib
    )

    def key_value_sums(parts):
        bit = len(parts) // 2
        while bit > 1:
            arrived = [send_xor(parts[k | bit], "group", bit) for k in range(bit)]
            parts = [add(parts[k], arrived[k]) for k in range(bit)]
            bit //= 2
        return parts[0], send_xor(parts[1], "group", 1)

    group_a = GroupSum(slots_a)
    dcross, *group_a.far = point(dcross, *group_a.far)
    group_a.start()
    dq2, *dkvs2 = run_backward(info, q2, ctx2, lse2, dcross, kvs2, False)
    dq2, out_pass, *dkvs2 = point(dq2, out_pass, *dkvs2)
    own2, got2 = key_value_sums(dkvs2)
    dz1, dself, *slots_b, vecs_b = run_after_cross(info, dz2, dq2, first, x, ctx1, w2, vec)
    dself, got2, out_pass, group_a.own, *group_a.arrived = point(
        dself, got2, out_pass, group_a.own, *group_a.arrived
    )
    sum_a = ReplicaSum(group_a.finish(), 0)
    sum_a.start()
    out_got = swap(out_pass)
    enc_keep, enc_pass, *slots_b, vecs_e = run_encoder_back(info, own2, got2, xe, w2, slots_b)
    group_b = GroupSum(slots_b)
    dself, enc_pass, *group_b.far = point(dself, enc_pass, *group_b.far)
    group_b.start()
    enc_got = swap(enc_pass)
    pairs = width // PAIR // 2
    dq1_a, *dkvs1_a = run_backward(info, q1, ctx1, lse1, dself, kvs1, True, 0, pairs)
    dself, sum_a.arrived, *dkvs1_a = point(dself, sum_a.arrived, *dkvs1_a)
    own1_a, got1_a = key_value_sums(dkvs1_a)
    sum_a.finish()
    sum_a.start()
    dq1_b, *dkvs1_b = run_backward(info, q1, ctx1, lse1, dself, kvs1, True, pairs, pairs)
    hops = len(group_b.arrived)
    group_b.own, dq1_b, sum_a.arrived, *moved = point(
        group_b.own, dq1_b, sum_a.arrived, *group_b.arrived, *dkvs1_b
    )
    group_b.arrived, dkvs1_b = moved[:hops], moved[hops:]
    own1_b, got1_b = key_value_sums(dkvs1_b)
    sum_b = ReplicaSum(group_b.finish())
    sum_b.start()
    sum_a.finish()
    sum_a.start()
    tgt_keep, tgt_pass, *slots_c = run_target_back(
        ff, info, dz1, (dq1_a, dq1_b), (own1_a, own1_b), (got1_a, got1_b), x, w1, (vecs_a, vecs_b, vecs_e)
    )

    tgt_pass, sum_a.arrived, sum_b.arrived, *slots_c = point(tgt_pass, sum_a.arrived, sum_b.arrived, *slots_c)

    def advance(*sums):
        for s in sums:
            if s.steps:
                s.finish()
            if s.steps:
                s.start()

    def behind(*values):
        *values, sum_a.value, sum_b.value = point(*values, sum_a.value, sum_b.value)
        return values

    group_c = GroupSum(slots_c)
    group_c.far = behind(*group_c.far)
    group_c.start()
    advance(sum_a, sum_b)
    sum_a.arrived, sum_b.arrived = point(sum_a.arrived, sum_b.arrived)
    advance(sum_a, sum_b)
    group_c.own, *group_c.arrived = behind(group_c.own, *group_c.arrived)
    parts_c = exchange(run_pieces(group_c.addends(), lax.axis_size("replica")))
    tgt_got = swap(tgt_pass)
    sum_a.arrived, sum_b.arrived = point(sum_a.arrived, sum_b.arrived)
    advance(sum_a, sum_b)
    parts_c, tgt_got = behind(parts_c, tgt_got)
    parts_c = exchange(run_sum_pieces(parts_c))
    while sum_a.steps or sum_b.steps:
        advance(sum_a, sum_b)
    a = sum_a.value.astype(F32)
    g_fi = jnp.transpose(a[: chunks * part].reshape(chunks, part, width), (1, 0, 2)).reshape(part, ff)
    g_fo = a[chunks * part : chunks * part + ffn_out.shape[0]]
    g_co = a[chunks * part + ffn_out.shape[0] :]

    def unswap(kept, arrived):
        return jnp.where(half == 0, jnp.stack([kept, arrived]), jnp.stack([arrived, kept]))

    outputs = (unswap(out_keep, out_got), unswap(tgt_keep, tgt_got), unswap(enc_keep, enc_got))
    g_fi, g_fo, g_co, out, grad_tgt, grad_enc, parts_c = point(g_fi, g_fo, g_co, *outputs, parts_c)
    cuts = tuple((i * part, (i + 1) * part) for i in range(3))
    g_sq, g_sk, g_sv, *g_vec = run_whole(parts_c, cuts, part, chunks)
    g_vec = [v.reshape(-1) for v in g_vec]
    b = sum_b.value.astype(F32)
    g_so, g_cq, g_ck, g_cv = (b[i * part : (i + 1) * part] for i in range(4))
    return (
        out, grad_tgt, grad_enc,
        g_sq, g_sk, g_sv, g_so, g_vec[SBQ], g_vec[SBV], g_vec[SBO], g_vec[N1G], g_vec[N1B],
        g_cq, g_ck, g_cv, g_co, g_vec[CBQ], g_vec[CBV], g_vec[CBO], g_vec[N2G], g_vec[N2B],
        g_fi, g_vec[FIB], g_fo, g_vec[FOB], g_vec[N3G], g_vec[N3B],
    )


def solution(mesh):
    seq, lens, mat, vec = P("replica", "group", None), P("replica"), P("group", None), P("group")
    layer = (mat,) * 4 + (vec,) * 5 + (mat,) * 4 + (vec,) * 5 + (mat, vec, mat, vec, vec, vec)
    in_specs = (seq, seq, lens, lens) + layer + (seq,)
    out_specs = (seq,) * 3 + layer
    return jax.shard_map(body, mesh=mesh, in_specs=in_specs, out_specs=out_specs, check_vma=False)
```
